256 devices in a mesh: tx: 8 (over x, core), gz: 32 (over y, z).
Axes of the slice: x: 4, y: 4, z: 8, core: 2. Of those that a mesh axis runs over, the one named last changes fastest.
Arguments:
- sources: float32 [8, 2, 128, 128, 128], P('tx', None, 'gz'), may hold values from -2 to 2
- contrast: float32 [2, 128, 128, 128], P(None, 'gz'), may hold values from -3 to 3
- spectrum: float32 [2, 256, 256, 256], P(None, None, 'gz'), may hold values from -6 to 6
- measured: float32 [8, 2, 1024], P('tx'), may hold values from -6.1 to 6.1
- receivers: int32 [8, 1024], P('tx'), may hold values from 0 to 2097151
- positions: int32 [8, 2], P('tx'), may hold values from 0 to 127
Outputs:
- sources_new: float32 [8, 2, 128, 128, 128], P('tx', None, 'gz')
- contrast_new: float32 [2, 128, 128, 128], P(None, 'gz')
The draws below stay inside these ranges and needn't reach their ends.
All inputs are finite; a program needn't handle non-finite values.
Results may differ from the reference program's by a relative error of at most 0.0001.
Values sent between devices are 32-bit elements; how exact they have to be, the bound alone decides.
A program may use at most 256 MiB of HBM per device.

```python
import math
import jax
import jax.numpy as jnp
from jax import lax

NC = 128
NP = 256
TX = 8
NREC = 1024


def draw_measured(key, part):
    ramp = jnp.arange(TX, dtype=jnp.float32) / max(TX - 1, 1)
    values = jnp.clip(jax.random.normal(key, (TX, 2, NREC), jnp.float32), -5.0, 5.0)
    scales = 0.7 * jnp.exp(ramp * (0.5 * math.log(3.0)))
    return values * scales[:, None, None]


def touch_ends(values, rng, low, high):
    shape = values.shape
    spot = [jax.random.randint(jax.random.fold_in(rng, axis), (), 0, shape[axis]) for axis in range(len(shape))]
    values = values.at[tuple(spot)].set(low)
    longest = shape.index(max(shape))
    spot[longest] = (spot[longest] + 1) % shape[longest]
    return values.at[tuple(spot)].set(high)


def level_of(own_key, extent, pieces, smallest, high):
    level = 1.0
    for dim, parts in pieces:
        steps = jax.random.uniform(jax.random.fold_in(jax.random.fold_in(own_key, 6), dim), (parts,), jnp.float32, smallest / len(pieces), high / len(pieces))
        level = level * jnp.repeat(jnp.exp(steps), extent[dim] // parts).reshape((-1,) + (1,) * (len(extent) - 1 - dim))
    return level


def bell_draw(stream_key, shape, width, reach, cuts=(), kind=jnp.bfloat16):
    level = level_of(stream_key, shape, cuts, -0.22, 0.18) if cuts else 1.0
    array = jax.random.normal(stream_key, shape, jnp.float32) * width * level
    return jnp.minimum(jnp.maximum(array, -reach), reach).astype(kind)


def setup_inputs(seed: int = 0) -> dict:
    splits = jax.random.split(jax.random.key(seed), 7)
    return {
        "sources": bell_draw(splits[0], (TX, 2, NC, NC, NC), 0.3, 2.0, ((0, 8), (2, 32)), jnp.float32),
        "contrast": bell_draw(splits[1], (2, NC, NC, NC), 0.5, 3.0, ((1, 32),), jnp.float32),
        "spectrum": bell_draw(splits[2], (2, NP, NP, NP), 1.0, 6.0, ((2, 32),), jnp.float32),
        "measured": draw_measured(jax.random.fold_in(splits[6], 71), 0),
        "receivers": touch_ends(jax.random.randint(splits[4], (TX, NREC), 0, NC * NC * NC), jax.random.fold_in(splits[4], 1), 0, (NC * NC * NC) - 1).astype(jnp.int32),
        "positions": touch_ends(jax.random.randint(splits[5], (TX, 2), 0, NC), jax.random.fold_in(splits[5], 1), 0, NC - 1).astype(jnp.int32),
    }


wave_number = 2.0 * math.pi / 12.0
reach_cells = 16.0
tikhonov = 1.0
step_length = 0.5
norm_floor = 1e-06

def incident(position):
    grid_shape = (NC, NC, NC)
    first_axis = lax.broadcasted_iota(jnp.int32, grid_shape, 0) + NC // 4
    along_second = lax.broadcasted_iota(jnp.int32, grid_shape, 1) - position[0]
    along_third = lax.broadcasted_iota(jnp.int32, grid_shape, 2) - position[1]
    squared = first_axis * first_axis + along_second * along_second + along_third * along_third
    radius = jnp.sqrt(squared.astype(jnp.float32))
    amplitude = reach_cells / (reach_cells + radius)
    return (amplitude * jnp.cos(wave_number * radius), amplitude * jnp.sin(wave_number * radius))

def convolve(real_part, imag_part, spec_real, spec_imag):
    complex_field = lax.complex(real_part, imag_part)
    padded = jnp.pad(complex_field, ((0, NC), (0, NC), (0, NC)))
    spectral = jnp.fft.fftn(padded) * lax.complex(spec_real, spec_imag)
    result = jnp.fft.ifftn(spectral)[:NC, :NC, :NC]
    return (jnp.real(result), jnp.imag(result))

def reference(sources, contrast, spectrum, measured, receivers, positions):
    zeros = jnp.zeros((NC, NC, NC), jnp.float32)

    def forward_step(running, step_items):
        source, position = step_items
        inc_real, inc_imag = incident(position)
        scat_real, scat_imag = convolve(source[0], source[1], spectrum[0], spectrum[1])
        total_real = inc_real + scat_real
        total_imag = inc_imag + scat_imag
        numer_real = running[0] + (source[0] * total_real + source[1] * total_imag)
        numer_imag = running[1] + (source[1] * total_real - source[0] * total_imag)
        weight = running[2] + (total_real * total_real + total_imag * total_imag)
        return ((numer_real, numer_imag, weight), jnp.stack([scat_real, scat_imag]))
    sums, scattered = lax.scan(forward_step, (zeros, zeros, zeros), (sources, positions))
    numer_real, numer_imag, weight = sums
    chi_real = (numer_real + tikhonov * contrast[0]) / (weight + tikhonov)
    chi_imag = (numer_imag + tikhonov * contrast[1]) / (weight + tikhonov)
    chi_power = chi_real * chi_real + chi_imag * chi_imag

    def norm_step(running, position):
        inc_real, inc_imag = incident(position)
        return (running + jnp.sum(chi_power * (inc_real * inc_real + inc_imag * inc_imag)), None)
    object_norm, unused = lax.scan(norm_step, jnp.zeros((), jnp.float32), positions)
    data_norm = jnp.sum(measured * measured)
    norm_ratio = object_norm / (data_norm + norm_floor)

    def update_step(running, step_items):
        source, scatter_pair, position, target, cell_index = step_items
        inc_real, inc_imag = incident(position)
        total_real = inc_real + scatter_pair[0]
        total_imag = inc_imag + scatter_pair[1]
        res_real = chi_real * total_real - chi_imag * total_imag - source[0]
        res_imag = chi_real * total_imag + chi_imag * total_real - source[1]
        flat_field = scatter_pair.reshape(2, NC * NC * NC)
        misfit = target - jnp.take(flat_field, cell_index, axis=1)
        placed = jnp.zeros((2, NC * NC * NC), jnp.float32).at[:, cell_index].add(misfit).reshape(2, NC, NC, NC)
        drive_real = norm_ratio * placed[0] - (chi_real * res_real + chi_imag * res_imag)
        drive_imag = norm_ratio * placed[1] - (chi_real * res_imag - chi_imag * res_real)
        back_real, back_imag = convolve(drive_real, drive_imag, spectrum[0], -spectrum[1])
        updated = jnp.stack([source[0] + step_length * (res_real + back_real), source[1] + step_length * (res_imag + back_imag)])
        return (running, updated)
    unused, sources_new = lax.scan(update_step, jnp.zeros((), jnp.float32), (sources, scattered, positions, measured, receivers))
    return (sources_new, jnp.stack([chi_real, chi_imag]))
```

```python
import math

import jax
import jax.numpy as jnp
import numpy as np
from jax import lax
from jax.experimental import pallas as pl
from jax.experimental.pallas import tpu as pltpu
from jax.sharding import PartitionSpec as P

MESH = pl.DeviceIdType.MESH
F32 = jnp.float32
BF16 = jnp.bfloat16

reach_cells = 16.0
tikhonov = 1.0
step_length = 0.5
norm_floor = 1e-06

NC = 128
NP = 256
GZ = 32
TX = 8
NREC = 1024
ROWS = 512


def dft_matrix():
    k = np.arange(NP)[:, None]
    n = np.arange(NC)[None, :]
    angle = 2.0 * np.pi * ((k * n) % NP) / NP
    cosine, sine = np.cos(angle), np.sin(angle)
    full = np.zeros((2, NP, 2, NC))
    full[0, :, 0, :] = cosine
    full[0, :, 1, :] = sine
    full[1, :, 0, :] = -sine
    full[1, :, 1, :] = cosine
    return full


def halves(table, axis):
    table = table.astype(np.float32)
    high = table.astype(jnp.bfloat16)
    low = (table - high.astype(np.float32)).astype(jnp.bfloat16)
    return np.concatenate([high, low], axis)


def dft_tables():
    full = dft_matrix()
    by_freq = full.reshape(2, GZ, 2, 4, 2, NC)
    by_plane = full.reshape(2, NP, 2, GZ, 4)
    aq = by_freq.transpose(2, 1, 0, 3, 4, 5).reshape(2 * NP, 2 * NC)
    ap = by_plane.transpose(0, 1, 2, 4, 3).reshape(2 * NP, 2 * NC)
    br = full.transpose(2, 3, 0, 1).reshape(2 * NC, 2 * NP)
    bir = full.reshape(2 * NP, 2 * NC)
    aip = by_plane.transpose(3, 2, 4, 0, 1).reshape(2 * NC, 2 * NP)
    aiq = by_freq.transpose(4, 5, 0, 2, 3, 1).reshape(2 * NC, 2 * NP)
    return (
        halves(aq, 1),
        halves(ap, 1),
        halves(br, 0),
        halves(bir, 0),
        halves(aip, 1),
        halves(aiq, 1),
    )


def split(x):
    high = x.astype(BF16)
    low = (x - high.astype(F32)).astype(BF16)
    return high, low


def left_dft(table, x):
    depth = x.shape[0]
    high, low = split(x)
    lhs = jnp.concatenate([table[:, :depth], table], axis=1)
    rhs = jnp.concatenate([high, low, high], axis=0)
    return jnp.dot(lhs, rhs, preferred_element_type=F32)


def right_dft(x, table):
    depth = x.shape[1]
    high, low = split(x)
    lhs = jnp.concatenate([high, low, high], axis=1)
    rhs = jnp.concatenate([table[:depth], table], axis=0)
    return jnp.dot(lhs, rhs, preferred_element_type=F32)


def sin_cos_twelfth(radius):
    turns = jnp.floor(radius * (1.0 / 12.0) + 0.5)
    half = (radius - 12.0 * turns) * (math.pi / 12.0)
    sq = half * half
    s = -2.5052108e-08
    for coef in (2.7557319e-06, -1.9841270e-04, 8.3333333e-03, -1.6666667e-01, 1.0):
        s = s * sq + coef
    s = s * half
    c = 2.0876757e-09
    for coef in (-2.7557319e-07, 2.4801587e-05, -1.3888889e-03, 4.1666667e-02, -0.5, 1.0):
        c = c * sq + coef
    return 2.0 * s * c, 1.0 - 2.0 * s * s


def kernel(
    src, contrast, spec_hbm, meas, cell, pos, aq, ap, br, bir, aip, aiq,
    out_src, out_chi,
    spec_raw, spec, y_buf, r_buf, u_buf, b_buf, inc, amp_sum, scat, res, drive,
    hot, part, half_in, half_sum, ring_in, chi_own, chi, extra, extra_all,
    obj, obj_all, spec_sem, send_sem, recv_sem, tx_send, tx_recv, ex_send, ex_recv,
    ob_send, ob_recv,
):
    me = lax.axis_index("gz")
    tx = lax.axis_index("tx")
    my_y = me // 8
    my_z = lax.rem(me, 8)
    my_x = tx // 2
    core = lax.rem(tx, 2)
    partner = 2 * my_x + 1 - core

    def peer_of(i):
        m = lax.rem(i, 8)
        odd = lax.rem(m, 2)
        dz = odd * ((m + 1) // 2) + (1 - odd) * (8 - m // 2)
        return lax.rem(my_y + i // 8, 4) * 8 + lax.rem(my_z + dz, 8)

    spec_copies = [
        pltpu.make_async_copy(
            spec_hbm.at[:, pl.ds(128 * n, 128)], spec_raw.at[n], spec_sem.at[n]
        )
        for n in range(2)
    ]
    for spec_copy in spec_copies:
        spec_copy.start()

    barrier = pltpu.get_barrier_semaphore()

    @pl.loop(1, GZ)
    def _(i):
        pl.semaphore_signal(barrier, inc=1, device_id={"gz": peer_of(i)}, device_id_type=MESH)

    @pl.loop(1, TX)
    def _(i):
        pl.semaphore_signal(
            barrier, inc=1, device_id={"tx": lax.rem(tx + i, TX)}, device_id_type=MESH
        )

    lane = lax.broadcasted_iota(jnp.int32, (8, 128), 1)
    share = jnp.sum(meas[...] * meas[...], keepdims=True)
    row = jnp.where(lane == 0, pos[0, 0].astype(F32), 0.0)
    row = row + jnp.where(lane == 1, pos[0, 1].astype(F32), 0.0)
    row = row + jnp.where(lane == 2, share, 0.0)
    extra[...] = row
    extra_all[pl.ds(pl.multiple_of(8 * tx, 8), 8), :] = row

    def start(sem_phase, phase, h, s_ref, d_ref):
        def block(g):
            return pl.ds(pl.multiple_of(h * 1024 + 32 * g, 32), 32)

        @pl.loop(1, GZ)
        def _(i):
            to = peer_of(i)
            pltpu.make_async_remote_copy(
                src_ref=s_ref.at[phase, block(to), :],
                dst_ref=d_ref.at[phase, block(me), :],
                send_sem=send_sem.at[sem_phase, h, to],
                recv_sem=recv_sem.at[sem_phase, h, me],
                device_id={"gz": to},
                device_id_type=MESH,
            ).start()

        d_ref[phase, block(me), :] = s_ref[phase, block(me), :]

    def wait(sem_phase, phase, h, s_ref, d_ref, receive):
        def block(g):
            return pl.ds(pl.multiple_of(h * 1024 + 32 * g, 32), 32)

        @pl.loop(1, GZ)
        def _(i):
            other = peer_of(i)
            copy = pltpu.make_async_remote_copy(
                src_ref=s_ref.at[phase, block(other), :],
                dst_ref=d_ref.at[phase, block(other), :],
                send_sem=send_sem.at[sem_phase, h, other],
                recv_sem=recv_sem.at[sem_phase, h, other],
                device_id={"gz": other},
                device_id_type=MESH,
            )
            if receive:
                copy.wait_recv()
            else:
                copy.wait_send()

    def forward_second(field, phase, ready):
        for h in range(2):
            for pp in range(2):
                x = jnp.concatenate(
                    [
                        jnp.concatenate(
                            [field[c, pl.ds((2 * pp + j) * NC, NC), :] for j in range(2)], axis=1
                        )
                        for c in range(2)
                    ],
                    axis=0,
                )
                y = left_dft(aq[pl.ds(h * 256, 256), :], x)
                for g in range(GZ):
                    for j in range(2):
                        y_buf[
                            phase, pl.ds(h * 1024 + g * 32 + (2 * pp + j) * 8, 8), :
                        ] = y[8 * g : 8 * g + 8, j * 128 : j * 128 + 128]
            if h == 0:
                ready()
            start(2 * phase, phase, h, y_buf, r_buf)

    def middle(phase, sign):
        @pl.loop(0, 2)
        def _(h):
            wait(2 * phase, phase, h, y_buf, r_buf, True)

            @pl.loop(0, 2)
            def _(jj):
                cols = []
                for j2 in range(2):
                    rows = []
                    for c in range(2):
                        for p in range(4):
                            rows.append(
                                r_buf[
                                    phase,
                                    pl.ds(h * 1024 + p * 8 + c * 4 + 2 * jj + j2, GZ, stride=32),
                                    :,
                                ]
                            )
                    cols.append(jnp.concatenate(rows, axis=0))
                z = left_dft(ap[...], jnp.concatenate(cols, axis=1))
                outs = []
                for j2 in range(2):
                    lanes = slice(j2 * NC, (j2 + 1) * NC)
                    w = right_dft(jnp.concatenate([z[:NP, lanes], z[NP:, lanes]], axis=1), br[...])
                    re, im = w[:, :NP], w[:, NP:]
                    k = h * 4 + 2 * jj + j2
                    sr, si = spec[0, k], spec[1, k] * sign
                    w = jnp.concatenate([re * sr - im * si, re * si + im * sr], axis=1)
                    v = right_dft(w, bir[...])
                    outs.append(jnp.concatenate([v[:, :NC], v[:, NC:]], axis=0))
                u = left_dft(aip[...], jnp.concatenate(outs, axis=1))
                for g in range(GZ):
                    for j2 in range(2):
                        at = pl.multiple_of(h * 1024 + g * 32 + jj * 16 + j2 * 8, 8)
                        u_buf[phase, pl.ds(at, 8), :] = u[
                            8 * g : 8 * g + 8, j2 * 128 : j2 * 128 + 128
                        ]

            start(2 * phase + 1, phase, h, u_buf, b_buf)

    def inverse_second(phase, pp):
        cols = []
        for j in range(2):
            p = 2 * pp + j
            rows = []
            for c in range(2):
                for h in range(2):
                    for k4 in range(4):
                        rows.append(
                            b_buf[
                                phase,
                                pl.ds(h * 1024 + k4 * 8 + c * 4 + p, GZ, stride=32),
                                :,
                            ]
                        )
            cols.append(jnp.concatenate(rows, axis=0))
        return left_dft(aiq[...], jnp.concatenate(cols, axis=1))

    def first_ready():
        pl.semaphore_wait(barrier, GZ - 1 + TX - 1)

    forward_second(src, 0, first_ready)

    def extra_copy(to, slot):
        return pltpu.make_async_remote_copy(
            src_ref=extra,
            dst_ref=extra_all.at[pl.ds(pl.multiple_of(8 * slot, 8), 8), :],
            send_sem=ex_send.at[to],
            recv_sem=ex_recv.at[slot],
            device_id={"tx": to},
            device_id_type=MESH,
        )

    @pl.loop(1, TX)
    def _(i):
        extra_copy(lax.rem(tx + i, TX), tx).start()

    def geometry(n, rows_n):
        index = lax.broadcasted_iota(jnp.int32, (rows_n, 128), 0) + n * rows_n
        a = lax.shift_right_logical(index, 7) + (me * 4 + NC // 4)
        b = lax.bitwise_and(index, 127)
        c = lax.broadcasted_iota(jnp.int32, (rows_n, 128), 1)
        return a, b, c

    @pl.loop(0, 16)
    def _(n):
        a, b, c = geometry(n, 32)
        b = b - pos[0, 0]
        c = c - pos[0, 1]
        radius = jnp.sqrt((a * a + b * b + c * c).astype(F32))
        amplitude = reach_cells / (reach_cells + radius)
        sine, cosine = sin_cos_twelfth(radius)
        at = pl.ds(pl.multiple_of(n * 32, 32), 32)
        inc[0, at, :] = amplitude * cosine
        inc[1, at, :] = amplitude * sine

    local = cell[...] - me * (ROWS * 128)
    cell_row = lax.shift_right_arithmetic(local, 7)
    cell_lane = lax.bitwise_and(local, 127)

    @pl.loop(0, 16)
    def _(n):
        index = lax.broadcasted_iota(jnp.int32, (32, NREC), 0) + n * 32
        hot[pl.ds(pl.multiple_of(n * 32, 32), 32), :] = jnp.where(
            index == cell_row, 1.0, 0.0
        ).astype(BF16)

    for spec_copy in spec_copies:
        spec_copy.wait()

    @pl.loop(0, 8)
    def _(k):
        for c in range(2):
            for n in range(2):
                spec[c, k, :, pl.ds(n * 128, 128)] = spec_raw[
                    n, pl.ds(c * 2048 + k, NP, stride=8), :
                ] * (2.0 ** -24)

    @pl.loop(1, TX)
    def _(i):
        other = lax.rem(tx + i, TX)
        extra_copy(other, other).wait_recv()

    @pl.loop(0, 16)
    def _(n):
        a, b, c = geometry(n, 32)
        a2 = (a * a).astype(F32)
        bf = b.astype(F32)
        cf = c.astype(F32)
        total = jnp.zeros((32, 128), F32)
        for j in range(TX):
            db = bf - extra_all[8 * j : 8 * j + 1, 0:1]
            dc = cf - extra_all[8 * j : 8 * j + 1, 1:2]
            radius = jnp.sqrt(a2 + db * db + dc * dc)
            amplitude = reach_cells / (reach_cells + radius)
            total = total + amplitude * amplitude
        amp_sum[pl.ds(pl.multiple_of(n * 32, 32), 32), :] = total

    middle(0, 1.0)

    for h in range(2):
        wait(1, 0, h, u_buf, b_buf, True)
    for pp in range(2):
        o = inverse_second(0, pp)
        for j in range(2):
            at = pl.ds((2 * pp + j) * NC, NC)
            lanes = slice(j * NC, (j + 1) * NC)
            for c in range(2):
                scat[c, at, :] = o[c * NC : (c + 1) * NC, lanes]

    @pl.loop(0, 16)
    def _(n):
        at = pl.ds(pl.multiple_of(n * 32, 32), 32)
        sr, si = src[0, at, :], src[1, at, :]
        tr = inc[0, at, :] + scat[0, at, :]
        ti = inc[1, at, :] + scat[1, at, :]
        inc[0, at, :] = tr
        inc[1, at, :] = ti
        part[0, at, :] = sr * tr + si * ti
        part[1, at, :] = si * tr - sr * ti
        part[2, at, :] = tr * tr + ti * ti

    def to_partner(s_ref, d_ref, which):
        return pltpu.make_async_remote_copy(
            src_ref=s_ref,
            dst_ref=d_ref,
            send_sem=tx_send.at[which],
            recv_sem=tx_recv.at[which],
            device_id={"tx": partner},
            device_id_type=MESH,
        )

    def half_rows(which):
        return pl.ds(pl.multiple_of(which * 256, 256), 256)

    core_copy = to_partner(part.at[:, half_rows(1 - core), :], half_in, 0)
    core_copy.start()

    pieces = []
    for c in range(2):
        pieces.append(split(scat[c]))
    columns = jnp.concatenate([pieces[0][0], pieces[1][0], pieces[0][1], pieces[1][1]], axis=1)
    found = lax.dot_general(
        columns, hot[...], (((0,), (0,)), ((), ())), preferred_element_type=F32
    )
    lane_index = lax.broadcasted_iota(jnp.int32, (NC, NREC), 0)
    on_lane = lane_index == cell_lane
    spread = []
    for c in range(2):
        both = found[c * NC : (c + 1) * NC] + found[(2 + c) * NC : (3 + c) * NC]
        sampled = jnp.sum(jnp.where(on_lane, both, 0.0), axis=0, keepdims=True)
        misfit = meas[c : c + 1, :] - sampled
        spread.append(split(jnp.where(on_lane, misfit, 0.0)))
    values = jnp.concatenate([spread[0][0], spread[1][0], spread[0][1], spread[1][1]], axis=0)
    placed = lax.dot_general(
        hot[...], values, (((1,), (1,)), ((), ())), preferred_element_type=F32
    )
    for c in range(2):
        drive[c] = placed[:, c * NC : (c + 1) * NC] + placed[:, (2 + c) * NC : (3 + c) * NC]

    core_copy.wait_recv()
    for q in range(3):
        half_sum[q] = part[q, half_rows(core), :] + half_in[q]

    def quarter(x):
        return pl.ds(pl.multiple_of(x * 64, 64), 64)

    def ring_copy(to, slot):
        return pltpu.make_async_remote_copy(
            src_ref=half_sum.at[:, quarter(to), :],
            dst_ref=ring_in.at[slot],
            send_sem=tx_send.at[1 + to],
            recv_sem=tx_recv.at[1 + slot],
            device_id={"tx": 2 * to + core},
            device_id_type=MESH,
        )

    def own_rows(x):
        return pl.ds(pl.multiple_of(core * 256 + x * 64, 64), 64)

    def chi_copy(to, slot):
        return pltpu.make_async_remote_copy(
            src_ref=chi_own,
            dst_ref=chi.at[:, own_rows(slot), :],
            send_sem=tx_send.at[5 + to],
            recv_sem=tx_recv.at[5 + slot],
            device_id={"tx": 2 * to + core},
            device_id_type=MESH,
        )

    @pl.loop(1, 4)
    def _(i):
        ring_copy(lax.rem(my_x + i, 4), my_x).start()

    ring_in[my_x] = half_sum[:, quarter(my_x), :]

    @pl.loop(1, 4)
    def _(i):
        other = lax.rem(my_x + i, 4)
        ring_copy(other, other).wait_recv()

    sums = []
    for q in range(3):
        sums.append(ring_in[0, q] + ring_in[1, q] + ring_in[2, q] + ring_in[3, q])
    below = sums[2] + tikhonov
    chi_r = (sums[0] + tikhonov * contrast[0, own_rows(my_x), :]) / below
    chi_i = (sums[1] + tikhonov * contrast[1, own_rows(my_x), :]) / below
    chi_own[0] = chi_r
    chi_own[1] = chi_i
    chi[0, own_rows(my_x), :] = chi_r
    chi[1, own_rows(my_x), :] = chi_i

    @pl.loop(1, 4)
    def _(i):
        chi_copy(lax.rem(my_x + i, 4), my_x).start()

    @pl.loop(1, 4)
    def _(i):
        other = lax.rem(my_x + i, 4)
        chi_copy(other, other).wait_recv()

    mine = chi.at[:, half_rows(core), :]
    theirs = chi.at[:, half_rows(1 - core), :]
    chi_send = to_partner(mine, mine, 9)
    chi_send.start()
    to_partner(theirs, theirs, 9).wait_recv()

    zero = jnp.zeros((32, 128), F32)

    def object_step(n, acc):
        at = pl.ds(pl.multiple_of(n * 32, 32), 32)
        cr, ci = chi[0, at, :], chi[1, at, :]
        out_chi[0, at, :] = cr
        out_chi[1, at, :] = ci
        return acc + (cr * cr + ci * ci) * amp_sum[at, :]

    acc = lax.fori_loop(0, 16, object_step, zero)
    own = acc[0:8] + acc[8:16] + acc[16:24] + acc[24:32]
    obj[...] = own
    obj_all[pl.ds(pl.multiple_of(8 * me, 8), 8), :] = own

    def obj_copy(to, slot):
        return pltpu.make_async_remote_copy(
            src_ref=obj,
            dst_ref=obj_all.at[pl.ds(pl.multiple_of(8 * slot, 8), 8), :],
            send_sem=ob_send.at[to],
            recv_sem=ob_recv.at[slot],
            device_id={"gz": to},
            device_id_type=MESH,
        )

    @pl.loop(1, GZ)
    def _(i):
        obj_copy(peer_of(i), me).start()

    @pl.loop(0, 16)
    def _(n):
        at = pl.ds(pl.multiple_of(n * 32, 32), 32)
        cr, ci = chi[0, at, :], chi[1, at, :]
        tr, ti = inc[0, at, :], inc[1, at, :]
        rr = cr * tr - ci * ti - src[0, at, :]
        ri = cr * ti + ci * tr - src[1, at, :]
        res[0, at, :] = rr
        res[1, at, :] = ri
        scat[0, at, :] = cr * rr + ci * ri
        scat[1, at, :] = cr * ri - ci * rr

    @pl.loop(1, GZ)
    def _(i):
        other = peer_of(i)
        obj_copy(other, other).wait_recv()

    object_norm = jnp.sum(obj_all[...], keepdims=True)
    data_norm = jnp.zeros((1, 1), F32)
    for j in range(TX):
        data_norm = data_norm + extra_all[8 * j : 8 * j + 1, 2:3]
    ratio = object_norm / (data_norm + norm_floor)

    @pl.loop(0, 16)
    def _(n):
        at = pl.ds(pl.multiple_of(n * 32, 32), 32)
        drive[0, at, :] = ratio * drive[0, at, :] - scat[0, at, :]
        drive[1, at, :] = ratio * drive[1, at, :] - scat[1, at, :]

    forward_second(drive, 1, lambda: None)
    middle(1, -1.0)
    for h in range(2):
        wait(3, 1, h, u_buf, b_buf, True)
    for pp in range(2):
        o = inverse_second(1, pp)
        for j in range(2):
            at = pl.ds((2 * pp + j) * NC, NC)
            lanes = slice(j * NC, (j + 1) * NC)
            for c in range(2):
                back = o[c * NC : (c + 1) * NC, lanes]
                out_src[c, at, :] = src[c, at, :] + step_length * (res[c, at, :] + back)

    for h in range(2):
        wait(0, 0, h, y_buf, r_buf, False)
        wait(1, 0, h, u_buf, b_buf, False)
        wait(2, 1, h, y_buf, r_buf, False)
        wait(3, 1, h, u_buf, b_buf, False)

    @pl.loop(1, GZ)
    def _(i):
        other = peer_of(i)
        obj_copy(other, other).wait_send()

    @pl.loop(1, TX)
    def _(i):
        other = lax.rem(tx + i, TX)
        extra_copy(other, other).wait_send()

    @pl.loop(1, 4)
    def _(i):
        other = lax.rem(my_x + i, 4)
        ring_copy(other, other).wait_send()
        chi_copy(other, other).wait_send()

    core_copy.wait_send()
    chi_send.wait_send()


def shards(sources, contrast, spectrum, measured, receivers, positions):
    vmem = pl.BlockSpec(memory_space=pltpu.VMEM)
    tables = [jnp.asarray(table) for table in dft_tables()]
    field = jax.ShapeDtypeStruct((2, ROWS, 128), F32)

    def buf(*shape):
        return pltpu.VMEM(shape, F32)

    dma = pltpu.SemaphoreType.DMA
    new, chi = pl.pallas_call(
        kernel,
        out_shape=(field, field),
        in_specs=[
            vmem,
            vmem,
            pl.BlockSpec(memory_space=pl.ANY),
            vmem,
            vmem,
            pl.BlockSpec(memory_space=pltpu.SMEM),
        ]
        + [vmem] * 6,
        out_specs=(vmem, vmem),
        scratch_shapes=[
            buf(2, 4096, 128),
            buf(2, 8, NP, NP),
            buf(2, 2048, 128),
            buf(2, 2048, 128),
            buf(2, 2048, 128),
            buf(2, 2048, 128),
            buf(2, ROWS, 128),
            buf(ROWS, 128),
            buf(2, ROWS, 128),
            buf(2, ROWS, 128),
            buf(2, ROWS, 128),
            pltpu.VMEM((ROWS, NREC), BF16),
            buf(3, ROWS, 128),
            buf(3, 256, 128),
            buf(3, 256, 128),
            buf(4, 3, 64, 128),
            buf(2, 64, 128),
            buf(2, ROWS, 128),
            buf(8, 128),
            buf(64, 128),
            buf(8, 128),
            buf(256, 128),
            dma((2,)),
            dma((4, 2, GZ)),
            dma((4, 2, GZ)),
            dma((10,)),
            dma((10,)),
            dma((TX,)),
            dma((TX,)),
            dma((GZ,)),
            dma((GZ,)),
        ],
        compiler_params=pltpu.CompilerParams(
            collective_id=0, has_side_effects=True, vmem_limit_bytes=60 * 1024 * 1024
        ),
    )(
        sources.reshape(2, ROWS, 128),
        contrast.reshape(2, ROWS, 128),
        spectrum.reshape(4096, NP),
        measured.reshape(2, NREC),
        receivers,
        positions,
        *tables,
    )
    return new.reshape(sources.shape), chi.reshape(contrast.shape)


def solution(mesh):
    in_specs = (
        P("tx", None, "gz", None, None),
        P(None, "gz", None, None),
        P(None, None, "gz", None),
        P("tx", None, None),
        P("tx", None),
        P("tx", None),
    )
    out_specs = (P("tx", None, "gz", None, None), P(None, "gz", None, None))
    return jax.shard_map(shards, mesh=mesh, in_specs=in_specs, out_specs=out_specs, check_vma=False)
```

```python
import math

import jax
import jax.numpy as jnp
import numpy as np
from jax import lax
from jax.experimental import pallas as pl
from jax.experimental.pallas import tpu as pltpu
from jax.sharding import PartitionSpec as P

MESH = pl.DeviceIdType.MESH
F32 = jnp.float32
BF16 = jnp.bfloat16

reach_cells = 16.0
tikhonov = 1.0
step_length = 0.5
norm_floor = 1e-06

NC = 128
NP = 256
GZ = 32
TX = 8
NREC = 1024
ROWS = 512


def dft_matrix():
    k = np.arange(NP)[:, None]
    n = np.arange(NC)[None, :]
    angle = 2.0 * np.pi * ((k * n) % NP) / NP
    cosine, sine = np.cos(angle), np.sin(angle)
    full = np.zeros((2, NP, 2, NC))
    full[0, :, 0, :] = cosine
    full[0, :, 1, :] = sine
    full[1, :, 0, :] = -sine
    full[1, :, 1, :] = cosine
    return full


def halves(table, axis):
    table = table.astype(np.float32)
    high = table.astype(jnp.bfloat16)
    low = (table - high.astype(np.float32)).astype(jnp.bfloat16)
    return np.concatenate([high, low], axis)


def dft_tables():
    full = dft_matrix()
    by_freq = full.reshape(2, GZ, 2, 4, 2, NC)
    by_pair = full.reshape(2, GZ, 4, 2, 2, NC)
    by_plane = full.reshape(2, NP, 2, GZ, 4)
    by_half = full.reshape(2, NP, 2, GZ, 2, 2)
    aq = by_freq.transpose(2, 1, 0, 3, 4, 5).reshape(2 * NP, 2 * NC)
    ap = by_plane.transpose(0, 1, 2, 4, 3).reshape(2 * NP, 2 * NC)
    br = full.transpose(2, 3, 0, 1).reshape(2 * NC, 2 * NP)
    bir = full.reshape(2 * NP, 2 * NC)
    aip = by_half.transpose(3, 4, 2, 5, 0, 1).reshape(2 * NC, 2 * NP)
    aiq = by_pair.transpose(4, 5, 0, 2, 3, 1).reshape(2 * NC, 2 * NP)
    return (
        halves(aq, 1),
        halves(ap, 1),
        halves(br, 0),
        halves(bir, 0),
        halves(aip, 1),
        halves(aiq, 1),
    )


def split(x):
    high = x.astype(BF16)
    low = (x - high.astype(F32)).astype(BF16)
    return high, low


def left_dft(table, x):
    depth = x.shape[0]
    high, low = split(x)
    lhs = jnp.concatenate([table[:, :depth], table], axis=1)
    rhs = jnp.concatenate([high, low, high], axis=0)
    return jnp.dot(lhs, rhs, preferred_element_type=F32)


def right_dft(x, table):
    depth = x.shape[1]
    high, low = split(x)
    lhs = jnp.concatenate([high, low, high], axis=1)
    rhs = jnp.concatenate([table[:depth], table], axis=0)
    return jnp.dot(lhs, rhs, preferred_element_type=F32)


def sin_cos_twelfth(radius):
    turns = jnp.floor(radius * (1.0 / 12.0) + 0.5)
    half = (radius - 12.0 * turns) * (math.pi / 12.0)
    sq = half * half
    s = -2.5052108e-08
    for coef in (2.7557319e-06, -1.9841270e-04, 8.3333333e-03, -1.6666667e-01, 1.0):
        s = s * sq + coef
    s = s * half
    c = 2.0876757e-09
    for coef in (-2.7557319e-07, 2.4801587e-05, -1.3888889e-03, 4.1666667e-02, -0.5, 1.0):
        c = c * sq + coef
    return 2.0 * s * c, 1.0 - 2.0 * s * s


def kernel(
    src, contrast, spec_hbm, meas, cell, pos, aq, ap, br, bir, aip, aiq,
    out_src, out_chi,
    spec_raw, spec, y_buf, r_buf, u_buf, b_buf, inc, amp_sum, scat, res, drive,
    hot, hot_plane, part, half_in, half_sum, ring_in, chi_own, chi, extra, extra_all,
    obj, obj_all, mf, mf_in, mf_own, mf_all, placed_freq,
    spec_sem, send_sem, recv_sem, tx_send, tx_recv, ex_send, ex_recv,
    ob_send, ob_recv, ma_send, ma_recv, mb_send, mb_recv,
):
    me = lax.axis_index("gz")
    tx = lax.axis_index("tx")
    my_y = me // 8
    my_z = lax.rem(me, 8)
    my_x = tx // 2
    core = lax.rem(tx, 2)
    partner = 2 * my_x + 1 - core

    def peer_of(i):
        m = lax.rem(i, 8)
        odd = lax.rem(m, 2)
        dz = odd * ((m + 1) // 2) + (1 - odd) * (8 - m // 2)
        return lax.rem(my_y + i // 8, 4) * 8 + lax.rem(my_z + dz, 8)

    spec_copies = [
        pltpu.make_async_copy(
            spec_hbm.at[:, pl.ds(128 * n, 128)], spec_raw.at[n], spec_sem.at[n]
        )
        for n in range(2)
    ]
    for spec_copy in spec_copies:
        spec_copy.start()

    barrier = pltpu.get_barrier_semaphore()

    @pl.loop(1, GZ)
    def _(i):
        pl.semaphore_signal(barrier, inc=1, device_id={"gz": peer_of(i)}, device_id_type=MESH)

    @pl.loop(1, TX)
    def _(i):
        pl.semaphore_signal(
            barrier, inc=1, device_id={"tx": lax.rem(tx + i, TX)}, device_id_type=MESH
        )

    lane = lax.broadcasted_iota(jnp.int32, (8, 128), 1)
    share = jnp.sum(meas[...] * meas[...], keepdims=True)
    row = jnp.where(lane == 0, pos[0, 0].astype(F32), 0.0)
    row = row + jnp.where(lane == 1, pos[0, 1].astype(F32), 0.0)
    row = row + jnp.where(lane == 2, share, 0.0)
    extra[...] = row
    extra_all[pl.ds(pl.multiple_of(8 * tx, 8), 8), :] = row

    def exchange_copy(sem_phase, chunk, offset, size, s_ref, d_ref, to, slot):
        phase = sem_phase // 2

        def block(g):
            return pl.ds(pl.multiple_of(offset + 32 * g, 8), size)

        return pltpu.make_async_remote_copy(
            src_ref=s_ref.at[phase, block(to), :],
            dst_ref=d_ref.at[phase, block(slot), :],
            send_sem=send_sem.at[sem_phase, chunk, to],
            recv_sem=recv_sem.at[sem_phase, chunk, slot],
            device_id={"gz": to},
            device_id_type=MESH,
        )

    def start(sem_phase, chunk, offset, size, s_ref, d_ref):
        @pl.loop(1, GZ)
        def _(i):
            exchange_copy(sem_phase, chunk, offset, size, s_ref, d_ref, peer_of(i), me).start()

        phase = sem_phase // 2
        own = pl.ds(pl.multiple_of(offset + 32 * me, 8), size)
        d_ref[phase, own, :] = s_ref[phase, own, :]

    def wait(sem_phase, chunk, offset, size, s_ref, d_ref, receive=True):
        @pl.loop(1, GZ)
        def _(i):
            other = peer_of(i)
            copy = exchange_copy(sem_phase, chunk, offset, size, s_ref, d_ref, other, other)
            if receive:
                copy.wait_recv()
            else:
                copy.wait_send()

    back_chunks = ((0, 16), (16, 8), (24, 8), (1024, 32))

    def forward_second(field, phase, h, ph):
        x = jnp.concatenate(
            [
                jnp.concatenate(
                    [field[c, pl.ds((2 * ph + j) * NC, NC), :] for j in range(2)], axis=1
                )
                for c in range(2)
            ],
            axis=0,
        )
        y = left_dft(aq[pl.ds(h * 256, 256), :], x)
        for g in range(GZ):
            for j in range(2):
                y_buf[phase, pl.ds(h * 1024 + g * 32 + (2 * ph + j) * 8, 8), :] = y[
                    8 * g : 8 * g + 8, j * 128 : j * 128 + 128
                ]

    def middle(phase, sign, ratio):
        @pl.loop(0, 4)
        def _(kk):
            h = kk // 2

            @pl.when(lax.rem(kk, 2) == 0)
            def _():
                if phase == 0:
                    wait(0, h, h * 1024, 32, y_buf, r_buf)
                else:
                    for ph in range(2):
                        wait(2, 2 * ph + h, h * 1024 + ph * 16, 16, y_buf, r_buf)

            cols = []
            for i in range(2):
                rows = []
                for c in range(2):
                    for p in range(4):
                        first = h * 1024 + p * 8 + c * 4 + 2 * lax.rem(kk, 2) + i
                        x = r_buf[phase, pl.ds(first, GZ, stride=32), :]
                        if ratio is not None:
                            x = x + ratio * placed_freq[
                                2 * kk + i, c * NC + p * GZ : c * NC + (p + 1) * GZ, :
                            ]
                        rows.append(x)
                cols.append(jnp.concatenate(rows, axis=0))
            z = left_dft(ap[...], jnp.concatenate(cols, axis=1))
            outs = []
            for i in range(2):
                lanes = slice(i * NC, (i + 1) * NC)
                w = right_dft(jnp.concatenate([z[:NP, lanes], z[NP:, lanes]], axis=1), br[...])
                re, im = w[:, :NP], w[:, NP:]
                sr, si = spec[0, 2 * kk + i], spec[1, 2 * kk + i] * sign
                w = jnp.concatenate([re * sr - im * si, re * si + im * sr], axis=1)
                v = right_dft(w, bir[...])
                outs.append(jnp.concatenate([v[:, :NC], v[:, NC:]], axis=0))
            u = left_dft(aip[...], jnp.concatenate(outs, axis=1))
            upper = lax.bitwise_and(lax.broadcasted_iota(jnp.int32, (256, NC), 0), 4) != 0
            even, odd = u[:, :NC], u[:, NC:]
            halves_of_u = (
                jnp.where(upper, pltpu.roll(odd, 4, 0), even),
                jnp.where(upper, odd, pltpu.roll(even, 252, 0)),
            )
            for ph in range(2):
                for g in range(GZ):
                    at = pl.multiple_of(ph * 1024 + g * 32 + kk * 8, 8)
                    u_buf[phase, pl.ds(at, 8), :] = halves_of_u[ph][8 * g : 8 * g + 8]

            for at_kk, chunks in ((1, (0,)), (2, (1,)), (3, (2, 3))):

                @pl.when(kk == at_kk)
                def _():
                    for chunk in chunks:
                        start(2 * phase + 1, chunk, *back_chunks[chunk], u_buf, b_buf)

    def wait_back(phase, ph):
        for chunk in ((0, 1, 2), (3,))[ph]:
            wait(2 * phase + 1, chunk, *back_chunks[chunk], u_buf, b_buf)

    def inverse_second(phase, ph):
        cols = []
        for p2 in range(2):
            rows = []
            for c in range(2):
                for kk in range(4):
                    for i in range(2):
                        first = ph * 1024 + kk * 8 + i * 4 + c * 2 + p2
                        rows.append(b_buf[phase, pl.ds(first, GZ, stride=32), :])
            cols.append(jnp.concatenate(rows, axis=0))
        return left_dft(aiq[...], jnp.concatenate(cols, axis=1))

    for h in range(2):
        for ph in range(2):
            forward_second(src, 0, h, ph)
        if h == 0:
            pl.semaphore_wait(barrier, GZ - 1 + TX - 1)
        start(0, h, h * 1024, 32, y_buf, r_buf)

    def extra_copy(to, slot):
        return pltpu.make_async_remote_copy(
            src_ref=extra,
            dst_ref=extra_all.at[pl.ds(pl.multiple_of(8 * slot, 8), 8), :],
            send_sem=ex_send.at[to],
            recv_sem=ex_recv.at[slot],
            device_id={"tx": to},
            device_id_type=MESH,
        )

    @pl.loop(1, TX)
    def _(i):
        extra_copy(lax.rem(tx + i, TX), tx).start()

    def geometry(n, rows_n):
        index = lax.broadcasted_iota(jnp.int32, (rows_n, 128), 0) + n * rows_n
        a = lax.shift_right_logical(index, 7) + (me * 4 + NC // 4)
        b = lax.bitwise_and(index, 127)
        c = lax.broadcasted_iota(jnp.int32, (rows_n, 128), 1)
        return a, b, c

    @pl.loop(0, 16)
    def _(n):
        a, b, c = geometry(n, 32)
        b = b - pos[0, 0]
        c = c - pos[0, 1]
        radius = jnp.sqrt((a * a + b * b + c * c).astype(F32))
        amplitude = reach_cells / (reach_cells + radius)
        sine, cosine = sin_cos_twelfth(radius)
        at = pl.ds(pl.multiple_of(n * 32, 32), 32)
        inc[0, at, :] = amplitude * cosine
        inc[1, at, :] = amplitude * sine

    local = cell[...] - me * (ROWS * 128)
    cell_row = lax.shift_right_arithmetic(local, 7)
    cell_lane = lax.bitwise_and(local, 127)

    @pl.loop(0, 16)
    def _(n):
        index = lax.broadcasted_iota(jnp.int32, (32, NREC), 0) + n * 32
        hot[pl.ds(pl.multiple_of(n * 32, 32), 32), :] = jnp.where(
            index == cell_row, 1.0, 0.0
        ).astype(BF16)

    row_index = lax.broadcasted_iota(jnp.int32, (NC, NREC), 0)
    plane = 4 * lax.bitwise_and(row_index, 31) + lax.shift_right_logical(row_index, 5)
    hot_plane[...] = jnp.where(
        plane == lax.shift_right_logical(cell[...], 14), 1.0, 0.0
    ).astype(BF16)

    for spec_copy in spec_copies:
        spec_copy.wait()

    @pl.loop(0, 8)
    def _(k):
        for c in range(2):
            for n in range(2):
                spec[c, k, :, pl.ds(n * 128, 128)] = spec_raw[
                    n, pl.ds(c * 2048 + k, NP, stride=8), :
                ] * (2.0 ** -24)

    @pl.loop(1, TX)
    def _(i):
        other = lax.rem(tx + i, TX)
        extra_copy(other, other).wait_recv()

    @pl.loop(0, 16)
    def _(n):
        a, b, c = geometry(n, 32)
        a2 = (a * a).astype(F32)
        bf = b.astype(F32)
        cf = c.astype(F32)
        total = jnp.zeros((32, 128), F32)
        for j in range(TX):
            db = bf - extra_all[8 * j : 8 * j + 1, 0:1]
            dc = cf - extra_all[8 * j : 8 * j + 1, 1:2]
            radius = jnp.sqrt(a2 + db * db + dc * dc)
            amplitude = reach_cells / (reach_cells + radius)
            total = total + amplitude * amplitude
        amp_sum[pl.ds(pl.multiple_of(n * 32, 32), 32), :] = total

    middle(0, 1.0, None)

    def to_partner(s_ref, d_ref, which):
        return pltpu.make_async_remote_copy(
            src_ref=s_ref,
            dst_ref=d_ref,
            send_sem=tx_send.at[which],
            recv_sem=tx_recv.at[which],
            device_id={"tx": partner},
            device_id_type=MESH,
        )

    def plane_rows(p):
        return pl.ds(pl.multiple_of(p * NC, NC), NC)

    def core_copy(ph):
        return to_partner(part.at[:, plane_rows(2 * ph + 1 - core), :], half_in.at[ph], 10 * ph)

    def ring_copy(ph, to, slot):
        return pltpu.make_async_remote_copy(
            src_ref=half_sum.at[ph, :, pl.ds(pl.multiple_of(to * 32, 32), 32), :],
            dst_ref=ring_in.at[ph, slot],
            send_sem=tx_send.at[10 * ph + 1 + to],
            recv_sem=tx_recv.at[10 * ph + 1 + slot],
            device_id={"tx": 2 * to + core},
            device_id_type=MESH,
        )

    def own_rows(ph, x):
        return pl.ds(pl.multiple_of((2 * ph + core) * NC + x * 32, 32), 32)

    def chi_copy(ph, to, slot):
        return pltpu.make_async_remote_copy(
            src_ref=chi_own.at[ph],
            dst_ref=chi.at[:, own_rows(ph, slot), :],
            send_sem=tx_send.at[10 * ph + 5 + to],
            recv_sem=tx_recv.at[10 * ph + 5 + slot],
            device_id={"tx": 2 * to + core},
            device_id_type=MESH,
        )

    def chi_send(ph, which):
        at = chi.at[:, plane_rows(2 * ph + which), :]
        return to_partner(at, at, 10 * ph + 9)

    def fields(ph):
        wait_back(0, ph)
        o = inverse_second(0, ph)
        for j in range(2):
            at = pl.ds((2 * ph + j) * NC, NC)
            for c in range(2):
                scat[c, at, :] = o[c * NC : (c + 1) * NC, j * NC : (j + 1) * NC]

        @pl.loop(0, 8)
        def _(n):
            at = pl.ds(pl.multiple_of(ph * 256 + n * 32, 32), 32)
            sr, si = src[0, at, :], src[1, at, :]
            tr = inc[0, at, :] + scat[0, at, :]
            ti = inc[1, at, :] + scat[1, at, :]
            inc[0, at, :] = tr
            inc[1, at, :] = ti
            part[0, at, :] = sr * tr + si * ti
            part[1, at, :] = si * tr - sr * ti
            part[2, at, :] = tr * tr + ti * ti

        core_copy(ph).start()

    def ring_start(ph):
        core_copy(ph).wait_recv()
        for q in range(3):
            half_sum[ph, q] = part[q, plane_rows(2 * ph + core), :] + half_in[ph, q]

        @pl.loop(1, 4)
        def _(i):
            ring_copy(ph, lax.rem(my_x + i, 4), my_x).start()

        ring_in[ph, my_x] = half_sum[ph, :, pl.ds(pl.multiple_of(my_x * 32, 32), 32), :]

    def contrast_start(ph):
        @pl.loop(1, 4)
        def _(i):
            other = lax.rem(my_x + i, 4)
            ring_copy(ph, other, other).wait_recv()

        sums = []
        for q in range(3):
            sums.append(
                ring_in[ph, 0, q] + ring_in[ph, 1, q] + ring_in[ph, 2, q] + ring_in[ph, 3, q]
            )
        below = sums[2] + tikhonov
        rows = own_rows(ph, my_x)
        for c in range(2):
            value = (sums[c] + tikhonov * contrast[c, rows, :]) / below
            chi_own[ph, c] = value
            chi[c, rows, :] = value

        @pl.loop(1, 4)
        def _(i):
            chi_copy(ph, lax.rem(my_x + i, 4), my_x).start()

    def contrast_forward(ph):
        @pl.loop(1, 4)
        def _(i):
            other = lax.rem(my_x + i, 4)
            chi_copy(ph, other, other).wait_recv()

        chi_send(ph, core).start()

    def residual(ph, acc):
        chi_send(ph, 1 - core).wait_recv()

        def step(n, acc):
            at = pl.ds(pl.multiple_of(ph * 256 + n * 32, 32), 32)
            cr, ci = chi[0, at, :], chi[1, at, :]
            out_chi[0, at, :] = cr
            out_chi[1, at, :] = ci
            tr, ti = inc[0, at, :], inc[1, at, :]
            rr = cr * tr - ci * ti - src[0, at, :]
            ri = cr * ti + ci * tr - src[1, at, :]
            res[0, at, :] = rr
            res[1, at, :] = ri
            drive[0, at, :] = -(cr * rr + ci * ri)
            drive[1, at, :] = -(cr * ri - ci * rr)
            return acc + (cr * cr + ci * ci) * amp_sum[at, :]

        return lax.fori_loop(0, 8, step, acc)

    def drive_start(ph):
        for h in range(2):
            forward_second(drive, 1, h, ph)
            start(2, 2 * ph + h, h * 1024 + ph * 16, 16, y_buf, r_buf)

    def misfit_copy(to, slot):
        return pltpu.make_async_remote_copy(
            src_ref=mf.at[to // 4],
            dst_ref=mf_in.at[slot],
            send_sem=ma_send.at[to],
            recv_sem=ma_recv.at[slot],
            device_id={"gz": to},
            device_id_type=MESH,
        )

    def misfit_back(to, slot):
        return pltpu.make_async_remote_copy(
            src_ref=mf_own,
            dst_ref=mf_all.at[slot // 4],
            send_sem=mb_send.at[to // 4],
            recv_sem=mb_recv.at[slot // 4],
            device_id={"gz": to},
            device_id_type=MESH,
        )

    def group_peer(i):
        return lax.rem(me + 4 * i, GZ)

    lane_index = lax.broadcasted_iota(jnp.int32, (NC, NREC), 0)

    def misfit_start():
        pieces = [split(scat[c]) for c in range(2)]
        columns = jnp.concatenate(
            [pieces[0][0], pieces[1][0], pieces[0][1], pieces[1][1]], axis=1
        )
        found = lax.dot_general(
            columns, hot[...], (((0,), (0,)), ((), ())), preferred_element_type=F32
        )
        on_lane = lane_index == cell_lane
        inside = (cell_row >= 0) & (cell_row < ROWS)
        misfit = []
        for c in range(2):
            both = found[c * NC : (c + 1) * NC] + found[(2 + c) * NC : (3 + c) * NC]
            sampled = jnp.sum(jnp.where(on_lane, both, 0.0), axis=0, keepdims=True)
            misfit.append(jnp.where(inside, meas[c : c + 1, :] - sampled, 0.0))
        rest = jnp.zeros((6, 128), F32)
        for i in range(8):
            at = slice(i * 128, (i + 1) * 128)
            mf[i] = jnp.concatenate([misfit[0][:, at], misfit[1][:, at], rest], axis=0)
        mf_in[me] = mf[me // 4]

        @pl.loop(1, GZ)
        def _(i):
            misfit_copy(peer_of(i), me).start()

    def misfit_forward():
        @pl.loop(1, GZ)
        def _(i):
            other = peer_of(i)
            misfit_copy(other, other).wait_recv()

        total = mf_in[0]
        for g in range(1, GZ):
            total = total + mf_in[g]
        mf_own[...] = total
        mf_all[me // 4] = total

        @pl.loop(1, 8)
        def _(i):
            misfit_back(group_peer(i), me).start()

    def placed_spectrum():
        @pl.loop(1, 8)
        def _(i):
            other = group_peer(i)
            misfit_back(other, other).wait_recv()

        mr = jnp.concatenate([mf_all[i, 0:1, :] for i in range(8)], axis=1)
        mi = jnp.concatenate([mf_all[i, 1:2, :] for i in range(8)], axis=1)
        second = lax.bitwise_and(lax.shift_right_logical(cell[...], 7), 127)

        @pl.loop(0, 8)
        def _(k):
            turn = lax.bitwise_and((8 * me + k) * second, 255)
            sine, cosine = sin_cos_twelfth(turn.astype(F32) * (12.0 / 256.0))
            on_lane = lane_index == cell_lane
            v = (
                split(jnp.where(on_lane, mr * cosine + mi * sine, 0.0)),
                split(jnp.where(on_lane, mi * cosine - mr * sine, 0.0)),
            )
            values = jnp.concatenate([v[0][0], v[1][0], v[0][1], v[1][1]], axis=0)
            found = lax.dot_general(
                hot_plane[...], values, (((1,), (1,)), ((), ())), preferred_element_type=F32
            )
            for c in range(2):
                placed_freq[k, pl.ds(c * NC, NC), :] = (
                    found[:, c * NC : (c + 1) * NC] + found[:, (2 + c) * NC : (3 + c) * NC]
                )

    def obj_copy(to, slot):
        return pltpu.make_async_remote_copy(
            src_ref=obj,
            dst_ref=obj_all.at[pl.ds(pl.multiple_of(8 * slot, 8), 8), :],
            send_sem=ob_send.at[to],
            recv_sem=ob_recv.at[slot],
            device_id={"gz": to},
            device_id_type=MESH,
        )

    def object_start(acc):
        own = acc[0:8] + acc[8:16] + acc[16:24] + acc[24:32]
        obj[...] = own
        obj_all[pl.ds(pl.multiple_of(8 * me, 8), 8), :] = own

        @pl.loop(1, GZ)
        def _(i):
            obj_copy(peer_of(i), me).start()

    def object_ratio():
        @pl.loop(1, GZ)
        def _(i):
            other = peer_of(i)
            obj_copy(other, other).wait_recv()

        object_norm = jnp.sum(obj_all[...], keepdims=True)
        data_norm = jnp.zeros((1, 1), F32)
        for j in range(TX):
            data_norm = data_norm + extra_all[8 * j : 8 * j + 1, 2:3]
        return object_norm / (data_norm + norm_floor)

    fields(0)
    ring_start(0)
    contrast_start(0)
    contrast_forward(0)
    fields(1)
    acc = residual(0, jnp.zeros((32, 128), F32))
    drive_start(0)
    ring_start(1)
    misfit_start()
    contrast_start(1)
    misfit_forward()
    contrast_forward(1)
    acc = residual(1, acc)
    object_start(acc)
    drive_start(1)
    placed_spectrum()
    middle(1, -1.0, object_ratio())
    for ph in range(2):
        wait_back(1, ph)
        o = inverse_second(1, ph)
        for j in range(2):
            at = pl.ds((2 * ph + j) * NC, NC)
            for c in range(2):
                back = o[c * NC : (c + 1) * NC, j * NC : (j + 1) * NC]
                out_src[c, at, :] = src[c, at, :] + step_length * (res[c, at, :] + back)

    for h in range(2):
        wait(0, h, h * 1024, 32, y_buf, r_buf, False)
        for ph in range(2):
            wait(2, 2 * ph + h, h * 1024 + ph * 16, 16, y_buf, r_buf, False)
    for phase in range(2):
        for chunk in range(4):
            wait(2 * phase + 1, chunk, *back_chunks[chunk], u_buf, b_buf, False)

    @pl.loop(1, GZ)
    def _(i):
        other = peer_of(i)
        obj_copy(other, other).wait_send()
        misfit_copy(other, other).wait_send()

    @pl.loop(1, TX)
    def _(i):
        other = lax.rem(tx + i, TX)
        extra_copy(other, other).wait_send()

    @pl.loop(1, 8)
    def _(i):
        other = group_peer(i)
        misfit_back(other, other).wait_send()

    for ph in range(2):

        @pl.loop(1, 4)
        def _(i):
            other = lax.rem(my_x + i, 4)
            ring_copy(ph, other, other).wait_send()
            chi_copy(ph, other, other).wait_send()

        core_copy(ph).wait_send()
        chi_send(ph, core).wait_send()


def shards(sources, contrast, spectrum, measured, receivers, positions):
    vmem = pl.BlockSpec(memory_space=pltpu.VMEM)
    tables = [jnp.asarray(table) for table in dft_tables()]
    field = jax.ShapeDtypeStruct((2, ROWS, 128), F32)

    def buf(*shape):
        return pltpu.VMEM(shape, F32)

    dma = pltpu.SemaphoreType.DMA
    new, chi = pl.pallas_call(
        kernel,
        out_shape=(field, field),
        in_specs=[
            vmem,
            vmem,
            pl.BlockSpec(memory_space=pl.ANY),
            vmem,
            vmem,
            pl.BlockSpec(memory_space=pltpu.SMEM),
        ]
        + [vmem] * 6,
        out_specs=(vmem, vmem),
        scratch_shapes=[
            buf(2, 4096, 128),
            buf(2, 8, NP, NP),
            buf(2, 2048, 128),
            buf(2, 2048, 128),
            buf(2, 2048, 128),
            buf(2, 2048, 128),
            buf(2, ROWS, 128),
            buf(ROWS, 128),
            buf(2, ROWS, 128),
            buf(2, ROWS, 128),
            buf(2, ROWS, 128),
            pltpu.VMEM((ROWS, NREC), BF16),
            pltpu.VMEM((NC, NREC), BF16),
            buf(3, ROWS, 128),
            buf(2, 3, NC, 128),
            buf(2, 3, NC, 128),
            buf(2, 4, 3, 32, 128),
            buf(2, 2, 32, 128),
            buf(2, ROWS, 128),
            buf(8, 128),
            buf(64, 128),
            buf(8, 128),
            buf(256, 128),
            buf(8, 8, 128),
            buf(GZ, 8, 128),
            buf(8, 128),
            buf(8, 8, 128),
            buf(8, 2 * NC, 128),
            dma((2,)),
            dma((4, 4, GZ)),
            dma((4, 4, GZ)),
            dma((20,)),
            dma((20,)),
            dma((TX,)),
            dma((TX,)),
            dma((GZ,)),
            dma((GZ,)),
            dma((GZ,)),
            dma((GZ,)),
            dma((8,)),
            dma((8,)),
        ],
        compiler_params=pltpu.CompilerParams(
            collective_id=0, has_side_effects=True, vmem_limit_bytes=60 * 1024 * 1024
        ),
    )(
        sources.reshape(2, ROWS, 128),
        contrast.reshape(2, ROWS, 128),
        spectrum.reshape(4096, NP),
        measured.reshape(2, NREC),
        receivers,
        positions,
        *tables,
    )
    return new.reshape(sources.shape), chi.reshape(contrast.shape)


def solution(mesh):
    in_specs = (
        P("tx", None, "gz", None, None),
        P(None, "gz", None, None),
        P(None, None, "gz", None),
        P("tx", None, None),
        P("tx", None),
        P("tx", None),
    )
    out_specs = (P("tx", None, "gz", None, None), P(None, "gz", None, None))
    return jax.shard_map(shards, mesh=mesh, in_specs=in_specs, out_specs=out_specs, check_vma=False)
```

```python
import math

import jax
import jax.numpy as jnp
import numpy as np
from jax import lax
from jax.experimental import pallas as pl
from jax.experimental.pallas import tpu as pltpu
from jax.sharding import PartitionSpec as P

MESH = pl.DeviceIdType.MESH
F32 = jnp.float32
BF16 = jnp.bfloat16

reach_cells = 16.0
tikhonov = 1.0
step_length = 0.5
norm_floor = 1e-06

NC = 128
NP = 256
GZ = 32
TX = 8
NREC = 1024
ROWS = 512


def dft_matrix():
    k = np.arange(NP)[:, None]
    n = np.arange(NC)[None, :]
    angle = 2.0 * np.pi * ((k * n) % NP) / NP
    cosine, sine = np.cos(angle), np.sin(angle)
    full = np.zeros((2, NP, 2, NC))
    full[0, :, 0, :] = cosine
    full[0, :, 1, :] = sine
    full[1, :, 0, :] = -sine
    full[1, :, 1, :] = cosine
    return full


def halves(table, axis):
    table = table.astype(np.float32)
    high = table.astype(jnp.bfloat16)
    low = (table - high.astype(np.float32)).astype(jnp.bfloat16)
    return np.concatenate([high, low], axis)


def dft_tables():
    full = dft_matrix()
    by_freq = full.reshape(2, GZ, 2, 4, 2, NC)
    by_pair = full.reshape(2, GZ, 4, 2, 2, NC)
    by_plane = full.reshape(2, NP, 2, GZ, 4)
    by_half = full.reshape(2, NP, 2, GZ, 2, 2)
    aq = by_freq.transpose(2, 1, 0, 3, 4, 5).reshape(2 * NP, 2 * NC)
    ap = by_plane.transpose(0, 1, 2, 4, 3).reshape(2 * NP, 2 * NC)
    br = full.transpose(2, 3, 0, 1).reshape(2 * NC, 2 * NP)
    bir = full.reshape(2 * NP, 2 * NC)
    aip = by_half.transpose(3, 4, 2, 5, 0, 1).reshape(2 * NC, 2 * NP)
    aiq = by_pair.transpose(4, 5, 0, 2, 3, 1).reshape(2 * NC, 2 * NP)
    return (
        halves(aq, 1),
        halves(ap, 1),
        halves(br, 0),
        halves(bir, 0),
        halves(aip, 1),
        halves(aiq, 1),
    )


def split(x):
    high = x.astype(BF16)
    low = (x - high.astype(F32)).astype(BF16)
    return high, low


def left_dft(table, x):
    depth = x.shape[0]
    high, low = split(x)
    lhs = jnp.concatenate([table[:, :depth], table], axis=1)
    rhs = jnp.concatenate([high, low, high], axis=0)
    return jnp.dot(lhs, rhs, preferred_element_type=F32)


def right_dft(x, table):
    depth = x.shape[1]
    high, low = split(x)
    lhs = jnp.concatenate([high, low, high], axis=1)
    rhs = jnp.concatenate([table[:depth], table], axis=0)
    return jnp.dot(lhs, rhs, preferred_element_type=F32)


def sin_cos_twelfth(radius):
    turns = jnp.floor(radius * (1.0 / 12.0) + 0.5)
    half = (radius - 12.0 * turns) * (math.pi / 12.0)
    sq = half * half
    s = -2.5052108e-08
    for coef in (2.7557319e-06, -1.9841270e-04, 8.3333333e-03, -1.6666667e-01, 1.0):
        s = s * sq + coef
    s = s * half
    c = 2.0876757e-09
    for coef in (-2.7557319e-07, 2.4801587e-05, -1.3888889e-03, 4.1666667e-02, -0.5, 1.0):
        c = c * sq + coef
    return 2.0 * s * c, 1.0 - 2.0 * s * s


def kernel(
    src, contrast, spec_hbm, meas, cell, pos, aq, ap, br, bir, aip, aiq,
    out_src, out_chi,
    spec_raw, spec, y_buf, r_buf, u_buf, b_buf, inc, amp_sum, scat, res, drive,
    hot, hot_plane, part, half_in, half_sum, ring_in, chi_own, chi, extra, extra_all,
    obj, obj_all, mf, mf_in, mf_own, mf_all, placed_freq,
    spec_sem, send_sem, recv_sem, tx_send, tx_recv, ex_send, ex_recv,
    ob_send, ob_recv, ma_send, ma_recv, mb_send, mb_recv,
):
    me = lax.axis_index("gz")
    tx = lax.axis_index("tx")
    my_y = me // 8
    my_z = lax.rem(me, 8)
    my_x = tx // 2
    core = lax.rem(tx, 2)
    partner = 2 * my_x + 1 - core

    y_part = [8 * lax.rem(my_y + d, 4) for d in range(4)]
    z_part = [lax.rem(my_z + d, 8) for d in range(8)]
    peers = [y_part[i // 8] + z_part[(3 * i) % 8] for i in range(1, GZ)]
    tx_peers = [lax.rem(tx + d, TX) for d in range(1, TX)]
    x_peers = [lax.rem(my_x + d, 4) for d in range(1, 4)]
    group_peers = [lax.rem(me + 4 * d, GZ) for d in range(1, 8)]

    spec_copies = [
        pltpu.make_async_copy(
            spec_hbm.at[:, pl.ds(128 * n, 128)], spec_raw.at[n], spec_sem.at[n]
        )
        for n in range(2)
    ]
    for spec_copy in spec_copies:
        spec_copy.start()

    barrier = pltpu.get_barrier_semaphore()

    for to in peers:
        pl.semaphore_signal(barrier, inc=1, device_id={"gz": to}, device_id_type=MESH)
    for to in tx_peers:
        pl.semaphore_signal(barrier, inc=1, device_id={"tx": to}, device_id_type=MESH)

    lane = lax.broadcasted_iota(jnp.int32, (8, 128), 1)
    share = jnp.sum(meas[...] * meas[...], keepdims=True)
    row = jnp.where(lane == 0, pos[0, 0].astype(F32), 0.0)
    row = row + jnp.where(lane == 1, pos[0, 1].astype(F32), 0.0)
    row = row + jnp.where(lane == 2, share, 0.0)
    extra[...] = row
    extra_all[pl.ds(pl.multiple_of(8 * tx, 8), 8), :] = row

    def exchange_copy(sem_phase, chunk, offset, size, s_ref, d_ref, to, slot):
        phase = sem_phase // 2

        def block(g):
            return pl.ds(pl.multiple_of(offset + 32 * g, 8), size)

        return pltpu.make_async_remote_copy(
            src_ref=s_ref.at[phase, block(to), :],
            dst_ref=d_ref.at[phase, block(slot), :],
            send_sem=send_sem.at[sem_phase, chunk],
            recv_sem=recv_sem.at[sem_phase, chunk],
            device_id={"gz": to},
            device_id_type=MESH,
        )

    def start(sem_phase, chunk, offset, size, s_ref, d_ref):
        for to in peers:
            exchange_copy(sem_phase, chunk, offset, size, s_ref, d_ref, to, me).start()
        phase = sem_phase // 2
        own = pl.ds(pl.multiple_of(offset + 32 * me, 8), size)
        d_ref[phase, own, :] = s_ref[phase, own, :]

    def wait(sem_phase, chunk, offset, size, s_ref, d_ref, receive=True):
        phase = sem_phase // 2
        rows = pl.ds(0, (GZ - 1) * size)
        copy = pltpu.make_async_remote_copy(
            src_ref=s_ref.at[phase, rows, :],
            dst_ref=d_ref.at[phase, rows, :],
            send_sem=send_sem.at[sem_phase, chunk],
            recv_sem=recv_sem.at[sem_phase, chunk],
            device_id={"gz": peers[0]},
            device_id_type=MESH,
        )
        if receive:
            copy.wait_recv()
        else:
            copy.wait_send()

    back_chunks = ((0, 16), (16, 8), (24, 8), (1024, 32))

    def forward_second(field, phase, h, ph):
        x = jnp.concatenate(
            [
                jnp.concatenate(
                    [field[c, pl.ds((2 * ph + j) * NC, NC), :] for j in range(2)], axis=1
                )
                for c in range(2)
            ],
            axis=0,
        )
        y = left_dft(aq[pl.ds(h * 256, 256), :], x)
        for g in range(GZ):
            for j in range(2):
                y_buf[phase, pl.ds(h * 1024 + g * 32 + (2 * ph + j) * 8, 8), :] = y[
                    8 * g : 8 * g + 8, j * 128 : j * 128 + 128
                ]

    def middle(phase, sign, ratio):
        @pl.loop(0, 4)
        def _(kk):
            h = kk // 2

            @pl.when(lax.rem(kk, 2) == 0)
            def _():
                if phase == 0:
                    wait(0, h, h * 1024, 32, y_buf, r_buf)
                else:
                    for ph in range(2):
                        wait(2, 2 * ph + h, h * 1024 + ph * 16, 16, y_buf, r_buf)

            cols = []
            for i in range(2):
                rows = []
                for c in range(2):
                    for p in range(4):
                        first = h * 1024 + p * 8 + c * 4 + 2 * lax.rem(kk, 2) + i
                        x = r_buf[phase, pl.ds(first, GZ, stride=32), :]
                        if ratio is not None:
                            x = x + ratio * placed_freq[
                                2 * kk + i, c * NC + p * GZ : c * NC + (p + 1) * GZ, :
                            ]
                        rows.append(x)
                cols.append(jnp.concatenate(rows, axis=0))
            z = left_dft(ap[...], jnp.concatenate(cols, axis=1))
            outs = []
            for i in range(2):
                lanes = slice(i * NC, (i + 1) * NC)
                w = right_dft(jnp.concatenate([z[:NP, lanes], z[NP:, lanes]], axis=1), br[...])
                re, im = w[:, :NP], w[:, NP:]
                sr, si = spec[0, 2 * kk + i], spec[1, 2 * kk + i] * sign
                w = jnp.concatenate([re * sr - im * si, re * si + im * sr], axis=1)
                v = right_dft(w, bir[...])
                outs.append(jnp.concatenate([v[:, :NC], v[:, NC:]], axis=0))
            u = left_dft(aip[...], jnp.concatenate(outs, axis=1))
            upper = lax.bitwise_and(lax.broadcasted_iota(jnp.int32, (256, NC), 0), 4) != 0
            even, odd = u[:, :NC], u[:, NC:]
            halves_of_u = (
                jnp.where(upper, pltpu.roll(odd, 4, 0), even),
                jnp.where(upper, odd, pltpu.roll(even, 252, 0)),
            )
            for ph in range(2):
                for g in range(GZ):
                    at = pl.multiple_of(ph * 1024 + g * 32 + kk * 8, 8)
                    u_buf[phase, pl.ds(at, 8), :] = halves_of_u[ph][8 * g : 8 * g + 8]

            for at_kk, chunks in ((1, (0,)), (2, (1,)), (3, (2, 3))):

                @pl.when(kk == at_kk)
                def _():
                    for chunk in chunks:
                        start(2 * phase + 1, chunk, *back_chunks[chunk], u_buf, b_buf)

    def wait_back(phase, ph):
        for chunk in ((0, 1, 2), (3,))[ph]:
            wait(2 * phase + 1, chunk, *back_chunks[chunk], u_buf, b_buf)

    def inverse_second(phase, ph):
        cols = []
        for p2 in range(2):
            rows = []
            for c in range(2):
                for kk in range(4):
                    for i in range(2):
                        first = ph * 1024 + kk * 8 + i * 4 + c * 2 + p2
                        rows.append(b_buf[phase, pl.ds(first, GZ, stride=32), :])
            cols.append(jnp.concatenate(rows, axis=0))
        return left_dft(aiq[...], jnp.concatenate(cols, axis=1))

    for h in range(2):
        for ph in range(2):
            forward_second(src, 0, h, ph)
        if h == 0:
            pl.semaphore_wait(barrier, GZ - 1 + TX - 1)
        start(0, h, h * 1024, 32, y_buf, r_buf)

    def extra_copy(to, src_ref, dst_ref):
        return pltpu.make_async_remote_copy(
            src_ref=src_ref,
            dst_ref=dst_ref,
            send_sem=ex_send,
            recv_sem=ex_recv,
            device_id={"tx": to},
            device_id_type=MESH,
        )

    for to in tx_peers:
        extra_copy(to, extra, extra_all.at[pl.ds(pl.multiple_of(8 * tx, 8), 8), :]).start()
    extra_sum = extra_all.at[pl.ds(0, 8 * (TX - 1)), :]
    extra_wait = extra_copy(tx_peers[0], extra_sum, extra_sum)

    def geometry(n, rows_n):
        index = lax.broadcasted_iota(jnp.int32, (rows_n, 128), 0) + n * rows_n
        a = lax.shift_right_logical(index, 7) + (me * 4 + NC // 4)
        b = lax.bitwise_and(index, 127)
        c = lax.broadcasted_iota(jnp.int32, (rows_n, 128), 1)
        return a, b, c

    @pl.loop(0, 16)
    def _(n):
        a, b, c = geometry(n, 32)
        b = b - pos[0, 0]
        c = c - pos[0, 1]
        radius = jnp.sqrt((a * a + b * b + c * c).astype(F32))
        amplitude = reach_cells / (reach_cells + radius)
        sine, cosine = sin_cos_twelfth(radius)
        at = pl.ds(pl.multiple_of(n * 32, 32), 32)
        inc[0, at, :] = amplitude * cosine
        inc[1, at, :] = amplitude * sine

    local = cell[...] - me * (ROWS * 128)
    cell_row = lax.shift_right_arithmetic(local, 7)
    cell_lane = lax.bitwise_and(local, 127)

    @pl.loop(0, 16)
    def _(n):
        index = lax.broadcasted_iota(jnp.int32, (32, NREC), 0) + n * 32
        hot[pl.ds(pl.multiple_of(n * 32, 32), 32), :] = jnp.where(
            index == cell_row, 1.0, 0.0
        ).astype(BF16)

    row_index = lax.broadcasted_iota(jnp.int32, (NC, NREC), 0)
    plane = 4 * lax.bitwise_and(row_index, 31) + lax.shift_right_logical(row_index, 5)
    hot_plane[...] = jnp.where(
        plane == lax.shift_right_logical(cell[...], 14), 1.0, 0.0
    ).astype(BF16)

    for spec_copy in spec_copies:
        spec_copy.wait()

    @pl.loop(0, 8)
    def _(k):
        for c in range(2):
            for n in range(2):
                spec[c, k, :, pl.ds(n * 128, 128)] = spec_raw[
                    n, pl.ds(c * 2048 + k, NP, stride=8), :
                ] * (2.0 ** -24)

    extra_wait.wait_recv()

    @pl.loop(0, 16)
    def _(n):
        a, b, c = geometry(n, 32)
        a2 = (a * a).astype(F32)
        bf = b.astype(F32)
        cf = c.astype(F32)
        total = jnp.zeros((32, 128), F32)
        for j in range(TX):
            db = bf - extra_all[8 * j : 8 * j + 1, 0:1]
            dc = cf - extra_all[8 * j : 8 * j + 1, 1:2]
            radius = jnp.sqrt(a2 + db * db + dc * dc)
            amplitude = reach_cells / (reach_cells + radius)
            total = total + amplitude * amplitude
        amp_sum[pl.ds(pl.multiple_of(n * 32, 32), 32), :] = total

    middle(0, 1.0, None)

    def to_partner(s_ref, d_ref, which):
        return pltpu.make_async_remote_copy(
            src_ref=s_ref,
            dst_ref=d_ref,
            send_sem=tx_send.at[which],
            recv_sem=tx_recv.at[which],
            device_id={"tx": partner},
            device_id_type=MESH,
        )

    def plane_rows(p):
        return pl.ds(pl.multiple_of(p * NC, NC), NC)

    def core_copy(ph):
        return to_partner(part.at[:, plane_rows(2 * ph + 1 - core), :], half_in.at[ph], 4 * ph)

    def ring_copy(ph, to, src_ref, dst_ref):
        return pltpu.make_async_remote_copy(
            src_ref=src_ref,
            dst_ref=dst_ref,
            send_sem=tx_send.at[4 * ph + 1],
            recv_sem=tx_recv.at[4 * ph + 1],
            device_id={"tx": 2 * to + core},
            device_id_type=MESH,
        )

    def ring_wait(ph):
        three = ring_in.at[ph, pl.ds(0, 3)]
        return ring_copy(ph, x_peers[0], three, three)

    def own_rows(ph, x):
        return pl.ds(pl.multiple_of((2 * ph + core) * NC + x * 32, 32), 32)

    def chi_copy(ph, to, src_ref, dst_ref):
        return pltpu.make_async_remote_copy(
            src_ref=src_ref,
            dst_ref=dst_ref,
            send_sem=tx_send.at[4 * ph + 2],
            recv_sem=tx_recv.at[4 * ph + 2],
            device_id={"tx": 2 * to + core},
            device_id_type=MESH,
        )

    def chi_wait(ph):
        three = chi.at[:, pl.ds(0, 96), :]
        return chi_copy(ph, x_peers[0], three, three)

    def chi_send(ph, which):
        at = chi.at[:, plane_rows(2 * ph + which), :]
        return to_partner(at, at, 4 * ph + 3)

    def fields(ph):
        wait_back(0, ph)
        o = inverse_second(0, ph)
        for j in range(2):
            at = pl.ds((2 * ph + j) * NC, NC)
            for c in range(2):
                scat[c, at, :] = o[c * NC : (c + 1) * NC, j * NC : (j + 1) * NC]

        @pl.loop(0, 8)
        def _(n):
            at = pl.ds(pl.multiple_of(ph * 256 + n * 32, 32), 32)
            sr, si = src[0, at, :], src[1, at, :]
            tr = inc[0, at, :] + scat[0, at, :]
            ti = inc[1, at, :] + scat[1, at, :]
            inc[0, at, :] = tr
            inc[1, at, :] = ti
            part[0, at, :] = sr * tr + si * ti
            part[1, at, :] = si * tr - sr * ti
            part[2, at, :] = tr * tr + ti * ti

        core_copy(ph).start()

    def ring_start(ph):
        core_copy(ph).wait_recv()
        for q in range(3):
            half_sum[ph, q] = part[q, plane_rows(2 * ph + core), :] + half_in[ph, q]

        for to in x_peers:
            ring_copy(
                ph,
                to,
                half_sum.at[ph, :, pl.ds(pl.multiple_of(to * 32, 32), 32), :],
                ring_in.at[ph, my_x],
            ).start()

        ring_in[ph, my_x] = half_sum[ph, :, pl.ds(pl.multiple_of(my_x * 32, 32), 32), :]

    def contrast_start(ph):
        ring_wait(ph).wait_recv()

        sums = []
        for q in range(3):
            sums.append(
                ring_in[ph, 0, q] + ring_in[ph, 1, q] + ring_in[ph, 2, q] + ring_in[ph, 3, q]
            )
        below = sums[2] + tikhonov
        rows = own_rows(ph, my_x)
        for c in range(2):
            value = (sums[c] + tikhonov * contrast[c, rows, :]) / below
            chi_own[ph, c] = value
            chi[c, rows, :] = value

        for to in x_peers:
            chi_copy(ph, to, chi_own.at[ph], chi.at[:, rows, :]).start()

    def contrast_forward(ph):
        chi_wait(ph).wait_recv()
        chi_send(ph, core).start()

    def residual(ph, acc):
        chi_send(ph, 1 - core).wait_recv()

        def step(n, acc):
            at = pl.ds(pl.multiple_of(ph * 256 + n * 32, 32), 32)
            cr, ci = chi[0, at, :], chi[1, at, :]
            out_chi[0, at, :] = cr
            out_chi[1, at, :] = ci
            tr, ti = inc[0, at, :], inc[1, at, :]
            rr = cr * tr - ci * ti - src[0, at, :]
            ri = cr * ti + ci * tr - src[1, at, :]
            res[0, at, :] = rr
            res[1, at, :] = ri
            drive[0, at, :] = -(cr * rr + ci * ri)
            drive[1, at, :] = -(cr * ri - ci * rr)
            return acc + (cr * cr + ci * ci) * amp_sum[at, :]

        return lax.fori_loop(0, 8, step, acc)

    def drive_start(ph):
        for h in range(2):
            forward_second(drive, 1, h, ph)
            start(2, 2 * ph + h, h * 1024 + ph * 16, 16, y_buf, r_buf)

    def misfit_copy(to, src_ref, dst_ref):
        return pltpu.make_async_remote_copy(
            src_ref=src_ref,
            dst_ref=dst_ref,
            send_sem=ma_send,
            recv_sem=ma_recv,
            device_id={"gz": to},
            device_id_type=MESH,
        )

    mf_most = mf_in.at[pl.ds(0, GZ - 1)]
    misfit_wait = misfit_copy(peers[0], mf_most, mf_most)

    def misfit_back(to, src_ref, dst_ref):
        return pltpu.make_async_remote_copy(
            src_ref=src_ref,
            dst_ref=dst_ref,
            send_sem=mb_send,
            recv_sem=mb_recv,
            device_id={"gz": to},
            device_id_type=MESH,
        )

    mf_seven = mf_all.at[pl.ds(0, 7)]
    back_wait = misfit_back(group_peers[0], mf_seven, mf_seven)

    lane_index = lax.broadcasted_iota(jnp.int32, (NC, NREC), 0)

    def misfit_start():
        pieces = [split(scat[c]) for c in range(2)]
        columns = jnp.concatenate(
            [pieces[0][0], pieces[1][0], pieces[0][1], pieces[1][1]], axis=1
        )
        found = lax.dot_general(
            columns, hot[...], (((0,), (0,)), ((), ())), preferred_element_type=F32
        )
        on_lane = lane_index == cell_lane
        inside = (cell_row >= 0) & (cell_row < ROWS)
        misfit = []
        for c in range(2):
            both = found[c * NC : (c + 1) * NC] + found[(2 + c) * NC : (3 + c) * NC]
            sampled = jnp.sum(jnp.where(on_lane, both, 0.0), axis=0, keepdims=True)
            misfit.append(jnp.where(inside, meas[c : c + 1, :] - sampled, 0.0))
        rest = jnp.zeros((6, 128), F32)
        for i in range(8):
            at = slice(i * 128, (i + 1) * 128)
            mf[i] = jnp.concatenate([misfit[0][:, at], misfit[1][:, at], rest], axis=0)
        mf_in[me] = mf[me // 4]

        for to in peers:
            misfit_copy(to, mf.at[to // 4], mf_in.at[me]).start()

    def misfit_forward():
        misfit_wait.wait_recv()
        total = mf_in[0]
        for g in range(1, GZ):
            total = total + mf_in[g]
        mf_own[...] = total
        mf_all[me // 4] = total

        for to in group_peers:
            misfit_back(to, mf_own, mf_all.at[me // 4]).start()

    def placed_spectrum():
        back_wait.wait_recv()
        mr = jnp.concatenate([mf_all[i, 0:1, :] for i in range(8)], axis=1)
        mi = jnp.concatenate([mf_all[i, 1:2, :] for i in range(8)], axis=1)
        second = lax.bitwise_and(lax.shift_right_logical(cell[...], 7), 127)

        @pl.loop(0, 8)
        def _(k):
            turn = lax.bitwise_and((8 * me + k) * second, 255)
            sine, cosine = sin_cos_twelfth(turn.astype(F32) * (12.0 / 256.0))
            on_lane = lane_index == cell_lane
            v = (
                split(jnp.where(on_lane, mr * cosine + mi * sine, 0.0)),
                split(jnp.where(on_lane, mi * cosine - mr * sine, 0.0)),
            )
            values = jnp.concatenate([v[0][0], v[1][0], v[0][1], v[1][1]], axis=0)
            found = lax.dot_general(
                hot_plane[...], values, (((1,), (1,)), ((), ())), preferred_element_type=F32
            )
            for c in range(2):
                placed_freq[k, pl.ds(c * NC, NC), :] = (
                    found[:, c * NC : (c + 1) * NC] + found[:, (2 + c) * NC : (3 + c) * NC]
                )

    def obj_copy(to, src_ref, dst_ref):
        return pltpu.make_async_remote_copy(
            src_ref=src_ref,
            dst_ref=dst_ref,
            send_sem=ob_send,
            recv_sem=ob_recv,
            device_id={"gz": to},
            device_id_type=MESH,
        )

    obj_most = obj_all.at[pl.ds(0, 8 * (GZ - 1)), :]
    obj_wait = obj_copy(peers[0], obj_most, obj_most)

    def object_start(acc):
        own = acc[0:8] + acc[8:16] + acc[16:24] + acc[24:32]
        obj[...] = own
        mine = pl.ds(pl.multiple_of(8 * me, 8), 8)
        obj_all[mine, :] = own
        for to in peers:
            obj_copy(to, obj, obj_all.at[mine, :]).start()

    def object_ratio():
        obj_wait.wait_recv()
        object_norm = jnp.sum(obj_all[...], keepdims=True)
        data_norm = jnp.zeros((1, 1), F32)
        for j in range(TX):
            data_norm = data_norm + extra_all[8 * j : 8 * j + 1, 2:3]
        return object_norm / (data_norm + norm_floor)

    fields(0)
    ring_start(0)
    contrast_start(0)
    contrast_forward(0)
    fields(1)
    acc = residual(0, jnp.zeros((32, 128), F32))
    drive_start(0)
    ring_start(1)
    misfit_start()
    contrast_start(1)
    misfit_forward()
    contrast_forward(1)
    acc = residual(1, acc)
    object_start(acc)
    drive_start(1)
    placed_spectrum()
    middle(1, -1.0, object_ratio())
    for ph in range(2):
        wait_back(1, ph)
        o = inverse_second(1, ph)
        for j in range(2):
            at = pl.ds((2 * ph + j) * NC, NC)
            for c in range(2):
                back = o[c * NC : (c + 1) * NC, j * NC : (j + 1) * NC]
                out_src[c, at, :] = src[c, at, :] + step_length * (res[c, at, :] + back)

    for h in range(2):
        wait(0, h, h * 1024, 32, y_buf, r_buf, False)
        for ph in range(2):
            wait(2, 2 * ph + h, h * 1024 + ph * 16, 16, y_buf, r_buf, False)
    for phase in range(2):
        for chunk in range(4):
            wait(2 * phase + 1, chunk, *back_chunks[chunk], u_buf, b_buf, False)

    obj_wait.wait_send()
    misfit_wait.wait_send()
    back_wait.wait_send()
    extra_wait.wait_send()
    for ph in range(2):
        ring_wait(ph).wait_send()
        chi_wait(ph).wait_send()
        core_copy(ph).wait_send()
        chi_send(ph, core).wait_send()


def shards(sources, contrast, spectrum, measured, receivers, positions):
    vmem = pl.BlockSpec(memory_space=pltpu.VMEM)
    tables = [jnp.asarray(table) for table in dft_tables()]
    field = jax.ShapeDtypeStruct((2, ROWS, 128), F32)

    def buf(*shape):
        return pltpu.VMEM(shape, F32)

    dma = pltpu.SemaphoreType.DMA
    new, chi = pl.pallas_call(
        kernel,
        out_shape=(field, field),
        in_specs=[
            vmem,
            vmem,
            pl.BlockSpec(memory_space=pl.ANY),
            vmem,
            vmem,
            pl.BlockSpec(memory_space=pltpu.SMEM),
        ]
        + [vmem] * 6,
        out_specs=(vmem, vmem),
        scratch_shapes=[
            buf(2, 4096, 128),
            buf(2, 8, NP, NP),
            buf(2, 2048, 128),
            buf(2, 2048, 128),
            buf(2, 2048, 128),
            buf(2, 2048, 128),
            buf(2, ROWS, 128),
            buf(ROWS, 128),
            buf(2, ROWS, 128),
            buf(2, ROWS, 128),
            buf(2, ROWS, 128),
            pltpu.VMEM((ROWS, NREC), BF16),
            pltpu.VMEM((NC, NREC), BF16),
            buf(3, ROWS, 128),
            buf(2, 3, NC, 128),
            buf(2, 3, NC, 128),
            buf(2, 4, 3, 32, 128),
            buf(2, 2, 32, 128),
            buf(2, ROWS, 128),
            buf(8, 128),
            buf(64, 128),
            buf(8, 128),
            buf(256, 128),
            buf(8, 8, 128),
            buf(GZ, 8, 128),
            buf(8, 128),
            buf(8, 8, 128),
            buf(8, 2 * NC, 128),
            dma((2,)),
            dma((4, 4)),
            dma((4, 4)),
            dma((8,)),
            dma((8,)),
        ]
        + [dma] * 8,
        compiler_params=pltpu.CompilerParams(
            collective_id=0, has_side_effects=True, vmem_limit_bytes=60 * 1024 * 1024
        ),
    )(
        sources.reshape(2, ROWS, 128),
        contrast.reshape(2, ROWS, 128),
        spectrum.reshape(4096, NP),
        measured.reshape(2, NREC),
        receivers,
        positions,
        *tables,
    )
    return new.reshape(sources.shape), chi.reshape(contrast.shape)


def solution(mesh):
    in_specs = (
        P("tx", None, "gz", None, None),
        P(None, "gz", None, None),
        P(None, None, "gz", None),
        P("tx", None, None),
        P("tx", None),
        P("tx", None),
    )
    out_specs = (P("tx", None, "gz", None, None), P(None, "gz", None, None))
    return jax.shard_map(shards, mesh=mesh, in_specs=in_specs, out_specs=out_specs, check_vma=False)
```

```python
import math

import jax
import jax.numpy as jnp
import numpy as np
from jax import lax
from jax.experimental import pallas as pl
from jax.experimental.pallas import tpu as pltpu
from jax.sharding import PartitionSpec as P

MESH = pl.DeviceIdType.MESH
F32 = jnp.float32
BF16 = jnp.bfloat16

reach_cells = 16.0
tikhonov = 1.0
step_length = 0.5
norm_floor = 1e-06

NC = 128
NP = 256
GZ = 32
TX = 8
NREC = 1024
ROWS = 512


def dft_matrix():
    k = np.arange(NP)[:, None]
    n = np.arange(NC)[None, :]
    angle = 2.0 * np.pi * ((k * n) % NP) / NP
    cosine, sine = np.cos(angle), np.sin(angle)
    full = np.zeros((2, NP, 2, NC))
    full[0, :, 0, :] = cosine
    full[0, :, 1, :] = sine
    full[1, :, 0, :] = -sine
    full[1, :, 1, :] = cosine
    return full


def halves(table, axis):
    table = table.astype(np.float32)
    high = table.astype(jnp.bfloat16)
    low = (table - high.astype(np.float32)).astype(jnp.bfloat16)
    return np.concatenate([high, low], axis)


def first_table():
    by_freq = dft_matrix().reshape(2, GZ, 2, 4, 2, NC)
    return halves(by_freq.transpose(2, 1, 0, 3, 4, 5).reshape(2 * NP, 2 * NC), 1)


def bits(x, shift, count):
    return lax.bitwise_and(lax.shift_right_logical(x, shift), (1 << count) - 1)


def freq_index(x):
    return bits(x, 0, 8), bits(x, 8, 1)


def freq_pair_index(x):
    return 8 * bits(x, 0, 5) + 2 * bits(x, 6, 2) + bits(x, 5, 1), bits(x, 8, 1)


def cell_index(x):
    return bits(x, 0, 7), bits(x, 7, 1)


def plane_index(x):
    return 4 * bits(x, 0, 5) + bits(x, 5, 2), bits(x, 7, 1)


def plane_half_index(x):
    return 4 * bits(x, 3, 5) + 2 * bits(x, 2, 1) + bits(x, 0, 1), bits(x, 1, 1)


def fill_table(ref, axis, row_of, column_of, rows_are_freq):
    height, width = ref.shape
    height, width = (height // 2, width) if axis == 0 else (height, width // 2)

    @pl.loop(0, height // 32)
    def _(n):
        a, part_a = row_of(lax.broadcasted_iota(jnp.int32, (32, width), 0) + n * 32)
        b, part_b = column_of(lax.broadcasted_iota(jnp.int32, (32, width), 1))
        quarter = (part_a - part_b) if rows_are_freq else (part_b - part_a)
        turn = lax.bitwise_and(a * b + 64 * quarter, 255)
        table = sin_cos_twelfth(turn.astype(F32) * (12.0 / 256.0))[1]
        high, low = split(table)
        rows = pl.ds(pl.multiple_of(n * 32, 32), 32)
        if axis == 0:
            ref[rows, :] = high
            ref[pl.ds(pl.multiple_of(height + n * 32, 32), 32), :] = low
        else:
            ref[rows, pl.ds(0, width)] = high
            ref[rows, pl.ds(width, width)] = low


def split(x):
    high = x.astype(BF16)
    low = (x - high.astype(F32)).astype(BF16)
    return high, low


def left_dft(table, x):
    depth = x.shape[0]
    high, low = split(x)
    lhs = jnp.concatenate([table[:, :depth], table], axis=1)
    rhs = jnp.concatenate([high, low, high], axis=0)
    return jnp.dot(lhs, rhs, preferred_element_type=F32)


def right_dft(x, table):
    depth = x.shape[1]
    high, low = split(x)
    lhs = jnp.concatenate([high, low, high], axis=1)
    rhs = jnp.concatenate([table[:depth], table], axis=0)
    return jnp.dot(lhs, rhs, preferred_element_type=F32)


def sin_cos_twelfth(radius):
    turns = jnp.floor(radius * (1.0 / 12.0) + 0.5)
    half = (radius - 12.0 * turns) * (math.pi / 12.0)
    sq = half * half
    s = -2.5052108e-08
    for coef in (2.7557319e-06, -1.9841270e-04, 8.3333333e-03, -1.6666667e-01, 1.0):
        s = s * sq + coef
    s = s * half
    c = 2.0876757e-09
    for coef in (-2.7557319e-07, 2.4801587e-05, -1.3888889e-03, 4.1666667e-02, -0.5, 1.0):
        c = c * sq + coef
    return 2.0 * s * c, 1.0 - 2.0 * s * s


def kernel(
    src_hbm, contrast_hbm, spec_hbm, meas_hbm, cell_hbm, pos,
    aq_hbm,
    new_hbm, chi_hbm,
    src, contrast, meas, cell, aq, ap, br, bir, aip, aiq, out_src,
    spec_raw, spec, y_buf, r_buf, u_buf, b_buf, inc, amp_sum, scat, res, drive,
    hot, hot_plane, part, half_in, half_sum, ring_in, chi_own, chi, extra, extra_all,
    obj, obj_all, mf, mf_in, mf_own, mf_all, placed_freq, found_first,
    load_sem, store_sem, send_sem, recv_sem, tx_send, tx_recv, ex_send, ex_recv,
    ob_send, ob_recv, ma_send, ma_recv, mb_send, mb_recv,
):
    me = lax.axis_index("gz")
    tx = lax.axis_index("tx")
    my_y = me // 8
    my_z = lax.rem(me, 8)
    my_x = tx // 2
    core = lax.rem(tx, 2)
    partner = 2 * my_x + 1 - core

    y_part = [8 * lax.rem(my_y + d, 4) for d in range(4)]
    z_part = [lax.rem(my_z + d, 8) for d in range(8)]
    peers = [y_part[i // 8] + z_part[(3 * i) % 8] for i in range(1, GZ)]
    tx_peers = [lax.rem(tx + d, TX) for d in range(1, TX)]
    x_peers = [lax.rem(my_x + d, 4) for d in range(1, 4)]
    group_peers = [lax.rem(me + 4 * d, GZ) for d in range(1, 8)]

    loads = {}
    for n, (name, hbm, vmem) in enumerate(
        (
            ("aq", aq_hbm, aq),
            ("src", src_hbm, src),
            ("meas", meas_hbm, meas),
            ("cell", cell_hbm, cell),
            ("spec0", spec_hbm.at[:, pl.ds(0, 128)], spec_raw.at[0]),
            ("spec1", spec_hbm.at[:, pl.ds(128, 128)], spec_raw.at[1]),
            ("contrast", contrast_hbm, contrast),
        )
    ):
        loads[name] = pltpu.make_async_copy(hbm, vmem, load_sem.at[n])

    def loaded(*names):
        for name in names:
            loads[name].wait()

    barrier = pltpu.get_barrier_semaphore()

    for to in peers:
        pl.semaphore_signal(barrier, inc=1, device_id={"gz": to}, device_id_type=MESH)
    for to in tx_peers:
        pl.semaphore_signal(barrier, inc=1, device_id={"tx": to}, device_id_type=MESH)

    for load in loads.values():
        load.start()
    loaded("meas")

    lane = lax.broadcasted_iota(jnp.int32, (8, 128), 1)
    share = jnp.sum(meas[...] * meas[...], keepdims=True)
    row = jnp.where(lane == 0, pos[0, 0].astype(F32), 0.0)
    row = row + jnp.where(lane == 1, pos[0, 1].astype(F32), 0.0)
    row = row + jnp.where(lane == 2, share, 0.0)
    extra[...] = row
    extra_all[pl.ds(pl.multiple_of(8 * tx, 8), 8), :] = row

    def exchange_copy(sem_phase, chunk, offset, size, s_ref, d_ref, to, slot):
        phase = sem_phase // 2

        def block(g):
            return pl.ds(pl.multiple_of(offset + 32 * g, 8), size)

        return pltpu.make_async_remote_copy(
            src_ref=s_ref.at[phase, block(to), :],
            dst_ref=d_ref.at[phase, block(slot), :],
            send_sem=send_sem.at[sem_phase, chunk],
            recv_sem=recv_sem.at[sem_phase, chunk],
            device_id={"gz": to},
            device_id_type=MESH,
        )

    def start(sem_phase, chunk, offset, size, s_ref, d_ref):
        for to in peers:
            exchange_copy(sem_phase, chunk, offset, size, s_ref, d_ref, to, me).start()
        phase = sem_phase // 2
        own = pl.ds(pl.multiple_of(offset + 32 * me, 8), size)
        d_ref[phase, own, :] = s_ref[phase, own, :]

    def wait(sem_phase, chunk, offset, size, s_ref, d_ref, receive=True):
        phase = sem_phase // 2
        rows = pl.ds(0, (GZ - 1) * size)
        copy = pltpu.make_async_remote_copy(
            src_ref=s_ref.at[phase, rows, :],
            dst_ref=d_ref.at[phase, rows, :],
            send_sem=send_sem.at[sem_phase, chunk],
            recv_sem=recv_sem.at[sem_phase, chunk],
            device_id={"gz": peers[0]},
            device_id_type=MESH,
        )
        if receive:
            copy.wait_recv()
        else:
            copy.wait_send()

    back_chunks = ((0, 16), (16, 8), (24, 8), (1024, 32))

    def forward_second(field, phase, h, ph):
        x = jnp.concatenate(
            [
                jnp.concatenate(
                    [field[c, pl.ds((2 * ph + j) * NC, NC), :] for j in range(2)], axis=1
                )
                for c in range(2)
            ],
            axis=0,
        )
        y = left_dft(aq[pl.ds(h * 256, 256), :], x)
        for g in range(GZ):
            for j in range(2):
                y_buf[phase, pl.ds(h * 1024 + g * 32 + (2 * ph + j) * 8, 8), :] = y[
                    8 * g : 8 * g + 8, j * 128 : j * 128 + 128
                ]

    def middle(phase, sign, ratio):
        @pl.loop(0, 4)
        def _(kk):
            h = kk // 2

            @pl.when(lax.rem(kk, 2) == 0)
            def _():
                if phase == 0:
                    wait(0, h, h * 1024, 32, y_buf, r_buf)
                else:
                    for ph in range(2):
                        wait(2, 2 * ph + h, h * 1024 + ph * 16, 16, y_buf, r_buf)

            cols = []
            for i in range(2):
                rows = []
                for c in range(2):
                    for p in range(4):
                        first = h * 1024 + p * 8 + c * 4 + 2 * lax.rem(kk, 2) + i
                        x = r_buf[phase, pl.ds(first, GZ, stride=32), :]
                        if ratio is not None:
                            x = x + ratio * placed_freq[
                                2 * kk + i, c * NC + p * GZ : c * NC + (p + 1) * GZ, :
                            ]
                        rows.append(x)
                cols.append(jnp.concatenate(rows, axis=0))
            z = left_dft(ap[...], jnp.concatenate(cols, axis=1))
            outs = []
            for i in range(2):
                lanes = slice(i * NC, (i + 1) * NC)
                w = right_dft(jnp.concatenate([z[:NP, lanes], z[NP:, lanes]], axis=1), br[...])
                re, im = w[:, :NP], w[:, NP:]
                sr, si = spec[0, 2 * kk + i], spec[1, 2 * kk + i] * sign
                w = jnp.concatenate([re * sr - im * si, re * si + im * sr], axis=1)
                v = right_dft(w, bir[...])
                outs.append(jnp.concatenate([v[:, :NC], v[:, NC:]], axis=0))
            u = left_dft(aip[...], jnp.concatenate(outs, axis=1))
            upper = lax.bitwise_and(lax.broadcasted_iota(jnp.int32, (256, NC), 0), 4) != 0
            even, odd = u[:, :NC], u[:, NC:]
            halves_of_u = (
                jnp.where(upper, pltpu.roll(odd, 4, 0), even),
                jnp.where(upper, odd, pltpu.roll(even, 252, 0)),
            )
            for ph in range(2):
                for g in range(GZ):
                    at = pl.multiple_of(ph * 1024 + g * 32 + kk * 8, 8)
                    u_buf[phase, pl.ds(at, 8), :] = halves_of_u[ph][8 * g : 8 * g + 8]

            for at_kk, chunks in ((1, (0,)), (2, (1,)), (3, (2, 3))):

                @pl.when(kk == at_kk)
                def _():
                    for chunk in chunks:
                        start(2 * phase + 1, chunk, *back_chunks[chunk], u_buf, b_buf)

    def wait_back(phase, ph):
        for chunk in ((0, 1, 2), (3,))[ph]:
            wait(2 * phase + 1, chunk, *back_chunks[chunk], u_buf, b_buf)

    def inverse_second(phase, ph):
        cols = []
        for p2 in range(2):
            rows = []
            for c in range(2):
                for kk in range(4):
                    for i in range(2):
                        first = ph * 1024 + kk * 8 + i * 4 + c * 2 + p2
                        rows.append(b_buf[phase, pl.ds(first, GZ, stride=32), :])
            cols.append(jnp.concatenate(rows, axis=0))
        return left_dft(aiq[...], jnp.concatenate(cols, axis=1))

    loaded("aq", "src")
    for h in range(2):
        for ph in range(2):
            forward_second(src, 0, h, ph)
        if h == 0:
            pl.semaphore_wait(barrier, GZ - 1 + TX - 1)
        start(0, h, h * 1024, 32, y_buf, r_buf)

    def extra_copy(to, src_ref, dst_ref):
        return pltpu.make_async_remote_copy(
            src_ref=src_ref,
            dst_ref=dst_ref,
            send_sem=ex_send,
            recv_sem=ex_recv,
            device_id={"tx": to},
            device_id_type=MESH,
        )

    for to in tx_peers:
        extra_copy(to, extra, extra_all.at[pl.ds(pl.multiple_of(8 * tx, 8), 8), :]).start()
    extra_sum = extra_all.at[pl.ds(0, 8 * (TX - 1)), :]
    extra_wait = extra_copy(tx_peers[0], extra_sum, extra_sum)

    def geometry(n, rows_n):
        index = lax.broadcasted_iota(jnp.int32, (rows_n, 128), 0) + n * rows_n
        a = lax.shift_right_logical(index, 7) + (me * 4 + NC // 4)
        b = lax.bitwise_and(index, 127)
        c = lax.broadcasted_iota(jnp.int32, (rows_n, 128), 1)
        return a, b, c

    @pl.loop(0, 16)
    def _(n):
        a, b, c = geometry(n, 32)
        b = b - pos[0, 0]
        c = c - pos[0, 1]
        radius = jnp.sqrt((a * a + b * b + c * c).astype(F32))
        amplitude = reach_cells / (reach_cells + radius)
        sine, cosine = sin_cos_twelfth(radius)
        at = pl.ds(pl.multiple_of(n * 32, 32), 32)
        inc[0, at, :] = amplitude * cosine
        inc[1, at, :] = amplitude * sine

    loaded("cell")
    local = cell[...] - me * (ROWS * 128)
    cell_row = lax.shift_right_arithmetic(local, 7)
    cell_lane = lax.bitwise_and(local, 127)

    @pl.loop(0, 16)
    def _(n):
        index = lax.broadcasted_iota(jnp.int32, (32, NREC), 0) + n * 32
        hot[pl.ds(pl.multiple_of(n * 32, 32), 32), :] = jnp.where(
            index == cell_row, 1.0, 0.0
        ).astype(BF16)

    row_index = lax.broadcasted_iota(jnp.int32, (NC, NREC), 0)
    plane = 4 * lax.bitwise_and(row_index, 31) + lax.shift_right_logical(row_index, 5)
    hot_plane[...] = jnp.where(
        plane == lax.shift_right_logical(cell[...], 14), 1.0, 0.0
    ).astype(BF16)

    loaded("spec0", "spec1")

    @pl.loop(0, 8)
    def _(k):
        for c in range(2):
            for n in range(2):
                spec[c, k, :, pl.ds(n * 128, 128)] = spec_raw[
                    n, pl.ds(c * 2048 + k, NP, stride=8), :
                ] * (2.0 ** -24)

    fill_table(ap, 1, freq_index, plane_index, True)
    fill_table(br, 0, cell_index, freq_index, False)
    fill_table(bir, 0, freq_index, cell_index, True)
    fill_table(aip, 1, plane_half_index, freq_index, False)

    def incident_power():
        extra_wait.wait_recv()

        @pl.loop(0, 16)
        def _(n):
            a, b, c = geometry(n, 32)
            a2 = (a * a).astype(F32)
            bf = b.astype(F32)
            cf = c.astype(F32)
            total = jnp.zeros((32, 128), F32)
            for j in range(TX):
                db = bf - extra_all[8 * j : 8 * j + 1, 0:1]
                dc = cf - extra_all[8 * j : 8 * j + 1, 1:2]
                radius = jnp.sqrt(a2 + db * db + dc * dc)
                amplitude = reach_cells / (reach_cells + radius)
                total = total + amplitude * amplitude
            amp_sum[pl.ds(pl.multiple_of(n * 32, 32), 32), :] = total

    middle(0, 1.0, None)
    loaded("contrast")
    fill_table(aiq, 1, cell_index, freq_pair_index, False)
    incident_power()

    def to_partner(s_ref, d_ref, which):
        return pltpu.make_async_remote_copy(
            src_ref=s_ref,
            dst_ref=d_ref,
            send_sem=tx_send.at[which],
            recv_sem=tx_recv.at[which],
            device_id={"tx": partner},
            device_id_type=MESH,
        )

    def plane_rows(p):
        return pl.ds(pl.multiple_of(p * NC, NC), NC)

    def core_copy(ph):
        return to_partner(part.at[:, plane_rows(2 * ph + 1 - core), :], half_in.at[ph], 4 * ph)

    def ring_copy(ph, to, src_ref, dst_ref):
        return pltpu.make_async_remote_copy(
            src_ref=src_ref,
            dst_ref=dst_ref,
            send_sem=tx_send.at[4 * ph + 1],
            recv_sem=tx_recv.at[4 * ph + 1],
            device_id={"tx": 2 * to + core},
            device_id_type=MESH,
        )

    def ring_wait(ph):
        three = ring_in.at[ph, pl.ds(0, 3)]
        return ring_copy(ph, x_peers[0], three, three)

    def own_rows(ph, x):
        return pl.ds(pl.multiple_of((2 * ph + core) * NC + x * 32, 32), 32)

    def chi_copy(ph, to, src_ref, dst_ref):
        return pltpu.make_async_remote_copy(
            src_ref=src_ref,
            dst_ref=dst_ref,
            send_sem=tx_send.at[4 * ph + 2],
            recv_sem=tx_recv.at[4 * ph + 2],
            device_id={"tx": 2 * to + core},
            device_id_type=MESH,
        )

    def chi_wait(ph):
        three = chi.at[:, pl.ds(0, 96), :]
        return chi_copy(ph, x_peers[0], three, three)

    def chi_send(ph, which):
        at = chi.at[:, plane_rows(2 * ph + which), :]
        return to_partner(at, at, 4 * ph + 3)

    def fields(ph):
        wait_back(0, ph)
        o = inverse_second(0, ph)
        for j in range(2):
            at = pl.ds((2 * ph + j) * NC, NC)
            for c in range(2):
                scat[c, at, :] = o[c * NC : (c + 1) * NC, j * NC : (j + 1) * NC]

        @pl.loop(0, 8)
        def _(n):
            at = pl.ds(pl.multiple_of(ph * 256 + n * 32, 32), 32)
            sr, si = src[0, at, :], src[1, at, :]
            tr = inc[0, at, :] + scat[0, at, :]
            ti = inc[1, at, :] + scat[1, at, :]
            inc[0, at, :] = tr
            inc[1, at, :] = ti
            part[0, at, :] = sr * tr + si * ti
            part[1, at, :] = si * tr - sr * ti
            part[2, at, :] = tr * tr + ti * ti

        core_copy(ph).start()

    def ring_start(ph):
        core_copy(ph).wait_recv()
        for q in range(3):
            half_sum[ph, q] = part[q, plane_rows(2 * ph + core), :] + half_in[ph, q]

        for to in x_peers:
            ring_copy(
                ph,
                to,
                half_sum.at[ph, :, pl.ds(pl.multiple_of(to * 32, 32), 32), :],
                ring_in.at[ph, my_x],
            ).start()

        ring_in[ph, my_x] = half_sum[ph, :, pl.ds(pl.multiple_of(my_x * 32, 32), 32), :]

    def contrast_start(ph):
        ring_wait(ph).wait_recv()

        sums = []
        for q in range(3):
            sums.append(
                ring_in[ph, 0, q] + ring_in[ph, 1, q] + ring_in[ph, 2, q] + ring_in[ph, 3, q]
            )
        below = sums[2] + tikhonov
        rows = own_rows(ph, my_x)
        for c in range(2):
            value = (sums[c] + tikhonov * contrast[c, rows, :]) / below
            chi_own[ph, c] = value
            chi[c, rows, :] = value

        for to in x_peers:
            chi_copy(ph, to, chi_own.at[ph], chi.at[:, rows, :]).start()

    def contrast_forward(ph):
        chi_wait(ph).wait_recv()
        chi_send(ph, core).start()

    def residual(ph, acc):
        chi_send(ph, 1 - core).wait_recv()

        def step(n, acc):
            at = pl.ds(pl.multiple_of(ph * 256 + n * 32, 32), 32)
            cr, ci = chi[0, at, :], chi[1, at, :]
            tr, ti = inc[0, at, :], inc[1, at, :]
            rr = cr * tr - ci * ti - src[0, at, :]
            ri = cr * ti + ci * tr - src[1, at, :]
            res[0, at, :] = rr
            res[1, at, :] = ri
            drive[0, at, :] = -(cr * rr + ci * ri)
            drive[1, at, :] = -(cr * ri - ci * rr)
            return acc + (cr * cr + ci * ci) * amp_sum[at, :]

        return lax.fori_loop(0, 8, step, acc)

    def drive_start(ph, h):
        forward_second(drive, 1, h, ph)
        start(2, 2 * ph + h, h * 1024 + ph * 16, 16, y_buf, r_buf)

    def misfit_copy(to, src_ref, dst_ref):
        return pltpu.make_async_remote_copy(
            src_ref=src_ref,
            dst_ref=dst_ref,
            send_sem=ma_send,
            recv_sem=ma_recv,
            device_id={"gz": to},
            device_id_type=MESH,
        )

    mf_most = mf_in.at[pl.ds(0, GZ - 1)]
    misfit_wait = misfit_copy(peers[0], mf_most, mf_most)

    def misfit_back(to, src_ref, dst_ref):
        return pltpu.make_async_remote_copy(
            src_ref=src_ref,
            dst_ref=dst_ref,
            send_sem=mb_send,
            recv_sem=mb_recv,
            device_id={"gz": to},
            device_id_type=MESH,
        )

    mf_seven = mf_all.at[pl.ds(0, 7)]
    back_wait = misfit_back(group_peers[0], mf_seven, mf_seven)

    lane_index = lax.broadcasted_iota(jnp.int32, (NC, NREC), 0)

    def found_at(ph):
        rows = pl.ds(ph * 256, 256)
        pieces = [split(scat[c, rows, :]) for c in range(2)]
        columns = jnp.concatenate(
            [pieces[0][0], pieces[1][0], pieces[0][1], pieces[1][1]], axis=1
        )
        return lax.dot_general(
            columns, hot[rows, :], (((0,), (0,)), ((), ())), preferred_element_type=F32
        )

    def misfit_start():
        found = found_first[...] + found_at(1)
        on_lane = lane_index == cell_lane
        inside = (cell_row >= 0) & (cell_row < ROWS)
        misfit = []
        for c in range(2):
            both = found[c * NC : (c + 1) * NC] + found[(2 + c) * NC : (3 + c) * NC]
            sampled = jnp.sum(jnp.where(on_lane, both, 0.0), axis=0, keepdims=True)
            misfit.append(jnp.where(inside, meas[c : c + 1, :] - sampled, 0.0))
        rest = jnp.zeros((6, 128), F32)
        for i in range(8):
            at = slice(i * 128, (i + 1) * 128)
            mf[i] = jnp.concatenate([misfit[0][:, at], misfit[1][:, at], rest], axis=0)
        mf_in[me] = mf[me // 4]

        for to in peers:
            misfit_copy(to, mf.at[to // 4], mf_in.at[me]).start()

    def misfit_forward():
        misfit_wait.wait_recv()
        total = mf_in[0]
        for g in range(1, GZ):
            total = total + mf_in[g]
        mf_own[...] = total
        mf_all[me // 4] = total

        for to in group_peers:
            misfit_back(to, mf_own, mf_all.at[me // 4]).start()

    def placed_spectrum():
        back_wait.wait_recv()
        mr = jnp.concatenate([mf_all[i, 0:1, :] for i in range(8)], axis=1)
        mi = jnp.concatenate([mf_all[i, 1:2, :] for i in range(8)], axis=1)
        second = lax.bitwise_and(lax.shift_right_logical(cell[...], 7), 127)

        @pl.loop(0, 8)
        def _(k):
            turn = lax.bitwise_and((8 * me + k) * second, 255)
            sine, cosine = sin_cos_twelfth(turn.astype(F32) * (12.0 / 256.0))
            on_lane = lane_index == cell_lane
            v = (
                split(jnp.where(on_lane, mr * cosine + mi * sine, 0.0)),
                split(jnp.where(on_lane, mi * cosine - mr * sine, 0.0)),
            )
            values = jnp.concatenate([v[0][0], v[1][0], v[0][1], v[1][1]], axis=0)
            found = lax.dot_general(
                hot_plane[...], values, (((1,), (1,)), ((), ())), preferred_element_type=F32
            )
            for c in range(2):
                placed_freq[k, pl.ds(c * NC, NC), :] = (
                    found[:, c * NC : (c + 1) * NC] + found[:, (2 + c) * NC : (3 + c) * NC]
                )

    def obj_copy(to, src_ref, dst_ref):
        return pltpu.make_async_remote_copy(
            src_ref=src_ref,
            dst_ref=dst_ref,
            send_sem=ob_send,
            recv_sem=ob_recv,
            device_id={"gz": to},
            device_id_type=MESH,
        )

    obj_most = obj_all.at[pl.ds(0, 8 * (GZ - 1)), :]
    obj_wait = obj_copy(peers[0], obj_most, obj_most)

    def object_start(acc):
        own = acc[0:8] + acc[8:16] + acc[16:24] + acc[24:32]
        obj[...] = own
        mine = pl.ds(pl.multiple_of(8 * me, 8), 8)
        obj_all[mine, :] = own
        for to in peers:
            obj_copy(to, obj, obj_all.at[mine, :]).start()

    def object_ratio():
        obj_wait.wait_recv()
        object_norm = jnp.sum(obj_all[...], keepdims=True)
        data_norm = jnp.zeros((1, 1), F32)
        for j in range(TX):
            data_norm = data_norm + extra_all[8 * j : 8 * j + 1, 2:3]
        return object_norm / (data_norm + norm_floor)

    fields(0)
    found_first[...] = found_at(0)
    ring_start(0)
    contrast_start(0)
    contrast_forward(0)
    fields(1)
    misfit_start()
    acc = residual(0, jnp.zeros((32, 128), F32))
    drive_start(0, 0)
    ring_start(1)
    drive_start(0, 1)
    contrast_start(1)
    misfit_forward()
    contrast_forward(1)
    acc = residual(1, acc)
    object_start(acc)
    drive_start(1, 0)
    drive_start(1, 1)
    placed_spectrum()
    chi_store = pltpu.make_async_copy(chi, chi_hbm, store_sem.at[2])
    chi_store.start()
    middle(1, -1.0, object_ratio())
    stores = []
    for ph in range(2):
        wait_back(1, ph)
        o = inverse_second(1, ph)
        for j in range(2):
            at = pl.ds((2 * ph + j) * NC, NC)
            for c in range(2):
                back = o[c * NC : (c + 1) * NC, j * NC : (j + 1) * NC]
                out_src[c, at, :] = src[c, at, :] + step_length * (res[c, at, :] + back)
        at = pl.ds(ph * 256, 256)
        stores.append(
            pltpu.make_async_copy(out_src.at[:, at, :], new_hbm.at[:, at, :], store_sem.at[ph])
        )
        stores[-1].start()

    for h in range(2):
        wait(0, h, h * 1024, 32, y_buf, r_buf, False)
        for ph in range(2):
            wait(2, 2 * ph + h, h * 1024 + ph * 16, 16, y_buf, r_buf, False)
    for phase in range(2):
        for chunk in range(4):
            wait(2 * phase + 1, chunk, *back_chunks[chunk], u_buf, b_buf, False)

    chi_store.wait()
    for store in stores:
        store.wait()
    obj_wait.wait_send()
    misfit_wait.wait_send()
    back_wait.wait_send()
    extra_wait.wait_send()
    for ph in range(2):
        ring_wait(ph).wait_send()
        chi_wait(ph).wait_send()
        core_copy(ph).wait_send()
        chi_send(ph, core).wait_send()


def shards(sources, contrast, spectrum, measured, receivers, positions):
    hbm = pl.BlockSpec(memory_space=pl.ANY)
    table = jnp.asarray(first_table())
    field = jax.ShapeDtypeStruct((2, ROWS, 128), F32)

    def buf(*shape):
        return pltpu.VMEM(shape, F32)

    dma = pltpu.SemaphoreType.DMA
    new, chi = pl.pallas_call(
        kernel,
        out_shape=(field, field),
        in_specs=[hbm] * 5 + [pl.BlockSpec(memory_space=pltpu.SMEM), hbm],
        out_specs=(hbm, hbm),
        scratch_shapes=[
            buf(2, ROWS, 128),
            buf(2, ROWS, 128),
            buf(2, NREC),
            pltpu.VMEM((1, NREC), jnp.int32),
            pltpu.VMEM((512, 512), BF16),
            pltpu.VMEM((512, 512), BF16),
            pltpu.VMEM((512, 512), BF16),
            pltpu.VMEM((1024, 256), BF16),
            pltpu.VMEM((256, 1024), BF16),
            pltpu.VMEM((256, 1024), BF16),
            buf(2, ROWS, 128),
            buf(2, 4096, 128),
            buf(2, 8, NP, NP),
            buf(2, 2048, 128),
            buf(2, 2048, 128),
            buf(2, 2048, 128),
            buf(2, 2048, 128),
            buf(2, ROWS, 128),
            buf(ROWS, 128),
            buf(2, ROWS, 128),
            buf(2, ROWS, 128),
            buf(2, ROWS, 128),
            pltpu.VMEM((ROWS, NREC), BF16),
            pltpu.VMEM((NC, NREC), BF16),
            buf(3, ROWS, 128),
            buf(2, 3, NC, 128),
            buf(2, 3, NC, 128),
            buf(2, 4, 3, 32, 128),
            buf(2, 2, 32, 128),
            buf(2, ROWS, 128),
            buf(8, 128),
            buf(64, 128),
            buf(8, 128),
            buf(256, 128),
            buf(8, 8, 128),
            buf(GZ, 8, 128),
            buf(8, 128),
            buf(8, 8, 128),
            buf(8, 2 * NC, 128),
            buf(512, NREC),
            dma((7,)),
            dma((3,)),
            dma((4, 4)),
            dma((4, 4)),
            dma((8,)),
            dma((8,)),
        ]
        + [dma] * 8,
        compiler_params=pltpu.CompilerParams(
            collective_id=0, has_side_effects=True, vmem_limit_bytes=60 * 1024 * 1024
        ),
    )(
        sources.reshape(2, ROWS, 128),
        contrast.reshape(2, ROWS, 128),
        spectrum.reshape(4096, NP),
        measured.reshape(2, NREC),
        receivers,
        positions,
        table,
    )
    return new.reshape(sources.shape), chi.reshape(contrast.shape)


def solution(mesh):
    in_specs = (
        P("tx", None, "gz", None, None),
        P(None, "gz", None, None),
        P(None, None, "gz", None),
        P("tx", None, None),
        P("tx", None),
        P("tx", None),
    )
    out_specs = (P("tx", None, "gz", None, None), P(None, "gz", None, None))
    return jax.shard_map(shards, mesh=mesh, in_specs=in_specs, out_specs=out_specs, check_vma=False)
```

```python
import math

import jax
import jax.numpy as jnp
import numpy as np
from jax import lax
from jax.experimental import pallas as pl
from jax.experimental.pallas import tpu as pltpu
from jax.sharding import PartitionSpec as P

MESH = pl.DeviceIdType.MESH
F32 = jnp.float32
BF16 = jnp.bfloat16

reach_cells = 16.0
tikhonov = 1.0
step_length = 0.5
norm_floor = 1e-06

NC = 128
NP = 256
GZ = 32
TX = 8
NREC = 1024
ROWS = 512


def dft_matrix():
    k = np.arange(NP)[:, None]
    n = np.arange(NC)[None, :]
    angle = 2.0 * np.pi * ((k * n) % NP) / NP
    cosine, sine = np.cos(angle), np.sin(angle)
    full = np.zeros((2, NP, 2, NC))
    full[0, :, 0, :] = cosine
    full[0, :, 1, :] = sine
    full[1, :, 0, :] = -sine
    full[1, :, 1, :] = cosine
    return full


def halves(table, axis):
    table = table.astype(np.float32)
    high = table.astype(jnp.bfloat16)
    low = (table - high.astype(np.float32)).astype(jnp.bfloat16)
    return np.concatenate([high, low], axis)


def first_table():
    by_freq = dft_matrix().reshape(2, GZ, 2, 4, 2, NC)
    return halves(by_freq.transpose(2, 1, 0, 3, 4, 5).reshape(2 * NP, 2 * NC), 1)


def bits(x, shift, count):
    return lax.bitwise_and(lax.shift_right_logical(x, shift), (1 << count) - 1)


def freq_index(x):
    return bits(x, 0, 8), bits(x, 8, 1)


def freq_pair_index(x):
    return 8 * bits(x, 0, 5) + 2 * bits(x, 6, 2) + bits(x, 5, 1), bits(x, 8, 1)


def cell_index(x):
    return bits(x, 0, 7), bits(x, 7, 1)


def plane_index(x):
    return 4 * bits(x, 0, 5) + bits(x, 5, 2), bits(x, 7, 1)


def plane_half_index(x):
    return 4 * bits(x, 3, 5) + 2 * bits(x, 2, 1) + bits(x, 0, 1), bits(x, 1, 1)


def fill_table(ref, axis, row_of, column_of, rows_are_freq):
    height, width = ref.shape
    height, width = (height // 2, width) if axis == 0 else (height, width // 2)

    @pl.loop(0, height // 32)
    def _(n):
        a, part_a = row_of(lax.broadcasted_iota(jnp.int32, (32, width), 0) + n * 32)
        b, part_b = column_of(lax.broadcasted_iota(jnp.int32, (32, width), 1))
        quarter = (part_a - part_b) if rows_are_freq else (part_b - part_a)
        turn = lax.bitwise_and(a * b + 64 * quarter, 255)
        table = sin_cos_twelfth(turn.astype(F32) * (12.0 / 256.0))[1]
        high, low = split(table)
        rows = pl.ds(pl.multiple_of(n * 32, 32), 32)
        if axis == 0:
            ref[rows, :] = high
            ref[pl.ds(pl.multiple_of(height + n * 32, 32), 32), :] = low
        else:
            ref[rows, pl.ds(0, width)] = high
            ref[rows, pl.ds(width, width)] = low


def split(x):
    high = x.astype(BF16)
    low = (x - high.astype(F32)).astype(BF16)
    return high, low


def left_dft(table, x):
    depth = x.shape[0]
    high, low = split(x)
    lhs = jnp.concatenate([table[:, :depth], table], axis=1)
    rhs = jnp.concatenate([high, low, high], axis=0)
    return jnp.dot(lhs, rhs, preferred_element_type=F32)


def right_dft(x, table):
    depth = x.shape[1]
    high, low = split(x)
    lhs = jnp.concatenate([high, low, high], axis=1)
    rhs = jnp.concatenate([table[:depth], table], axis=0)
    return jnp.dot(lhs, rhs, preferred_element_type=F32)


def sin_cos_twelfth(radius):
    turns = jnp.floor(radius * (1.0 / 12.0) + 0.5)
    half = (radius - 12.0 * turns) * (math.pi / 12.0)
    sq = half * half
    s = -2.5052108e-08
    for coef in (2.7557319e-06, -1.9841270e-04, 8.3333333e-03, -1.6666667e-01, 1.0):
        s = s * sq + coef
    s = s * half
    c = 2.0876757e-09
    for coef in (-2.7557319e-07, 2.4801587e-05, -1.3888889e-03, 4.1666667e-02, -0.5, 1.0):
        c = c * sq + coef
    return 2.0 * s * c, 1.0 - 2.0 * s * s


def kernel(
    src_hbm, contrast_hbm, spec_hbm, meas_hbm, cell_hbm, pos,
    aq_hbm,
    new_hbm, chi_hbm,
    src, contrast, meas, cell, aq, ap, br, bir, aip, aiq, out_src,
    spec_raw, spec, y_buf, r_buf, u_buf, b_buf, inc, amp_sum, scat, res, drive,
    hot, hot_plane, part, half_in, half_sum, ring_in, chi_own, chi, extra, extra_all,
    obj, obj_all, mf, mf_in, mf_own, mf_all, placed_freq, found_first,
    load_sem, store_sem, send_sem, recv_sem, tx_send, tx_recv, ex_send, ex_recv,
    ob_send, ob_recv, ma_send, ma_recv, mb_send, mb_recv,
):
    me = lax.axis_index("gz")
    tx = lax.axis_index("tx")
    my_y = me // 8
    my_z = lax.rem(me, 8)
    my_x = tx // 2
    core = lax.rem(tx, 2)
    partner = 2 * my_x + 1 - core

    y_part = [8 * lax.rem(my_y + d, 4) for d in range(4)]
    z_part = [lax.rem(my_z + d, 8) for d in range(8)]
    peers = [y_part[i // 8] + z_part[(3 * i) % 8] for i in range(1, GZ)]
    tx_peers = [lax.rem(tx + d, TX) for d in range(1, TX)]
    x_peers = [lax.rem(my_x + d, 4) for d in range(1, 4)]
    group_peers = [lax.rem(me + 4 * d, GZ) for d in range(1, 8)]

    loads = {}
    for n, (name, hbm, vmem) in enumerate(
        (
            ("aq", aq_hbm, aq),
            ("src", src_hbm, src),
            ("meas", meas_hbm, meas),
            ("cell", cell_hbm, cell),
            ("spec0", spec_hbm.at[:, pl.ds(0, 128)], spec_raw.at[0]),
            ("spec1", spec_hbm.at[:, pl.ds(128, 128)], spec_raw.at[1]),
            ("contrast", contrast_hbm, contrast),
        )
    ):
        loads[name] = pltpu.make_async_copy(hbm, vmem, load_sem.at[n])

    def loaded(*names):
        for name in names:
            loads[name].wait()

    barrier = pltpu.get_barrier_semaphore()

    for to in peers:
        pl.semaphore_signal(barrier, inc=1, device_id={"gz": to}, device_id_type=MESH)
    for to in tx_peers:
        pl.semaphore_signal(barrier, inc=1, device_id={"tx": to}, device_id_type=MESH)

    for load in loads.values():
        load.start()
    loaded("meas")

    lane = lax.broadcasted_iota(jnp.int32, (8, 128), 1)
    share = jnp.sum(meas[...] * meas[...], keepdims=True)
    row = jnp.where(lane == 0, pos[0, 0].astype(F32), 0.0)
    row = row + jnp.where(lane == 1, pos[0, 1].astype(F32), 0.0)
    row = row + jnp.where(lane == 2, share, 0.0)
    extra[...] = row
    extra_all[pl.ds(pl.multiple_of(8 * tx, 8), 8), :] = row

    chunks = (
        ((0, 1, 0, 32), (1, 1, 0, 32)),
        ((0, 1, 0, 16), (0, 1, 16, 8), (0, 1, 24, 8), (1, 1, 0, 32)),
        ((0, 2, 0, 16), (0, 1, 16, 16), (1, 1, 16, 16)),
        ((0, 2, 0, 16), (0, 1, 16, 16), (1, 1, 16, 16)),
    )
    buffers = ((y_buf, r_buf), (u_buf, b_buf))

    def exchange_copy(trip, chunk, src_at, dst_at, to):
        phase = trip // 2
        s_ref, d_ref = buffers[trip % 2]
        return pltpu.make_async_remote_copy(
            src_ref=s_ref.at[(phase,) + src_at],
            dst_ref=d_ref.at[(phase,) + dst_at],
            send_sem=send_sem.at[trip, chunk],
            recv_sem=recv_sem.at[trip, chunk],
            device_id={"gz": to},
            device_id_type=MESH,
        )

    def start(trip, chunk):
        first, count, offset, size = chunks[trip][chunk]

        def block(g):
            return pl.ds(first, count), pl.ds(pl.multiple_of(offset + 32 * g, 8), size)

        for to in peers:
            exchange_copy(trip, chunk, block(to), block(me), to).start()
        s_ref, d_ref = buffers[trip % 2]
        for half in range(first, first + count):
            own = (trip // 2, half, pl.ds(pl.multiple_of(offset + 32 * me, 8), size))
            d_ref[own] = s_ref[own]

    def wait(trip, chunk, receive=True):
        first, count, offset, size = chunks[trip][chunk]
        at = (pl.ds(0, count), pl.ds(0, (GZ - 1) * size))
        copy = exchange_copy(trip, chunk, at, at, peers[0])
        if receive:
            copy.wait_recv()
        else:
            copy.wait_send()

    def forward_second(field, phase, h, ph):
        x = jnp.concatenate(
            [
                jnp.concatenate(
                    [field[c, pl.ds((2 * ph + j) * NC, NC), :] for j in range(2)], axis=1
                )
                for c in range(2)
            ],
            axis=0,
        )
        y = left_dft(aq[pl.ds(h * 256, 256), :], x)
        for g in range(GZ):
            for j in range(2):
                y_buf[phase, h, pl.ds(g * 32 + (2 * ph + j) * 8, 8), :] = y[
                    8 * g : 8 * g + 8, j * 128 : j * 128 + 128
                ]

    def middle(phase, sign, ratio):
        @pl.loop(0, 4)
        def _(kk):
            h = kk // 2

            for h_now, needed in (((0, (0,)), (1, (1,))), ((0, (0, 1)), (1, (2,))))[phase]:

                @pl.when(kk == 2 * h_now)
                def _():
                    for chunk in needed:
                        wait(2 * phase, chunk)

            cols = []
            for i in range(2):
                rows = []
                for c in range(2):
                    for p in range(4):
                        first = p * 8 + c * 4 + 2 * lax.rem(kk, 2) + i
                        x = r_buf[phase, h, pl.ds(first, GZ, stride=32), :]
                        if ratio is not None:
                            x = x + ratio * placed_freq[
                                2 * kk + i, c * NC + p * GZ : c * NC + (p + 1) * GZ, :
                            ]
                        rows.append(x)
                cols.append(jnp.concatenate(rows, axis=0))
            z = left_dft(ap[...], jnp.concatenate(cols, axis=1))
            outs = []
            for i in range(2):
                lanes = slice(i * NC, (i + 1) * NC)
                w = right_dft(jnp.concatenate([z[:NP, lanes], z[NP:, lanes]], axis=1), br[...])
                re, im = w[:, :NP], w[:, NP:]
                sr, si = spec[0, 2 * kk + i], spec[1, 2 * kk + i] * sign
                w = jnp.concatenate([re * sr - im * si, re * si + im * sr], axis=1)
                v = right_dft(w, bir[...])
                outs.append(jnp.concatenate([v[:, :NC], v[:, NC:]], axis=0))
            u = left_dft(aip[...], jnp.concatenate(outs, axis=1))
            upper = lax.bitwise_and(lax.broadcasted_iota(jnp.int32, (256, NC), 0), 4) != 0
            even, odd = u[:, :NC], u[:, NC:]
            halves_of_u = (
                jnp.where(upper, pltpu.roll(odd, 4, 0), even),
                jnp.where(upper, odd, pltpu.roll(even, 252, 0)),
            )
            for ph in range(2):
                for g in range(GZ):
                    at = pl.multiple_of(g * 32 + kk * 8, 8)
                    u_buf[phase, ph, pl.ds(at, 8), :] = halves_of_u[ph][8 * g : 8 * g + 8]

            for at_kk, done in (((1, (0,)), (2, (1,)), (3, (2, 3))), ((1, (0,)), (3, (1, 2))))[phase]:

                @pl.when(kk == at_kk)
                def _():
                    for chunk in done:
                        start(2 * phase + 1, chunk)

    def wait_back(phase, ph):
        for chunk in (((0, 1, 2), (3,)), ((0, 1), (2,)))[phase][ph]:
            wait(2 * phase + 1, chunk)

    def inverse_second(phase, ph):
        cols = []
        for p2 in range(2):
            rows = []
            for c in range(2):
                for kk in range(4):
                    for i in range(2):
                        first = kk * 8 + i * 4 + c * 2 + p2
                        rows.append(b_buf[phase, ph, pl.ds(first, GZ, stride=32), :])
            cols.append(jnp.concatenate(rows, axis=0))
        return left_dft(aiq[...], jnp.concatenate(cols, axis=1))

    loaded("aq", "src")
    for h in range(2):
        for ph in range(2):
            forward_second(src, 0, h, ph)
        if h == 0:
            pl.semaphore_wait(barrier, GZ - 1 + TX - 1)
        start(0, h)

    def extra_copy(to, src_ref, dst_ref):
        return pltpu.make_async_remote_copy(
            src_ref=src_ref,
            dst_ref=dst_ref,
            send_sem=ex_send,
            recv_sem=ex_recv,
            device_id={"tx": to},
            device_id_type=MESH,
        )

    for to in tx_peers:
        extra_copy(to, extra, extra_all.at[pl.ds(pl.multiple_of(8 * tx, 8), 8), :]).start()
    extra_sum = extra_all.at[pl.ds(0, 8 * (TX - 1)), :]
    extra_wait = extra_copy(tx_peers[0], extra_sum, extra_sum)

    def geometry(n, rows_n):
        index = lax.broadcasted_iota(jnp.int32, (rows_n, 128), 0) + n * rows_n
        a = lax.shift_right_logical(index, 7) + (me * 4 + NC // 4)
        b = lax.bitwise_and(index, 127)
        c = lax.broadcasted_iota(jnp.int32, (rows_n, 128), 1)
        return a, b, c

    @pl.loop(0, 16)
    def _(n):
        a, b, c = geometry(n, 32)
        b = b - pos[0, 0]
        c = c - pos[0, 1]
        radius = jnp.sqrt((a * a + b * b + c * c).astype(F32))
        amplitude = reach_cells / (reach_cells + radius)
        sine, cosine = sin_cos_twelfth(radius)
        at = pl.ds(pl.multiple_of(n * 32, 32), 32)
        inc[0, at, :] = amplitude * cosine
        inc[1, at, :] = amplitude * sine

    loaded("cell")
    local = cell[...] - me * (ROWS * 128)
    cell_row = lax.shift_right_arithmetic(local, 7)
    cell_lane = lax.bitwise_and(local, 127)

    @pl.loop(0, 16)
    def _(n):
        index = lax.broadcasted_iota(jnp.int32, (32, NREC), 0) + n * 32
        hot[pl.ds(pl.multiple_of(n * 32, 32), 32), :] = jnp.where(
            index == cell_row, 1.0, 0.0
        ).astype(BF16)

    row_index = lax.broadcasted_iota(jnp.int32, (NC, NREC), 0)
    plane = 4 * lax.bitwise_and(row_index, 31) + lax.shift_right_logical(row_index, 5)
    hot_plane[...] = jnp.where(
        plane == lax.shift_right_logical(cell[...], 14), 1.0, 0.0
    ).astype(BF16)

    loaded("spec0", "spec1")

    @pl.loop(0, 8)
    def _(k):
        for c in range(2):
            for n in range(2):
                spec[c, k, :, pl.ds(n * 128, 128)] = spec_raw[
                    n, pl.ds(c * 2048 + k, NP, stride=8), :
                ] * (2.0 ** -24)

    fill_table(ap, 1, freq_index, plane_index, True)
    fill_table(br, 0, cell_index, freq_index, False)
    fill_table(bir, 0, freq_index, cell_index, True)
    fill_table(aip, 1, plane_half_index, freq_index, False)

    def incident_power():
        extra_wait.wait_recv()

        @pl.loop(0, 16)
        def _(n):
            a, b, c = geometry(n, 32)
            a2 = (a * a).astype(F32)
            bf = b.astype(F32)
            cf = c.astype(F32)
            total = jnp.zeros((32, 128), F32)
            for j in range(TX):
                db = bf - extra_all[8 * j : 8 * j + 1, 0:1]
                dc = cf - extra_all[8 * j : 8 * j + 1, 1:2]
                radius = jnp.sqrt(a2 + db * db + dc * dc)
                amplitude = reach_cells / (reach_cells + radius)
                total = total + amplitude * amplitude
            amp_sum[pl.ds(pl.multiple_of(n * 32, 32), 32), :] = total

    middle(0, 1.0, None)
    loaded("contrast")
    fill_table(aiq, 1, cell_index, freq_pair_index, False)
    incident_power()

    def to_partner(s_ref, d_ref, which):
        return pltpu.make_async_remote_copy(
            src_ref=s_ref,
            dst_ref=d_ref,
            send_sem=tx_send.at[which],
            recv_sem=tx_recv.at[which],
            device_id={"tx": partner},
            device_id_type=MESH,
        )

    def plane_rows(p):
        return pl.ds(pl.multiple_of(p * NC, NC), NC)

    def core_copy(ph):
        return to_partner(part.at[:, plane_rows(2 * ph + 1 - core), :], half_in.at[ph], 4 * ph)

    def ring_copy(ph, to, src_ref, dst_ref):
        return pltpu.make_async_remote_copy(
            src_ref=src_ref,
            dst_ref=dst_ref,
            send_sem=tx_send.at[4 * ph + 1],
            recv_sem=tx_recv.at[4 * ph + 1],
            device_id={"tx": 2 * to + core},
            device_id_type=MESH,
        )

    def ring_wait(ph):
        three = ring_in.at[ph, pl.ds(0, 3)]
        return ring_copy(ph, x_peers[0], three, three)

    def own_rows(ph, x):
        return pl.ds(pl.multiple_of((2 * ph + core) * NC + x * 32, 32), 32)

    def chi_copy(ph, to, src_ref, dst_ref):
        return pltpu.make_async_remote_copy(
            src_ref=src_ref,
            dst_ref=dst_ref,
            send_sem=tx_send.at[4 * ph + 2],
            recv_sem=tx_recv.at[4 * ph + 2],
            device_id={"tx": 2 * to + core},
            device_id_type=MESH,
        )

    def chi_wait(ph):
        three = chi.at[:, pl.ds(0, 96), :]
        return chi_copy(ph, x_peers[0], three, three)

    def chi_send(ph, which):
        at = chi.at[:, plane_rows(2 * ph + which), :]
        return to_partner(at, at, 4 * ph + 3)

    def fields(ph):
        wait_back(0, ph)
        o = inverse_second(0, ph)
        for j in range(2):
            at = pl.ds((2 * ph + j) * NC, NC)
            for c in range(2):
                scat[c, at, :] = o[c * NC : (c + 1) * NC, j * NC : (j + 1) * NC]

        @pl.loop(0, 8)
        def _(n):
            at = pl.ds(pl.multiple_of(ph * 256 + n * 32, 32), 32)
            sr, si = src[0, at, :], src[1, at, :]
            tr = inc[0, at, :] + scat[0, at, :]
            ti = inc[1, at, :] + scat[1, at, :]
            inc[0, at, :] = tr
            inc[1, at, :] = ti
            part[0, at, :] = sr * tr + si * ti
            part[1, at, :] = si * tr - sr * ti
            part[2, at, :] = tr * tr + ti * ti

        core_copy(ph).start()

    def ring_start(ph):
        core_copy(ph).wait_recv()
        for q in range(3):
            half_sum[ph, q] = part[q, plane_rows(2 * ph + core), :] + half_in[ph, q]

        for to in x_peers:
            ring_copy(
                ph,
                to,
                half_sum.at[ph, :, pl.ds(pl.multiple_of(to * 32, 32), 32), :],
                ring_in.at[ph, my_x],
            ).start()

        ring_in[ph, my_x] = half_sum[ph, :, pl.ds(pl.multiple_of(my_x * 32, 32), 32), :]

    def contrast_start(ph):
        ring_wait(ph).wait_recv()

        sums = []
        for q in range(3):
            sums.append(
                ring_in[ph, 0, q] + ring_in[ph, 1, q] + ring_in[ph, 2, q] + ring_in[ph, 3, q]
            )
        below = sums[2] + tikhonov
        rows = own_rows(ph, my_x)
        for c in range(2):
            value = (sums[c] + tikhonov * contrast[c, rows, :]) / below
            chi_own[ph, c] = value
            chi[c, rows, :] = value

        for to in x_peers:
            chi_copy(ph, to, chi_own.at[ph], chi.at[:, rows, :]).start()

    def contrast_forward(ph):
        chi_wait(ph).wait_recv()
        chi_send(ph, core).start()

    def residual(ph, acc):
        chi_send(ph, 1 - core).wait_recv()

        def step(n, acc):
            at = pl.ds(pl.multiple_of(ph * 256 + n * 32, 32), 32)
            cr, ci = chi[0, at, :], chi[1, at, :]
            tr, ti = inc[0, at, :], inc[1, at, :]
            rr = cr * tr - ci * ti - src[0, at, :]
            ri = cr * ti + ci * tr - src[1, at, :]
            res[0, at, :] = rr
            res[1, at, :] = ri
            drive[0, at, :] = -(cr * rr + ci * ri)
            drive[1, at, :] = -(cr * ri - ci * rr)
            return acc + (cr * cr + ci * ci) * amp_sum[at, :]

        return lax.fori_loop(0, 8, step, acc)

    def drive_start(ph):
        for h in range(2):
            forward_second(drive, 1, h, ph)
            if ph == 1:
                start(2, 1 + h)
        if ph == 0:
            start(2, 0)

    def misfit_copy(to, src_ref, dst_ref):
        return pltpu.make_async_remote_copy(
            src_ref=src_ref,
            dst_ref=dst_ref,
            send_sem=ma_send,
            recv_sem=ma_recv,
            device_id={"gz": to},
            device_id_type=MESH,
        )

    mf_most = mf_in.at[pl.ds(0, GZ - 1)]
    misfit_wait = misfit_copy(peers[0], mf_most, mf_most)

    def misfit_back(to, src_ref, dst_ref):
        return pltpu.make_async_remote_copy(
            src_ref=src_ref,
            dst_ref=dst_ref,
            send_sem=mb_send,
            recv_sem=mb_recv,
            device_id={"gz": to},
            device_id_type=MESH,
        )

    mf_seven = mf_all.at[pl.ds(0, 7)]
    back_wait = misfit_back(group_peers[0], mf_seven, mf_seven)

    lane_index = lax.broadcasted_iota(jnp.int32, (NC, NREC), 0)

    def found_at(ph):
        rows = pl.ds(ph * 256, 256)
        pieces = [split(scat[c, rows, :]) for c in range(2)]
        columns = jnp.concatenate(
            [pieces[0][0], pieces[1][0], pieces[0][1], pieces[1][1]], axis=1
        )
        return lax.dot_general(
            columns, hot[rows, :], (((0,), (0,)), ((), ())), preferred_element_type=F32
        )

    def misfit_start():
        found = found_first[...] + found_at(1)
        on_lane = lane_index == cell_lane
        inside = (cell_row >= 0) & (cell_row < ROWS)
        misfit = []
        for c in range(2):
            both = found[c * NC : (c + 1) * NC] + found[(2 + c) * NC : (3 + c) * NC]
            sampled = jnp.sum(jnp.where(on_lane, both, 0.0), axis=0, keepdims=True)
            misfit.append(jnp.where(inside, meas[c : c + 1, :] - sampled, 0.0))
        for i in range(8):
            at = slice(i * 128, (i + 1) * 128)
            mf[i] = jnp.concatenate([misfit[0][:, at], misfit[1][:, at]], axis=0)
        mf_in[me] = mf[me // 4]

        for to in peers:
            misfit_copy(to, mf.at[to // 4], mf_in.at[me]).start()

    def misfit_forward():
        misfit_wait.wait_recv()
        total = mf_in[0]
        for g in range(1, GZ):
            total = total + mf_in[g]
        mf_own[...] = total
        mf_all[me // 4] = total

        for to in group_peers:
            misfit_back(to, mf_own, mf_all.at[me // 4]).start()

    def placed_spectrum():
        back_wait.wait_recv()
        mr = jnp.concatenate([mf_all[i, 0:1, :] for i in range(8)], axis=1)
        mi = jnp.concatenate([mf_all[i, 1:2, :] for i in range(8)], axis=1)
        second = lax.bitwise_and(lax.shift_right_logical(cell[...], 7), 127)

        @pl.loop(0, 8)
        def _(k):
            turn = lax.bitwise_and((8 * me + k) * second, 255)
            sine, cosine = sin_cos_twelfth(turn.astype(F32) * (12.0 / 256.0))
            on_lane = lane_index == cell_lane
            v = (
                split(jnp.where(on_lane, mr * cosine + mi * sine, 0.0)),
                split(jnp.where(on_lane, mi * cosine - mr * sine, 0.0)),
            )
            values = jnp.concatenate([v[0][0], v[1][0], v[0][1], v[1][1]], axis=0)
            found = lax.dot_general(
                hot_plane[...], values, (((1,), (1,)), ((), ())), preferred_element_type=F32
            )
            for c in range(2):
                placed_freq[k, pl.ds(c * NC, NC), :] = (
                    found[:, c * NC : (c + 1) * NC] + found[:, (2 + c) * NC : (3 + c) * NC]
                )

    def obj_copy(to, src_ref, dst_ref):
        return pltpu.make_async_remote_copy(
            src_ref=src_ref,
            dst_ref=dst_ref,
            send_sem=ob_send,
            recv_sem=ob_recv,
            device_id={"gz": to},
            device_id_type=MESH,
        )

    obj_most = obj_all.at[pl.ds(0, GZ - 1)]
    obj_wait = obj_copy(peers[0], obj_most, obj_most)

    def object_start(acc):
        own = jnp.sum(acc, axis=0, keepdims=True)
        obj[...] = own
        obj_all[me] = own
        for to in peers:
            obj_copy(to, obj, obj_all.at[me]).start()

    def object_ratio():
        obj_wait.wait_recv()
        rows = jnp.concatenate([obj_all[g] for g in range(GZ)], axis=0)
        object_norm = jnp.sum(rows, keepdims=True)
        data_norm = jnp.zeros((1, 1), F32)
        for j in range(TX):
            data_norm = data_norm + extra_all[8 * j : 8 * j + 1, 2:3]
        return object_norm / (data_norm + norm_floor)

    fields(0)
    found_first[...] = found_at(0)
    ring_start(0)
    contrast_start(0)
    fields(1)
    contrast_forward(0)
    ring_start(1)
    misfit_start()
    acc = residual(0, jnp.zeros((32, 128), F32))
    drive_start(0)
    contrast_start(1)
    misfit_forward()
    contrast_forward(1)
    acc = residual(1, acc)
    object_start(acc)
    drive_start(1)
    placed_spectrum()
    chi_store = pltpu.make_async_copy(chi, chi_hbm, store_sem.at[2])
    chi_store.start()
    middle(1, -1.0, object_ratio())
    stores = []
    for ph in range(2):
        wait_back(1, ph)
        o = inverse_second(1, ph)
        for j in range(2):
            at = pl.ds((2 * ph + j) * NC, NC)
            for c in range(2):
                back = o[c * NC : (c + 1) * NC, j * NC : (j + 1) * NC]
                out_src[c, at, :] = src[c, at, :] + step_length * (res[c, at, :] + back)
        at = pl.ds(ph * 256, 256)
        stores.append(
            pltpu.make_async_copy(out_src.at[:, at, :], new_hbm.at[:, at, :], store_sem.at[ph])
        )
        stores[-1].start()

    for trip in range(4):
        for chunk in range(len(chunks[trip])):
            wait(trip, chunk, False)

    chi_store.wait()
    for store in stores:
        store.wait()
    obj_wait.wait_send()
    misfit_wait.wait_send()
    back_wait.wait_send()
    extra_wait.wait_send()
    for ph in range(2):
        ring_wait(ph).wait_send()
        chi_wait(ph).wait_send()
        core_copy(ph).wait_send()
        chi_send(ph, core).wait_send()


def shards(sources, contrast, spectrum, measured, receivers, positions):
    hbm = pl.BlockSpec(memory_space=pl.ANY)
    table = jnp.asarray(first_table())
    field = jax.ShapeDtypeStruct((2, ROWS, 128), F32)

    def buf(*shape):
        return pltpu.VMEM(shape, F32)

    dma = pltpu.SemaphoreType.DMA
    new, chi = pl.pallas_call(
        kernel,
        out_shape=(field, field),
        in_specs=[hbm] * 5 + [pl.BlockSpec(memory_space=pltpu.SMEM), hbm],
        out_specs=(hbm, hbm),
        scratch_shapes=[
            buf(2, ROWS, 128),
            buf(2, ROWS, 128),
            buf(2, NREC),
            pltpu.VMEM((1, NREC), jnp.int32),
            pltpu.VMEM((512, 512), BF16),
            pltpu.VMEM((512, 512), BF16),
            pltpu.VMEM((512, 512), BF16),
            pltpu.VMEM((1024, 256), BF16),
            pltpu.VMEM((256, 1024), BF16),
            pltpu.VMEM((256, 1024), BF16),
            buf(2, ROWS, 128),
            buf(2, 4096, 128),
            buf(2, 8, NP, NP),
            buf(2, 2, 1024, 128),
            buf(2, 2, 1024, 128),
            buf(2, 2, 1024, 128),
            buf(2, 2, 1024, 128),
            buf(2, ROWS, 128),
            buf(ROWS, 128),
            buf(2, ROWS, 128),
            buf(2, ROWS, 128),
            buf(2, ROWS, 128),
            pltpu.VMEM((ROWS, NREC), BF16),
            pltpu.VMEM((NC, NREC), BF16),
            buf(3, ROWS, 128),
            buf(2, 3, NC, 128),
            buf(2, 3, NC, 128),
            buf(2, 4, 3, 32, 128),
            buf(2, 2, 32, 128),
            buf(2, ROWS, 128),
            buf(8, 128),
            buf(64, 128),
            buf(1, 128),
            buf(GZ, 1, 128),
            buf(8, 2, 128),
            buf(GZ, 2, 128),
            buf(2, 128),
            buf(8, 2, 128),
            buf(8, 2 * NC, 128),
            buf(512, NREC),
            dma((7,)),
            dma((3,)),
            dma((4, 4)),
            dma((4, 4)),
            dma((8,)),
            dma((8,)),
        ]
        + [dma] * 8,
        compiler_params=pltpu.CompilerParams(
            collective_id=0, has_side_effects=True, vmem_limit_bytes=60 * 1024 * 1024
        ),
    )(
        sources.reshape(2, ROWS, 128),
        contrast.reshape(2, ROWS, 128),
        spectrum.reshape(4096, NP),
        measured.reshape(2, NREC),
        receivers,
        positions,
        table,
    )
    return new.reshape(sources.shape), chi.reshape(contrast.shape)


def solution(mesh):
    in_specs = (
        P("tx", None, "gz", None, None),
        P(None, "gz", None, None),
        P(None, None, "gz", None),
        P("tx", None, None),
        P("tx", None),
        P("tx", None),
    )
    out_specs = (P("tx", None, "gz", None, None), P(None, "gz", None, None))
    return jax.shard_map(shards, mesh=mesh, in_specs=in_specs, out_specs=out_specs, check_vma=False)
```

```python
import math

import jax
import jax.numpy as jnp
import numpy as np
from jax import lax
from jax.experimental import pallas as pl
from jax.experimental.pallas import tpu as pltpu
from jax.sharding import PartitionSpec as P

MESH = pl.DeviceIdType.MESH
F32 = jnp.float32
BF16 = jnp.bfloat16

reach_cells = 16.0
tikhonov = 1.0
step_length = 0.5
norm_floor = 1e-06

NC = 128
NP = 256
GZ = 32
TX = 8
NREC = 1024
ROWS = 512


def dft_matrix():
    k = np.arange(NP)[:, None]
    n = np.arange(NC)[None, :]
    angle = 2.0 * np.pi * ((k * n) % NP) / NP
    cosine, sine = np.cos(angle), np.sin(angle)
    full = np.zeros((2, NP, 2, NC))
    full[0, :, 0, :] = cosine
    full[0, :, 1, :] = sine
    full[1, :, 0, :] = -sine
    full[1, :, 1, :] = cosine
    return full


def halves(table, axis):
    table = table.astype(np.float32)
    high = table.astype(jnp.bfloat16)
    low = (table - high.astype(np.float32)).astype(jnp.bfloat16)
    return np.concatenate([high, low], axis)


def first_table():
    by_freq = dft_matrix().reshape(2, GZ, 2, 4, 2, NC)
    return halves(by_freq.transpose(2, 1, 0, 3, 4, 5).reshape(2 * NP, 2 * NC), 1)


def bits(x, shift, count):
    return lax.bitwise_and(lax.shift_right_logical(x, shift), (1 << count) - 1)


def freq_index(x):
    return bits(x, 0, 8), bits(x, 8, 1)


def freq_pair_index(x):
    return 8 * bits(x, 0, 5) + 2 * bits(x, 6, 2) + bits(x, 5, 1), bits(x, 8, 1)


def cell_index(x):
    return bits(x, 0, 7), bits(x, 7, 1)


def plane_index(x):
    return 4 * bits(x, 0, 5) + bits(x, 5, 2), bits(x, 7, 1)


def plane_half_index(x):
    return 4 * bits(x, 3, 5) + 2 * bits(x, 2, 1) + bits(x, 0, 1), bits(x, 1, 1)


def fill_table(ref, axis, row_of, column_of, rows_are_freq):
    height, width = ref.shape
    height, width = (height // 2, width) if axis == 0 else (height, width // 2)

    @pl.loop(0, height // 32)
    def _(n):
        a, part_a = row_of(lax.broadcasted_iota(jnp.int32, (32, width), 0) + n * 32)
        b, part_b = column_of(lax.broadcasted_iota(jnp.int32, (32, width), 1))
        quarter = (part_a - part_b) if rows_are_freq else (part_b - part_a)
        turn = lax.bitwise_and(a * b + 64 * quarter, 255)
        table = sin_cos_twelfth(turn.astype(F32) * (12.0 / 256.0))[1]
        high, low = split(table)
        rows = pl.ds(pl.multiple_of(n * 32, 32), 32)
        if axis == 0:
            ref[rows, :] = high
            ref[pl.ds(pl.multiple_of(height + n * 32, 32), 32), :] = low
        else:
            ref[rows, pl.ds(0, width)] = high
            ref[rows, pl.ds(width, width)] = low


def split(x):
    high = x.astype(BF16)
    low = (x - high.astype(F32)).astype(BF16)
    return high, low


def left_dft(table, x):
    depth = x.shape[0]
    high, low = split(x)
    lhs = jnp.concatenate([table[:, :depth], table], axis=1)
    rhs = jnp.concatenate([high, low, high], axis=0)
    return jnp.dot(lhs, rhs, preferred_element_type=F32)


def right_dft(x, table):
    depth = x.shape[1]
    high, low = split(x)
    lhs = jnp.concatenate([high, low, high], axis=1)
    rhs = jnp.concatenate([table[:depth], table], axis=0)
    return jnp.dot(lhs, rhs, preferred_element_type=F32)


def sin_cos_twelfth(radius):
    turns = jnp.floor(radius * (1.0 / 12.0) + 0.5)
    half = (radius - 12.0 * turns) * (math.pi / 12.0)
    sq = half * half
    s = -2.5052108e-08
    for coef in (2.7557319e-06, -1.9841270e-04, 8.3333333e-03, -1.6666667e-01, 1.0):
        s = s * sq + coef
    s = s * half
    c = 2.0876757e-09
    for coef in (-2.7557319e-07, 2.4801587e-05, -1.3888889e-03, 4.1666667e-02, -0.5, 1.0):
        c = c * sq + coef
    return 2.0 * s * c, 1.0 - 2.0 * s * s


def kernel(
    src_hbm, contrast_hbm, spec_hbm, meas_hbm, cell_hbm, pos,
    aq_hbm,
    new_hbm, chi_hbm,
    src, contrast, meas, cell, aq, ap, br, bir, aip, aiq, out_src,
    spec_raw, spec, y_buf, r_buf, u_buf, b_buf, inc, amp_sum, scat, res, drive,
    hot, hot_plane, part, half_in, half_sum, ring_in, chi_own, chi, extra, extra_all,
    obj, obj_all, mf, mf_in, mf_own, mf_all, placed_freq, found_first,
    load_sem, store_sem, send_sem, recv_sem, tx_send, tx_recv, ex_send, ex_recv,
    ob_send, ob_recv, ma_send, ma_recv, mb_send, mb_recv,
):
    me = lax.axis_index("gz")
    tx = lax.axis_index("tx")
    my_y = me // 8
    my_z = lax.rem(me, 8)
    my_x = tx // 2
    core = lax.rem(tx, 2)
    partner = 2 * my_x + 1 - core

    y_part = [8 * lax.rem(my_y + d, 4) for d in range(4)]
    z_part = [lax.rem(my_z + d, 8) for d in range(8)]
    peers = [y_part[i // 8] + z_part[(3 * i) % 8] for i in range(1, GZ)]
    tx_peers = [lax.rem(tx + d, TX) for d in range(1, TX)]
    x_peers = [lax.rem(my_x + d, 4) for d in range(1, 4)]
    group_peers = [lax.rem(me + 4 * d, GZ) for d in range(1, 8)]

    loads = {}
    for n, (name, hbm, vmem) in enumerate(
        (
            ("aq", aq_hbm, aq),
            ("src", src_hbm, src),
            ("meas", meas_hbm, meas),
            ("cell", cell_hbm, cell),
            ("spec0", spec_hbm.at[:, pl.ds(0, 128)], spec_raw.at[0]),
            ("spec1", spec_hbm.at[:, pl.ds(128, 128)], spec_raw.at[1]),
            ("contrast", contrast_hbm, contrast),
        )
    ):
        loads[name] = pltpu.make_async_copy(hbm, vmem, load_sem.at[n])

    def loaded(*names):
        for name in names:
            loads[name].wait()

    barrier = pltpu.get_barrier_semaphore()

    for to in peers:
        pl.semaphore_signal(barrier, inc=1, device_id={"gz": to}, device_id_type=MESH)
    for to in tx_peers:
        pl.semaphore_signal(barrier, inc=1, device_id={"tx": to}, device_id_type=MESH)

    for load in loads.values():
        load.start()
    loaded("meas")

    lane = lax.broadcasted_iota(jnp.int32, (8, 128), 1)
    share = jnp.sum(meas[...] * meas[...], keepdims=True)
    row = jnp.where(lane == 0, pos[0, 0].astype(F32), 0.0)
    row = row + jnp.where(lane == 1, pos[0, 1].astype(F32), 0.0)
    row = row + jnp.where(lane == 2, share, 0.0)
    extra[...] = row
    extra_all[pl.ds(pl.multiple_of(8 * tx, 8), 8), :] = row

    chunks = (
        ((0, 1, 0, 32), (1, 1, 0, 32)),
        ((0, 1, 0, 16), (0, 1, 16, 8), (0, 1, 24, 8), (1, 1, 0, 32)),
        ((0, 2, 0, 16), (0, 1, 16, 16), (1, 1, 16, 16)),
        ((0, 2, 0, 8), (0, 2, 8, 8), (0, 1, 16, 16), (1, 1, 16, 16)),
    )
    buffers = ((y_buf, r_buf), (u_buf, b_buf))

    def exchange_copy(trip, chunk, src_at, dst_at, to):
        phase = trip // 2
        s_ref, d_ref = buffers[trip % 2]
        return pltpu.make_async_remote_copy(
            src_ref=s_ref.at[(phase,) + src_at],
            dst_ref=d_ref.at[(phase,) + dst_at],
            send_sem=send_sem.at[trip, chunk],
            recv_sem=recv_sem.at[trip, chunk],
            device_id={"gz": to},
            device_id_type=MESH,
        )

    def start(trip, chunk):
        first, count, offset, size = chunks[trip][chunk]

        def block(g):
            return pl.ds(first, count), pl.ds(pl.multiple_of(offset + 32 * g, 8), size)

        for to in peers:
            exchange_copy(trip, chunk, block(to), block(me), to).start()
        s_ref, d_ref = buffers[trip % 2]
        for half in range(first, first + count):
            own = (trip // 2, half, pl.ds(pl.multiple_of(offset + 32 * me, 8), size))
            d_ref[own] = s_ref[own]

    def wait(trip, chunk, receive=True):
        first, count, offset, size = chunks[trip][chunk]
        at = (pl.ds(0, count), pl.ds(0, (GZ - 1) * size))
        copy = exchange_copy(trip, chunk, at, at, peers[0])
        if receive:
            copy.wait_recv()
        else:
            copy.wait_send()

    def forward_second(field, phase, h, ph):
        x = jnp.concatenate(
            [
                jnp.concatenate(
                    [field[c, pl.ds((2 * ph + j) * NC, NC), :] for j in range(2)], axis=1
                )
                for c in range(2)
            ],
            axis=0,
        )
        y = left_dft(aq[pl.ds(h * 256, 256), :], x)
        for g in range(GZ):
            for j in range(2):
                y_buf[phase, h, pl.ds(g * 32 + (2 * ph + j) * 8, 8), :] = y[
                    8 * g : 8 * g + 8, j * 128 : j * 128 + 128
                ]

    def middle(phase, sign, ratio):
        @pl.loop(0, 4)
        def _(kk):
            h = kk // 2

            for h_now, needed in (((0, (0,)), (1, (1,))), ((0, (0, 1)), (1, (2,))))[phase]:

                @pl.when(kk == 2 * h_now)
                def _():
                    for chunk in needed:
                        wait(2 * phase, chunk)

            cols = []
            for i in range(2):
                rows = []
                for c in range(2):
                    for p in range(4):
                        first = p * 8 + c * 4 + 2 * lax.rem(kk, 2) + i
                        x = r_buf[phase, h, pl.ds(first, GZ, stride=32), :]
                        if ratio is not None:
                            x = x + ratio * placed_freq[
                                2 * kk + i, c * NC + p * GZ : c * NC + (p + 1) * GZ, :
                            ]
                        rows.append(x)
                cols.append(jnp.concatenate(rows, axis=0))
            z = left_dft(ap[...], jnp.concatenate(cols, axis=1))
            outs = []
            for i in range(2):
                lanes = slice(i * NC, (i + 1) * NC)
                w = right_dft(jnp.concatenate([z[:NP, lanes], z[NP:, lanes]], axis=1), br[...])
                re, im = w[:, :NP], w[:, NP:]
                sr, si = spec[0, 2 * kk + i], spec[1, 2 * kk + i] * sign
                w = jnp.concatenate([re * sr - im * si, re * si + im * sr], axis=1)
                v = right_dft(w, bir[...])
                outs.append(jnp.concatenate([v[:, :NC], v[:, NC:]], axis=0))
            u = left_dft(aip[...], jnp.concatenate(outs, axis=1))
            upper = lax.bitwise_and(lax.broadcasted_iota(jnp.int32, (256, NC), 0), 4) != 0
            even, odd = u[:, :NC], u[:, NC:]
            halves_of_u = (
                jnp.where(upper, pltpu.roll(odd, 4, 0), even),
                jnp.where(upper, odd, pltpu.roll(even, 252, 0)),
            )
            for ph in range(2):
                for g in range(GZ):
                    at = pl.multiple_of(g * 32 + kk * 8, 8)
                    u_buf[phase, ph, pl.ds(at, 8), :] = halves_of_u[ph][8 * g : 8 * g + 8]

            for at_kk, done in (((1, (0,)), (2, (1,)), (3, (2, 3))), ((0, (0,)), (1, (1,)), (3, (2, 3))))[phase]:

                @pl.when(kk == at_kk)
                def _():
                    for chunk in done:
                        start(2 * phase + 1, chunk)

    def wait_back(phase, ph):
        for chunk in ((0, 1, 2), (3,))[ph]:
            wait(2 * phase + 1, chunk)

    def inverse_second(phase, ph):
        cols = []
        for p2 in range(2):
            rows = []
            for c in range(2):
                for kk in range(4):
                    for i in range(2):
                        first = kk * 8 + i * 4 + c * 2 + p2
                        rows.append(b_buf[phase, ph, pl.ds(first, GZ, stride=32), :])
            cols.append(jnp.concatenate(rows, axis=0))
        return left_dft(aiq[...], jnp.concatenate(cols, axis=1))

    loaded("aq", "src")
    for h in range(2):
        for ph in range(2):
            forward_second(src, 0, h, ph)
        if h == 0:
            pl.semaphore_wait(barrier, GZ - 1 + TX - 1)
        start(0, h)

    def extra_copy(to, src_ref, dst_ref):
        return pltpu.make_async_remote_copy(
            src_ref=src_ref,
            dst_ref=dst_ref,
            send_sem=ex_send,
            recv_sem=ex_recv,
            device_id={"tx": to},
            device_id_type=MESH,
        )

    for to in tx_peers:
        extra_copy(to, extra, extra_all.at[pl.ds(pl.multiple_of(8 * tx, 8), 8), :]).start()
    extra_sum = extra_all.at[pl.ds(0, 8 * (TX - 1)), :]
    extra_wait = extra_copy(tx_peers[0], extra_sum, extra_sum)

    def geometry(n, rows_n):
        index = lax.broadcasted_iota(jnp.int32, (rows_n, 128), 0) + n * rows_n
        a = lax.shift_right_logical(index, 7) + (me * 4 + NC // 4)
        b = lax.bitwise_and(index, 127)
        c = lax.broadcasted_iota(jnp.int32, (rows_n, 128), 1)
        return a, b, c

    @pl.loop(0, 16)
    def _(n):
        a, b, c = geometry(n, 32)
        b = b - pos[0, 0]
        c = c - pos[0, 1]
        radius = jnp.sqrt((a * a + b * b + c * c).astype(F32))
        amplitude = reach_cells / (reach_cells + radius)
        sine, cosine = sin_cos_twelfth(radius)
        at = pl.ds(pl.multiple_of(n * 32, 32), 32)
        inc[0, at, :] = amplitude * cosine
        inc[1, at, :] = amplitude * sine

    loaded("cell")
    local = cell[...] - me * (ROWS * 128)
    cell_row = lax.shift_right_arithmetic(local, 7)
    cell_lane = lax.bitwise_and(local, 127)

    @pl.loop(0, 16)
    def _(n):
        index = lax.broadcasted_iota(jnp.int32, (32, NREC), 0) + n * 32
        hot[pl.ds(pl.multiple_of(n * 32, 32), 32), :] = jnp.where(
            index == cell_row, 1.0, 0.0
        ).astype(BF16)

    row_index = lax.broadcasted_iota(jnp.int32, (NC, NREC), 0)
    plane = 4 * lax.bitwise_and(row_index, 31) + lax.shift_right_logical(row_index, 5)
    hot_plane[...] = jnp.where(
        plane == lax.shift_right_logical(cell[...], 14), 1.0, 0.0
    ).astype(BF16)

    loaded("spec0", "spec1")

    @pl.loop(0, 8)
    def _(k):
        for c in range(2):
            for n in range(2):
                spec[c, k, :, pl.ds(n * 128, 128)] = spec_raw[
                    n, pl.ds(c * 2048 + k, NP, stride=8), :
                ] * (2.0 ** -24)

    fill_table(ap, 1, freq_index, plane_index, True)
    fill_table(br, 0, cell_index, freq_index, False)
    fill_table(bir, 0, freq_index, cell_index, True)
    fill_table(aip, 1, plane_half_index, freq_index, False)

    def incident_power():
        extra_wait.wait_recv()

        @pl.loop(0, 16)
        def _(n):
            a, b, c = geometry(n, 32)
            a2 = (a * a).astype(F32)
            bf = b.astype(F32)
            cf = c.astype(F32)
            total = jnp.zeros((32, 128), F32)
            for j in range(TX):
                db = bf - extra_all[8 * j : 8 * j + 1, 0:1]
                dc = cf - extra_all[8 * j : 8 * j + 1, 1:2]
                radius = jnp.sqrt(a2 + db * db + dc * dc)
                amplitude = reach_cells / (reach_cells + radius)
                total = total + amplitude * amplitude
            amp_sum[pl.ds(pl.multiple_of(n * 32, 32), 32), :] = total

    middle(0, 1.0, None)
    loaded("contrast")
    fill_table(aiq, 1, cell_index, freq_pair_index, False)
    incident_power()

    def to_partner(s_ref, d_ref, which):
        return pltpu.make_async_remote_copy(
            src_ref=s_ref,
            dst_ref=d_ref,
            send_sem=tx_send.at[which],
            recv_sem=tx_recv.at[which],
            device_id={"tx": partner},
            device_id_type=MESH,
        )

    def plane_rows(p):
        return pl.ds(pl.multiple_of(p * NC, NC), NC)

    def core_copy(ph):
        return to_partner(part.at[:, plane_rows(2 * ph + 1 - core), :], half_in.at[ph], 4 * ph)

    def ring_copy(ph, to, src_ref, dst_ref):
        return pltpu.make_async_remote_copy(
            src_ref=src_ref,
            dst_ref=dst_ref,
            send_sem=tx_send.at[4 * ph + 1],
            recv_sem=tx_recv.at[4 * ph + 1],
            device_id={"tx": 2 * to + core},
            device_id_type=MESH,
        )

    def ring_wait(ph):
        three = ring_in.at[ph, pl.ds(0, 3)]
        return ring_copy(ph, x_peers[0], three, three)

    def own_rows(ph, x):
        return pl.ds(pl.multiple_of((2 * ph + core) * NC + x * 32, 32), 32)

    def chi_copy(ph, to, src_ref, dst_ref):
        return pltpu.make_async_remote_copy(
            src_ref=src_ref,
            dst_ref=dst_ref,
            send_sem=tx_send.at[4 * ph + 2],
            recv_sem=tx_recv.at[4 * ph + 2],
            device_id={"tx": 2 * to + core},
            device_id_type=MESH,
        )

    def chi_wait(ph):
        three = chi.at[:, pl.ds(0, 96), :]
        return chi_copy(ph, x_peers[0], three, three)

    def chi_send(ph, which):
        at = chi.at[:, plane_rows(2 * ph + which), :]
        return to_partner(at, at, 4 * ph + 3)

    def fields(ph):
        wait_back(0, ph)
        o = inverse_second(0, ph)
        for j in range(2):
            at = pl.ds((2 * ph + j) * NC, NC)
            for c in range(2):
                scat[c, at, :] = o[c * NC : (c + 1) * NC, j * NC : (j + 1) * NC]

        @pl.loop(0, 8)
        def _(n):
            at = pl.ds(pl.multiple_of(ph * 256 + n * 32, 32), 32)
            sr, si = src[0, at, :], src[1, at, :]
            tr = inc[0, at, :] + scat[0, at, :]
            ti = inc[1, at, :] + scat[1, at, :]
            inc[0, at, :] = tr
            inc[1, at, :] = ti
            part[0, at, :] = sr * tr + si * ti
            part[1, at, :] = si * tr - sr * ti
            part[2, at, :] = tr * tr + ti * ti

        core_copy(ph).start()

    def ring_start(ph):
        core_copy(ph).wait_recv()
        for q in range(3):
            half_sum[ph, q] = part[q, plane_rows(2 * ph + core), :] + half_in[ph, q]

        for to in x_peers:
            ring_copy(
                ph,
                to,
                half_sum.at[ph, :, pl.ds(pl.multiple_of(to * 32, 32), 32), :],
                ring_in.at[ph, my_x],
            ).start()

        ring_in[ph, my_x] = half_sum[ph, :, pl.ds(pl.multiple_of(my_x * 32, 32), 32), :]

    def contrast_start(ph):
        ring_wait(ph).wait_recv()

        sums = []
        for q in range(3):
            sums.append(
                ring_in[ph, 0, q] + ring_in[ph, 1, q] + ring_in[ph, 2, q] + ring_in[ph, 3, q]
            )
        below = sums[2] + tikhonov
        rows = own_rows(ph, my_x)
        for c in range(2):
            value = (sums[c] + tikhonov * contrast[c, rows, :]) / below
            chi_own[ph, c] = value
            chi[c, rows, :] = value

        for to in x_peers:
            chi_copy(ph, to, chi_own.at[ph], chi.at[:, rows, :]).start()

    def contrast_forward(ph):
        chi_wait(ph).wait_recv()
        chi_send(ph, core).start()

    def residual(ph, acc):
        chi_send(ph, 1 - core).wait_recv()

        def step(n, acc):
            at = pl.ds(pl.multiple_of(ph * 256 + n * 32, 32), 32)
            cr, ci = chi[0, at, :], chi[1, at, :]
            tr, ti = inc[0, at, :], inc[1, at, :]
            rr = cr * tr - ci * ti - src[0, at, :]
            ri = cr * ti + ci * tr - src[1, at, :]
            res[0, at, :] = rr
            res[1, at, :] = ri
            drive[0, at, :] = -(cr * rr + ci * ri)
            drive[1, at, :] = -(cr * ri - ci * rr)
            return acc + (cr * cr + ci * ci) * amp_sum[at, :]

        return lax.fori_loop(0, 8, step, acc)

    def drive_start(ph):
        for h in range(2):
            forward_second(drive, 1, h, ph)
            if ph == 1:
                start(2, 1 + h)
        if ph == 0:
            start(2, 0)

    def misfit_copy(to, src_ref, dst_ref):
        return pltpu.make_async_remote_copy(
            src_ref=src_ref,
            dst_ref=dst_ref,
            send_sem=ma_send,
            recv_sem=ma_recv,
            device_id={"gz": to},
            device_id_type=MESH,
        )

    mf_most = mf_in.at[pl.ds(0, GZ - 1)]
    misfit_wait = misfit_copy(peers[0], mf_most, mf_most)

    def misfit_back(to, src_ref, dst_ref):
        return pltpu.make_async_remote_copy(
            src_ref=src_ref,
            dst_ref=dst_ref,
            send_sem=mb_send,
            recv_sem=mb_recv,
            device_id={"gz": to},
            device_id_type=MESH,
        )

    mf_seven = mf_all.at[pl.ds(0, 7)]
    back_wait = misfit_back(group_peers[0], mf_seven, mf_seven)

    lane_index = lax.broadcasted_iota(jnp.int32, (NC, NREC), 0)

    def found_at(ph):
        rows = pl.ds(ph * 256, 256)
        pieces = [split(scat[c, rows, :]) for c in range(2)]
        columns = jnp.concatenate(
            [pieces[0][0], pieces[1][0], pieces[0][1], pieces[1][1]], axis=1
        )
        return lax.dot_general(
            columns, hot[rows, :], (((0,), (0,)), ((), ())), preferred_element_type=F32
        )

    def misfit_start():
        found = found_first[...] + found_at(1)
        on_lane = lane_index == cell_lane
        inside = (cell_row >= 0) & (cell_row < ROWS)
        misfit = []
        for c in range(2):
            both = found[c * NC : (c + 1) * NC] + found[(2 + c) * NC : (3 + c) * NC]
            sampled = jnp.sum(jnp.where(on_lane, both, 0.0), axis=0, keepdims=True)
            misfit.append(jnp.where(inside, meas[c : c + 1, :] - sampled, 0.0))
        for i in range(8):
            at = slice(i * 128, (i + 1) * 128)
            mf[i] = jnp.concatenate([misfit[0][:, at], misfit[1][:, at]], axis=0)
        mf_in[me] = mf[me // 4]

        for to in peers:
            misfit_copy(to, mf.at[to // 4], mf_in.at[me]).start()

    def misfit_forward():
        misfit_wait.wait_recv()
        total = mf_in[0]
        for g in range(1, GZ):
            total = total + mf_in[g]
        mf_own[...] = total
        mf_all[me // 4] = total

        for to in group_peers:
            misfit_back(to, mf_own, mf_all.at[me // 4]).start()

    def placed_spectrum():
        back_wait.wait_recv()
        mr = jnp.concatenate([mf_all[i, 0:1, :] for i in range(8)], axis=1)
        mi = jnp.concatenate([mf_all[i, 1:2, :] for i in range(8)], axis=1)
        second = lax.bitwise_and(lax.shift_right_logical(cell[...], 7), 127)

        @pl.loop(0, 8)
        def _(k):
            turn = lax.bitwise_and((8 * me + k) * second, 255)
            sine, cosine = sin_cos_twelfth(turn.astype(F32) * (12.0 / 256.0))
            on_lane = lane_index == cell_lane
            v = (
                split(jnp.where(on_lane, mr * cosine + mi * sine, 0.0)),
                split(jnp.where(on_lane, mi * cosine - mr * sine, 0.0)),
            )
            values = jnp.concatenate([v[0][0], v[1][0], v[0][1], v[1][1]], axis=0)
            found = lax.dot_general(
                hot_plane[...], values, (((1,), (1,)), ((), ())), preferred_element_type=F32
            )
            for c in range(2):
                placed_freq[k, pl.ds(c * NC, NC), :] = (
                    found[:, c * NC : (c + 1) * NC] + found[:, (2 + c) * NC : (3 + c) * NC]
                )

    def obj_copy(to, src_ref, dst_ref):
        return pltpu.make_async_remote_copy(
            src_ref=src_ref,
            dst_ref=dst_ref,
            send_sem=ob_send,
            recv_sem=ob_recv,
            device_id={"gz": to},
            device_id_type=MESH,
        )

    obj_most = obj_all.at[pl.ds(0, GZ - 1)]
    obj_wait = obj_copy(peers[0], obj_most, obj_most)

    def object_start(acc):
        own = jnp.sum(acc, axis=0, keepdims=True)
        obj[...] = own
        obj_all[me] = own
        for to in peers:
            obj_copy(to, obj, obj_all.at[me]).start()

    def object_ratio():
        obj_wait.wait_recv()
        rows = jnp.concatenate([obj_all[g] for g in range(GZ)], axis=0)
        object_norm = jnp.sum(rows, keepdims=True)
        data_norm = jnp.zeros((1, 1), F32)
        for j in range(TX):
            data_norm = data_norm + extra_all[8 * j : 8 * j + 1, 2:3]
        return object_norm / (data_norm + norm_floor)

    fields(0)
    found_first[...] = found_at(0)
    ring_start(0)
    contrast_start(0)
    fields(1)
    misfit_start()
    ring_start(1)
    contrast_forward(0)
    acc = residual(0, jnp.zeros((32, 128), F32))
    drive_start(0)
    contrast_start(1)
    misfit_forward()
    contrast_forward(1)
    acc = residual(1, acc)
    object_start(acc)
    drive_start(1)
    placed_spectrum()
    chi_store = pltpu.make_async_copy(chi, chi_hbm, store_sem.at[2])
    chi_store.start()
    middle(1, -1.0, object_ratio())
    stores = []
    for ph in range(2):
        wait_back(1, ph)
        o = inverse_second(1, ph)
        for j in range(2):
            at = pl.ds((2 * ph + j) * NC, NC)
            for c in range(2):
                back = o[c * NC : (c + 1) * NC, j * NC : (j + 1) * NC]
                out_src[c, at, :] = src[c, at, :] + step_length * (res[c, at, :] + back)
        at = pl.ds(ph * 256, 256)
        stores.append(
            pltpu.make_async_copy(out_src.at[:, at, :], new_hbm.at[:, at, :], store_sem.at[ph])
        )
        stores[-1].start()

    for trip in range(4):
        for chunk in range(len(chunks[trip])):
            wait(trip, chunk, False)

    chi_store.wait()
    for store in stores:
        store.wait()
    obj_wait.wait_send()
    misfit_wait.wait_send()
    back_wait.wait_send()
    extra_wait.wait_send()
    for ph in range(2):
        ring_wait(ph).wait_send()
        chi_wait(ph).wait_send()
        core_copy(ph).wait_send()
        chi_send(ph, core).wait_send()


def deliver_kernel(new_in, chi_in, new_out, chi_out):
    new_out[...] = new_in[...]
    chi_out[...] = chi_in[...]


def deliver(new, chi):
    block = pl.BlockSpec(memory_space=pltpu.VMEM)
    shape = jax.ShapeDtypeStruct((2, ROWS, 128), F32)
    return pl.pallas_call(
        deliver_kernel,
        out_shape=(shape, shape),
        in_specs=(block, block),
        out_specs=(block, block),
    )(new, chi)


def shards(sources, contrast, spectrum, measured, receivers, positions):
    hbm = pl.BlockSpec(memory_space=pl.ANY)
    table = jnp.asarray(first_table())
    field = jax.ShapeDtypeStruct((2, ROWS, 128), F32)

    def buf(*shape):
        return pltpu.VMEM(shape, F32)

    dma = pltpu.SemaphoreType.DMA
    new, chi = pl.pallas_call(
        kernel,
        out_shape=(field, field),
        in_specs=[hbm] * 5 + [pl.BlockSpec(memory_space=pltpu.SMEM), hbm],
        out_specs=(hbm, hbm),
        scratch_shapes=[
            buf(2, ROWS, 128),
            buf(2, ROWS, 128),
            buf(2, NREC),
            pltpu.VMEM((1, NREC), jnp.int32),
            pltpu.VMEM((512, 512), BF16),
            pltpu.VMEM((512, 512), BF16),
            pltpu.VMEM((512, 512), BF16),
            pltpu.VMEM((1024, 256), BF16),
            pltpu.VMEM((256, 1024), BF16),
            pltpu.VMEM((256, 1024), BF16),
            buf(2, ROWS, 128),
            buf(2, 4096, 128),
            buf(2, 8, NP, NP),
            buf(2, 2, 1024, 128),
            buf(2, 2, 1024, 128),
            buf(2, 2, 1024, 128),
            buf(2, 2, 1024, 128),
            buf(2, ROWS, 128),
            buf(ROWS, 128),
            buf(2, ROWS, 128),
            buf(2, ROWS, 128),
            buf(2, ROWS, 128),
            pltpu.VMEM((ROWS, NREC), BF16),
            pltpu.VMEM((NC, NREC), BF16),
            buf(3, ROWS, 128),
            buf(2, 3, NC, 128),
            buf(2, 3, NC, 128),
            buf(2, 4, 3, 32, 128),
            buf(2, 2, 32, 128),
            buf(2, ROWS, 128),
            buf(8, 128),
            buf(64, 128),
            buf(1, 128),
            buf(GZ, 1, 128),
            buf(8, 2, 128),
            buf(GZ, 2, 128),
            buf(2, 128),
            buf(8, 2, 128),
            buf(8, 2 * NC, 128),
            buf(512, NREC),
            dma((7,)),
            dma((3,)),
            dma((4, 4)),
            dma((4, 4)),
            dma((8,)),
            dma((8,)),
        ]
        + [dma] * 8,
        compiler_params=pltpu.CompilerParams(
            collective_id=0, has_side_effects=True, vmem_limit_bytes=60 * 1024 * 1024
        ),
    )(
        sources.reshape(2, ROWS, 128),
        contrast.reshape(2, ROWS, 128),
        spectrum.reshape(4096, NP),
        measured.reshape(2, NREC),
        receivers,
        positions,
        table,
    )
    new, chi = deliver(new, chi)
    return new.reshape(sources.shape), chi.reshape(contrast.shape)


def solution(mesh):
    in_specs = (
        P("tx", None, "gz", None, None),
        P(None, "gz", None, None),
        P(None, None, "gz", None),
        P("tx", None, None),
        P("tx", None),
        P("tx", None),
    )
    out_specs = (P("tx", None, "gz", None, None), P(None, "gz", None, None))
    return jax.shard_map(shards, mesh=mesh, in_specs=in_specs, out_specs=out_specs, check_vma=False)
```

```python
import math

import jax
import jax.numpy as jnp
import numpy as np
from jax import lax
from jax.experimental import pallas as pl
from jax.experimental.pallas import tpu as pltpu
from jax.sharding import PartitionSpec as P

MESH = pl.DeviceIdType.MESH
F32 = jnp.float32
BF16 = jnp.bfloat16

reach_cells = 16.0
tikhonov = 1.0
step_length = 0.5
norm_floor = 1e-06

NC = 128
NP = 256
GZ = 32
TX = 8
NREC = 1024
ROWS = 512


def dft_matrix():
    k = np.arange(NP)[:, None]
    n = np.arange(NC)[None, :]
    angle = 2.0 * np.pi * ((k * n) % NP) / NP
    cosine, sine = np.cos(angle), np.sin(angle)
    full = np.zeros((2, NP, 2, NC))
    full[0, :, 0, :] = cosine
    full[0, :, 1, :] = sine
    full[1, :, 0, :] = -sine
    full[1, :, 1, :] = cosine
    return full


def halves(table, axis):
    table = table.astype(np.float32)
    high = table.astype(jnp.bfloat16)
    low = (table - high.astype(np.float32)).astype(jnp.bfloat16)
    return np.concatenate([high, low], axis)


def first_table():
    by_freq = dft_matrix().reshape(2, GZ, 2, 4, 2, NC)
    return halves(by_freq.transpose(2, 1, 0, 3, 4, 5).reshape(2 * NP, 2 * NC), 1)


def bits(x, shift, count):
    return lax.bitwise_and(lax.shift_right_logical(x, shift), (1 << count) - 1)


def freq_index(x):
    return bits(x, 0, 8), bits(x, 8, 1)


def freq_pair_index(x):
    return 8 * bits(x, 0, 5) + 2 * bits(x, 6, 2) + bits(x, 5, 1), bits(x, 8, 1)


def cell_index(x):
    return bits(x, 0, 7), bits(x, 7, 1)


def plane_index(x):
    return 4 * bits(x, 0, 5) + bits(x, 5, 2), bits(x, 7, 1)


def plane_half_index(x):
    return 4 * bits(x, 3, 5) + 2 * bits(x, 2, 1) + bits(x, 0, 1), bits(x, 1, 1)


def fill_table(ref, axis, row_of, column_of, rows_are_freq):
    height, width = ref.shape
    height, width = (height // 2, width) if axis == 0 else (height, width // 2)

    @pl.loop(0, height // 32)
    def _(n):
        a, part_a = row_of(lax.broadcasted_iota(jnp.int32, (32, width), 0) + n * 32)
        b, part_b = column_of(lax.broadcasted_iota(jnp.int32, (32, width), 1))
        quarter = (part_a - part_b) if rows_are_freq else (part_b - part_a)
        turn = lax.bitwise_and(a * b + 64 * quarter, 255)
        table = sin_cos_twelfth(turn.astype(F32) * (12.0 / 256.0))[1]
        high, low = split(table)
        rows = pl.ds(pl.multiple_of(n * 32, 32), 32)
        if axis == 0:
            ref[rows, :] = high
            ref[pl.ds(pl.multiple_of(height + n * 32, 32), 32), :] = low
        else:
            ref[rows, pl.ds(0, width)] = high
            ref[rows, pl.ds(width, width)] = low


def split(x):
    high = x.astype(BF16)
    low = (x - high.astype(F32)).astype(BF16)
    return high, low


def left_dft(table, x):
    depth = x.shape[0]
    high, low = split(x)
    lhs = jnp.concatenate([table[:, :depth], table], axis=1)
    rhs = jnp.concatenate([high, low, high], axis=0)
    return jnp.dot(lhs, rhs, preferred_element_type=F32)


def right_dft(x, table):
    depth = x.shape[1]
    high, low = split(x)
    lhs = jnp.concatenate([high, low, high], axis=1)
    rhs = jnp.concatenate([table[:depth], table], axis=0)
    return jnp.dot(lhs, rhs, preferred_element_type=F32)


def sin_cos_twelfth(radius):
    turns = jnp.floor(radius * (1.0 / 12.0) + 0.5)
    half = (radius - 12.0 * turns) * (math.pi / 12.0)
    sq = half * half
    s = -2.5052108e-08
    for coef in (2.7557319e-06, -1.9841270e-04, 8.3333333e-03, -1.6666667e-01, 1.0):
        s = s * sq + coef
    s = s * half
    c = 2.0876757e-09
    for coef in (-2.7557319e-07, 2.4801587e-05, -1.3888889e-03, 4.1666667e-02, -0.5, 1.0):
        c = c * sq + coef
    return 2.0 * s * c, 1.0 - 2.0 * s * s


def kernel(
    src_hbm, contrast_hbm, spec_hbm, meas_hbm, cell_hbm, pos_hbm,
    aq_hbm,
    new_hbm, chi_hbm,
    src, contrast, meas, cell, pos, aq, ap, br, bir, aip, aiq, out_src,
    spec_raw, spec, y_buf, r_buf, u_buf, b_buf, inc, amp_sum, scat, res, drive,
    hot, hot_plane, part, ring_in, chi_own, chi, extra, extra_all,
    obj, obj_all, mf, mf_in, mf_own, mf_all, placed_freq, found_first,
    load_sem, store_sem, send_sem, recv_sem, tx_send, tx_recv, ex_send, ex_recv,
    ob_send, ob_recv, ma_send, ma_recv, mb_send, mb_recv,
):
    me = lax.axis_index("gz")
    tx = lax.axis_index("tx")
    my_y = me // 8
    my_z = lax.rem(me, 8)
    my_x = tx // 2
    core = lax.rem(tx, 2)
    partner = 2 * my_x + 1 - core

    y_part = [8 * lax.rem(my_y + d, 4) for d in range(4)]
    z_part = [lax.rem(my_z + d, 8) for d in range(8)]
    peers = [y_part[i // 8] + z_part[(3 * i) % 8] for i in range(1, GZ)]
    tx_peers = [lax.rem(tx + d, TX) for d in range(1, TX)]
    x_peers = [lax.rem(my_x + d, 4) for d in range(1, 4)]
    group_peers = [lax.rem(me + 4 * d, GZ) for d in range(1, 8)]

    loads = {}
    for n, (name, hbm, vmem) in enumerate(
        (
            ("aq", aq_hbm, aq),
            ("src", src_hbm, src),
            ("meas", meas_hbm, meas),
            ("cell", cell_hbm, cell),
            ("pos", pos_hbm, pos),
            ("spec0", spec_hbm.at[:, pl.ds(0, 128)], spec_raw.at[0]),
            ("spec1", spec_hbm.at[:, pl.ds(128, 128)], spec_raw.at[1]),
            ("contrast", contrast_hbm, contrast),
        )
    ):
        loads[name] = pltpu.make_async_copy(hbm, vmem, load_sem.at[n])

    def loaded(*names):
        for name in names:
            loads[name].wait()

    barrier = pltpu.get_barrier_semaphore()

    for to in peers:
        pl.semaphore_signal(barrier, inc=1, device_id={"gz": to}, device_id_type=MESH)
    for to in tx_peers:
        pl.semaphore_signal(barrier, inc=1, device_id={"tx": to}, device_id_type=MESH)

    for load in loads.values():
        load.start()
    loaded("meas", "pos")

    lane = lax.broadcasted_iota(jnp.int32, (8, 128), 1)
    share = jnp.sum(meas[...] * meas[...], keepdims=True)
    row = jnp.where(lane == 0, pos[0:1, 0:1].astype(F32), 0.0)
    row = row + jnp.where(lane == 1, pos[0:1, 1:2].astype(F32), 0.0)
    row = row + jnp.where(lane == 2, share, 0.0)
    extra[...] = row
    extra_all[pl.ds(pl.multiple_of(8 * tx, 8), 8), :] = row

    chunks = (
        ((0, 1, 0, 32), (1, 1, 0, 32)),
        ((0, 1, 0, 16), (0, 1, 16, 8), (0, 1, 24, 8), (1, 1, 0, 32)),
        ((0, 2, 0, 16), (0, 1, 16, 16), (1, 1, 16, 16)),
        ((0, 2, 0, 8), (0, 2, 8, 8), (0, 1, 16, 16), (1, 1, 16, 16)),
    )
    buffers = ((y_buf, r_buf), (u_buf, b_buf))

    def exchange_copy(trip, chunk, src_at, dst_at, to):
        phase = trip // 2
        s_ref, d_ref = buffers[trip % 2]
        return pltpu.make_async_remote_copy(
            src_ref=s_ref.at[(phase,) + src_at],
            dst_ref=d_ref.at[(phase,) + dst_at],
            send_sem=send_sem.at[trip, chunk],
            recv_sem=recv_sem.at[trip, chunk],
            device_id={"gz": to},
            device_id_type=MESH,
        )

    def start(trip, chunk):
        first, count, offset, size = chunks[trip][chunk]

        def block(g):
            return pl.ds(first, count), pl.ds(pl.multiple_of(offset + 32 * g, 8), size)

        for to in peers:
            exchange_copy(trip, chunk, block(to), block(me), to).start()
        s_ref, d_ref = buffers[trip % 2]
        for half in range(first, first + count):
            own = (trip // 2, half, pl.ds(pl.multiple_of(offset + 32 * me, 8), size))
            d_ref[own] = s_ref[own]

    def wait(trip, chunk, receive=True):
        first, count, offset, size = chunks[trip][chunk]
        at = (pl.ds(0, count), pl.ds(0, (GZ - 1) * size))
        copy = exchange_copy(trip, chunk, at, at, peers[0])
        if receive:
            copy.wait_recv()
        else:
            copy.wait_send()

    def forward_second(field, phase, h, ph):
        x = jnp.concatenate(
            [
                jnp.concatenate(
                    [field[c, pl.ds((2 * ph + j) * NC, NC), :] for j in range(2)], axis=1
                )
                for c in range(2)
            ],
            axis=0,
        )
        y = left_dft(aq[pl.ds(h * 256, 256), :], x)
        for g in range(GZ):
            for j in range(2):
                y_buf[phase, h, pl.ds(g * 32 + (2 * ph + j) * 8, 8), :] = y[
                    8 * g : 8 * g + 8, j * 128 : j * 128 + 128
                ]

    def middle(phase, sign, ratio):
        @pl.loop(0, 4)
        def _(kk):
            h = kk // 2

            for h_now, needed in (((0, (0,)), (1, (1,))), ((0, (0, 1)), (1, (2,))))[phase]:

                @pl.when(kk == 2 * h_now)
                def _():
                    for chunk in needed:
                        wait(2 * phase, chunk)

            cols = []
            for i in range(2):
                rows = []
                for c in range(2):
                    for p in range(4):
                        first = p * 8 + c * 4 + 2 * lax.rem(kk, 2) + i
                        x = r_buf[phase, h, pl.ds(first, GZ, stride=32), :]
                        if ratio is not None:
                            x = x + ratio * placed_freq[
                                2 * kk + i, c * NC + p * GZ : c * NC + (p + 1) * GZ, :
                            ]
                        rows.append(x)
                cols.append(jnp.concatenate(rows, axis=0))
            z = left_dft(ap[...], jnp.concatenate(cols, axis=1))
            outs = []
            for i in range(2):
                lanes = slice(i * NC, (i + 1) * NC)
                w = right_dft(jnp.concatenate([z[:NP, lanes], z[NP:, lanes]], axis=1), br[...])
                re, im = w[:, :NP], w[:, NP:]
                sr, si = spec[0, 2 * kk + i], spec[1, 2 * kk + i] * sign
                w = jnp.concatenate([re * sr - im * si, re * si + im * sr], axis=1)
                v = right_dft(w, bir[...])
                outs.append(jnp.concatenate([v[:, :NC], v[:, NC:]], axis=0))
            u = left_dft(aip[...], jnp.concatenate(outs, axis=1))
            upper = lax.bitwise_and(lax.broadcasted_iota(jnp.int32, (256, NC), 0), 4) != 0
            even, odd = u[:, :NC], u[:, NC:]
            halves_of_u = (
                jnp.where(upper, pltpu.roll(odd, 4, 0), even),
                jnp.where(upper, odd, pltpu.roll(even, 252, 0)),
            )
            for ph in range(2):
                for g in range(GZ):
                    at = pl.multiple_of(g * 32 + kk * 8, 8)
                    u_buf[phase, ph, pl.ds(at, 8), :] = halves_of_u[ph][8 * g : 8 * g + 8]

            for at_kk, done in (((1, (0,)), (2, (1,)), (3, (2, 3))), ((0, (0,)), (1, (1,)), (3, (2, 3))))[phase]:

                @pl.when(kk == at_kk)
                def _():
                    for chunk in done:
                        start(2 * phase + 1, chunk)

    def wait_back(phase, ph):
        for chunk in ((0, 1, 2), (3,))[ph]:
            wait(2 * phase + 1, chunk)

    def inverse_second(phase, ph):
        cols = []
        for p2 in range(2):
            rows = []
            for c in range(2):
                for kk in range(4):
                    for i in range(2):
                        first = kk * 8 + i * 4 + c * 2 + p2
                        rows.append(b_buf[phase, ph, pl.ds(first, GZ, stride=32), :])
            cols.append(jnp.concatenate(rows, axis=0))
        return left_dft(aiq[...], jnp.concatenate(cols, axis=1))

    loaded("aq", "src")
    for h in range(2):
        for ph in range(2):
            forward_second(src, 0, h, ph)
        if h == 0:
            pl.semaphore_wait(barrier, GZ - 1 + TX - 1)
        start(0, h)

    def extra_copy(to, src_ref, dst_ref):
        return pltpu.make_async_remote_copy(
            src_ref=src_ref,
            dst_ref=dst_ref,
            send_sem=ex_send,
            recv_sem=ex_recv,
            device_id={"tx": to},
            device_id_type=MESH,
        )

    for to in tx_peers:
        extra_copy(to, extra, extra_all.at[pl.ds(pl.multiple_of(8 * tx, 8), 8), :]).start()
    extra_sum = extra_all.at[pl.ds(0, 8 * (TX - 1)), :]
    extra_wait = extra_copy(tx_peers[0], extra_sum, extra_sum)

    def geometry(n, rows_n):
        index = lax.broadcasted_iota(jnp.int32, (rows_n, 128), 0) + n * rows_n
        a = lax.shift_right_logical(index, 7) + (me * 4 + NC // 4)
        b = lax.bitwise_and(index, 127)
        c = lax.broadcasted_iota(jnp.int32, (rows_n, 128), 1)
        return a, b, c

    @pl.loop(0, 16)
    def _(n):
        a, b, c = geometry(n, 32)
        b = b - pos[0:1, 0:1]
        c = c - pos[0:1, 1:2]
        radius = jnp.sqrt((a * a + b * b + c * c).astype(F32))
        amplitude = reach_cells / (reach_cells + radius)
        sine, cosine = sin_cos_twelfth(radius)
        at = pl.ds(pl.multiple_of(n * 32, 32), 32)
        inc[0, at, :] = amplitude * cosine
        inc[1, at, :] = amplitude * sine

    loaded("cell")
    local = cell[...] - me * (ROWS * 128)
    cell_row = lax.shift_right_arithmetic(local, 7)
    cell_lane = lax.bitwise_and(local, 127)

    @pl.loop(0, 16)
    def _(n):
        index = lax.broadcasted_iota(jnp.int32, (32, NREC), 0) + n * 32
        hot[pl.ds(pl.multiple_of(n * 32, 32), 32), :] = jnp.where(
            index == cell_row, 1.0, 0.0
        ).astype(BF16)

    row_index = lax.broadcasted_iota(jnp.int32, (NC, NREC), 0)
    plane = 4 * lax.bitwise_and(row_index, 31) + lax.shift_right_logical(row_index, 5)
    hot_plane[...] = jnp.where(
        plane == lax.shift_right_logical(cell[...], 14), 1.0, 0.0
    ).astype(BF16)

    loaded("spec0", "spec1")

    @pl.loop(0, 8)
    def _(k):
        for c in range(2):
            for n in range(2):
                spec[c, k, :, pl.ds(n * 128, 128)] = spec_raw[
                    n, pl.ds(c * 2048 + k, NP, stride=8), :
                ] * (2.0 ** -24)

    fill_table(ap, 1, freq_index, plane_index, True)
    fill_table(br, 0, cell_index, freq_index, False)
    fill_table(bir, 0, freq_index, cell_index, True)
    fill_table(aip, 1, plane_half_index, freq_index, False)

    def incident_power():
        extra_wait.wait_recv()

        @pl.loop(0, 16)
        def _(n):
            a, b, c = geometry(n, 32)
            a2 = (a * a).astype(F32)
            bf = b.astype(F32)
            cf = c.astype(F32)
            total = jnp.zeros((32, 128), F32)
            for j in range(TX):
                db = bf - extra_all[8 * j : 8 * j + 1, 0:1]
                dc = cf - extra_all[8 * j : 8 * j + 1, 1:2]
                radius = jnp.sqrt(a2 + db * db + dc * dc)
                amplitude = reach_cells / (reach_cells + radius)
                total = total + amplitude * amplitude
            amp_sum[pl.ds(pl.multiple_of(n * 32, 32), 32), :] = total

    middle(0, 1.0, None)
    loaded("contrast")
    fill_table(aiq, 1, cell_index, freq_pair_index, False)
    incident_power()

    def to_partner(s_ref, d_ref, which):
        return pltpu.make_async_remote_copy(
            src_ref=s_ref,
            dst_ref=d_ref,
            send_sem=tx_send.at[which],
            recv_sem=tx_recv.at[which],
            device_id={"tx": partner},
            device_id_type=MESH,
        )

    def plane_rows(p):
        return pl.ds(pl.multiple_of(p * NC, NC), NC)

    def ring_copy(ph, to, src_ref, dst_ref):
        return pltpu.make_async_remote_copy(
            src_ref=src_ref,
            dst_ref=dst_ref,
            send_sem=tx_send.at[4 * ph + 1],
            recv_sem=tx_recv.at[4 * ph + 1],
            device_id={"tx": to},
            device_id_type=MESH,
        )

    def ring_wait(ph):
        seven = ring_in.at[ph, pl.ds(0, TX - 1)]
        return ring_copy(ph, tx_peers[0], seven, seven)

    def own_rows(ph, x):
        return pl.ds(pl.multiple_of((2 * ph + core) * NC + x * 32, 32), 32)

    def chi_copy(ph, to, src_ref, dst_ref):
        return pltpu.make_async_remote_copy(
            src_ref=src_ref,
            dst_ref=dst_ref,
            send_sem=tx_send.at[4 * ph + 2],
            recv_sem=tx_recv.at[4 * ph + 2],
            device_id={"tx": 2 * to + core},
            device_id_type=MESH,
        )

    def chi_wait(ph):
        three = chi.at[:, pl.ds(0, 96), :]
        return chi_copy(ph, x_peers[0], three, three)

    def chi_send(ph, which):
        at = chi.at[:, plane_rows(2 * ph + which), :]
        return to_partner(at, at, 4 * ph + 3)

    def fields(ph):
        wait_back(0, ph)
        o = inverse_second(0, ph)
        for j in range(2):
            at = pl.ds((2 * ph + j) * NC, NC)
            for c in range(2):
                scat[c, at, :] = o[c * NC : (c + 1) * NC, j * NC : (j + 1) * NC]

        @pl.loop(0, 8)
        def _(n):
            at = pl.ds(pl.multiple_of(ph * 256 + n * 32, 32), 32)
            sr, si = src[0, at, :], src[1, at, :]
            tr = inc[0, at, :] + scat[0, at, :]
            ti = inc[1, at, :] + scat[1, at, :]
            inc[0, at, :] = tr
            inc[1, at, :] = ti
            part[0, at, :] = sr * tr + si * ti
            part[1, at, :] = si * tr - sr * ti
            part[2, at, :] = tr * tr + ti * ti

        def share(t):
            first = (2 * ph + lax.rem(t, 2)) * NC + (t // 2) * 32
            return pl.ds(pl.multiple_of(first, 32), 32)

        for to in tx_peers:
            ring_copy(ph, to, part.at[:, share(to), :], ring_in.at[ph, tx]).start()
        ring_in[ph, tx] = part[:, share(tx), :]

    def contrast_start(ph):
        ring_wait(ph).wait_recv()

        sums = []
        for q in range(3):
            total = ring_in[ph, 0, q]
            for t in range(1, TX):
                total = total + ring_in[ph, t, q]
            sums.append(total)
        below = sums[2] + tikhonov
        rows = own_rows(ph, my_x)
        for c in range(2):
            value = (sums[c] + tikhonov * contrast[c, rows, :]) / below
            chi_own[ph, c] = value
            chi[c, rows, :] = value

        for to in x_peers:
            chi_copy(ph, to, chi_own.at[ph], chi.at[:, rows, :]).start()

    def contrast_forward(ph):
        chi_wait(ph).wait_recv()
        chi_send(ph, core).start()

    def residual(ph, acc):
        chi_send(ph, 1 - core).wait_recv()

        def step(n, acc):
            at = pl.ds(pl.multiple_of(ph * 256 + n * 32, 32), 32)
            cr, ci = chi[0, at, :], chi[1, at, :]
            tr, ti = inc[0, at, :], inc[1, at, :]
            rr = cr * tr - ci * ti - src[0, at, :]
            ri = cr * ti + ci * tr - src[1, at, :]
            res[0, at, :] = rr
            res[1, at, :] = ri
            drive[0, at, :] = -(cr * rr + ci * ri)
            drive[1, at, :] = -(cr * ri - ci * rr)
            return acc + (cr * cr + ci * ci) * amp_sum[at, :]

        return lax.fori_loop(0, 8, step, acc)

    def drive_start(ph):
        for h in range(2):
            forward_second(drive, 1, h, ph)
            if ph == 1:
                start(2, 1 + h)
        if ph == 0:
            start(2, 0)

    def misfit_copy(to, src_ref, dst_ref):
        return pltpu.make_async_remote_copy(
            src_ref=src_ref,
            dst_ref=dst_ref,
            send_sem=ma_send,
            recv_sem=ma_recv,
            device_id={"gz": to},
            device_id_type=MESH,
        )

    mf_most = mf_in.at[pl.ds(0, GZ - 1)]
    misfit_wait = misfit_copy(peers[0], mf_most, mf_most)

    def misfit_back(to, src_ref, dst_ref):
        return pltpu.make_async_remote_copy(
            src_ref=src_ref,
            dst_ref=dst_ref,
            send_sem=mb_send,
            recv_sem=mb_recv,
            device_id={"gz": to},
            device_id_type=MESH,
        )

    mf_seven = mf_all.at[pl.ds(0, 7)]
    back_wait = misfit_back(group_peers[0], mf_seven, mf_seven)

    lane_index = lax.broadcasted_iota(jnp.int32, (NC, NREC), 0)

    def found_at(ph):
        rows = pl.ds(ph * 256, 256)
        pieces = [split(scat[c, rows, :]) for c in range(2)]
        columns = jnp.concatenate(
            [pieces[0][0], pieces[1][0], pieces[0][1], pieces[1][1]], axis=1
        )
        return lax.dot_general(
            columns, hot[rows, :], (((0,), (0,)), ((), ())), preferred_element_type=F32
        )

    def misfit_start():
        found = found_first[...] + found_at(1)
        on_lane = lane_index == cell_lane
        inside = (cell_row >= 0) & (cell_row < ROWS)
        misfit = []
        for c in range(2):
            both = found[c * NC : (c + 1) * NC] + found[(2 + c) * NC : (3 + c) * NC]
            sampled = jnp.sum(jnp.where(on_lane, both, 0.0), axis=0, keepdims=True)
            misfit.append(jnp.where(inside, meas[c : c + 1, :] - sampled, 0.0))
        for i in range(8):
            at = slice(i * 128, (i + 1) * 128)
            mf[i] = jnp.concatenate([misfit[0][:, at], misfit[1][:, at]], axis=0)
        mf_in[me] = mf[me // 4]

        for to in peers:
            misfit_copy(to, mf.at[to // 4], mf_in.at[me]).start()

    def misfit_forward():
        misfit_wait.wait_recv()
        total = mf_in[0]
        for g in range(1, GZ):
            total = total + mf_in[g]
        mf_own[...] = total
        mf_all[me // 4] = total

        for to in group_peers:
            misfit_back(to, mf_own, mf_all.at[me // 4]).start()

    def placed_spectrum():
        back_wait.wait_recv()
        mr = jnp.concatenate([mf_all[i, 0:1, :] for i in range(8)], axis=1)
        mi = jnp.concatenate([mf_all[i, 1:2, :] for i in range(8)], axis=1)
        second = lax.bitwise_and(lax.shift_right_logical(cell[...], 7), 127)

        @pl.loop(0, 8)
        def _(k):
            turn = lax.bitwise_and((8 * me + k) * second, 255)
            sine, cosine = sin_cos_twelfth(turn.astype(F32) * (12.0 / 256.0))
            on_lane = lane_index == cell_lane
            v = (
                split(jnp.where(on_lane, mr * cosine + mi * sine, 0.0)),
                split(jnp.where(on_lane, mi * cosine - mr * sine, 0.0)),
            )
            values = jnp.concatenate([v[0][0], v[1][0], v[0][1], v[1][1]], axis=0)
            found = lax.dot_general(
                hot_plane[...], values, (((1,), (1,)), ((), ())), preferred_element_type=F32
            )
            for c in range(2):
                placed_freq[k, pl.ds(c * NC, NC), :] = (
                    found[:, c * NC : (c + 1) * NC] + found[:, (2 + c) * NC : (3 + c) * NC]
                )

    def obj_copy(to, src_ref, dst_ref):
        return pltpu.make_async_remote_copy(
            src_ref=src_ref,
            dst_ref=dst_ref,
            send_sem=ob_send,
            recv_sem=ob_recv,
            device_id={"gz": to},
            device_id_type=MESH,
        )

    obj_most = obj_all.at[pl.ds(0, GZ - 1)]
    obj_wait = obj_copy(peers[0], obj_most, obj_most)

    def object_start(acc):
        own = jnp.sum(acc, axis=0, keepdims=True)
        obj[...] = own
        obj_all[me] = own
        for to in peers:
            obj_copy(to, obj, obj_all.at[me]).start()

    def object_ratio():
        obj_wait.wait_recv()
        rows = jnp.concatenate([obj_all[g] for g in range(GZ)], axis=0)
        object_norm = jnp.sum(rows, keepdims=True)
        data_norm = jnp.zeros((1, 1), F32)
        for j in range(TX):
            data_norm = data_norm + extra_all[8 * j : 8 * j + 1, 2:3]
        return object_norm / (data_norm + norm_floor)

    fields(0)
    found_first[...] = found_at(0)
    contrast_start(0)
    fields(1)
    misfit_start()
    contrast_forward(0)
    acc = residual(0, jnp.zeros((32, 128), F32))
    drive_start(0)
    contrast_start(1)
    misfit_forward()
    contrast_forward(1)
    acc = residual(1, acc)
    object_start(acc)
    drive_start(1)
    placed_spectrum()
    chi_store = pltpu.make_async_copy(chi, chi_hbm, store_sem.at[2])
    chi_store.start()
    middle(1, -1.0, object_ratio())
    stores = []
    for ph in range(2):
        wait_back(1, ph)
        o = inverse_second(1, ph)
        for j in range(2):
            at = pl.ds((2 * ph + j) * NC, NC)
            for c in range(2):
                back = o[c * NC : (c + 1) * NC, j * NC : (j + 1) * NC]
                out_src[c, at, :] = src[c, at, :] + step_length * (res[c, at, :] + back)
        at = pl.ds(ph * 256, 256)
        stores.append(
            pltpu.make_async_copy(out_src.at[:, at, :], new_hbm.at[:, at, :], store_sem.at[ph])
        )
        stores[-1].start()

    for trip in range(4):
        for chunk in range(len(chunks[trip])):
            wait(trip, chunk, False)

    chi_store.wait()
    for store in stores:
        store.wait()
    obj_wait.wait_send()
    misfit_wait.wait_send()
    back_wait.wait_send()
    extra_wait.wait_send()
    for ph in range(2):
        ring_wait(ph).wait_send()
        chi_wait(ph).wait_send()
        chi_send(ph, core).wait_send()


def deliver_kernel(new_in, chi_in, new_out, chi_out):
    new_out[...] = new_in[...]
    chi_out[...] = chi_in[...]


def deliver(new, chi):
    block = pl.BlockSpec(memory_space=pltpu.VMEM)
    shape = jax.ShapeDtypeStruct((2, ROWS, 128), F32)
    return pl.pallas_call(
        deliver_kernel,
        out_shape=(shape, shape),
        in_specs=(block, block),
        out_specs=(block, block),
    )(new, chi)


def shards(sources, contrast, spectrum, measured, receivers, positions):
    hbm = pl.BlockSpec(memory_space=pl.ANY)
    table = jnp.asarray(first_table())
    field = jax.ShapeDtypeStruct((2, ROWS, 128), F32)

    def buf(*shape):
        return pltpu.VMEM(shape, F32)

    dma = pltpu.SemaphoreType.DMA
    new, chi = pl.pallas_call(
        kernel,
        out_shape=(field, field),
        in_specs=[hbm] * 7,
        out_specs=(hbm, hbm),
        scratch_shapes=[
            buf(2, ROWS, 128),
            buf(2, ROWS, 128),
            buf(2, NREC),
            pltpu.VMEM((1, NREC), jnp.int32),
            pltpu.VMEM((1, 2), jnp.int32),
            pltpu.VMEM((512, 512), BF16),
            pltpu.VMEM((512, 512), BF16),
            pltpu.VMEM((512, 512), BF16),
            pltpu.VMEM((1024, 256), BF16),
            pltpu.VMEM((256, 1024), BF16),
            pltpu.VMEM((256, 1024), BF16),
            buf(2, ROWS, 128),
            buf(2, 4096, 128),
            buf(2, 8, NP, NP),
            buf(2, 2, 1024, 128),
            buf(2, 2, 1024, 128),
            buf(2, 2, 1024, 128),
            buf(2, 2, 1024, 128),
            buf(2, ROWS, 128),
            buf(ROWS, 128),
            buf(2, ROWS, 128),
            buf(2, ROWS, 128),
            buf(2, ROWS, 128),
            pltpu.VMEM((ROWS, NREC), BF16),
            pltpu.VMEM((NC, NREC), BF16),
            buf(3, ROWS, 128),
            buf(2, TX, 3, 32, 128),
            buf(2, 2, 32, 128),
            buf(2, ROWS, 128),
            buf(8, 128),
            buf(64, 128),
            buf(1, 128),
            buf(GZ, 1, 128),
            buf(8, 2, 128),
            buf(GZ, 2, 128),
            buf(2, 128),
            buf(8, 2, 128),
            buf(8, 2 * NC, 128),
            buf(512, NREC),
            dma((8,)),
            dma((3,)),
            dma((4, 4)),
            dma((4, 4)),
            dma((8,)),
            dma((8,)),
        ]
        + [dma] * 8,
        compiler_params=pltpu.CompilerParams(
            collective_id=0, has_side_effects=True, vmem_limit_bytes=60 * 1024 * 1024
        ),
    )(
        sources.reshape(2, ROWS, 128),
        contrast.reshape(2, ROWS, 128),
        spectrum.reshape(4096, NP),
        measured.reshape(2, NREC),
        receivers,
        positions,
        table,
    )
    new, chi = deliver(new, chi)
    return new.reshape(sources.shape), chi.reshape(contrast.shape)


def solution(mesh):
    in_specs = (
        P("tx", None, "gz", None, None),
        P(None, "gz", None, None),
        P(None, None, "gz", None),
        P("tx", None, None),
        P("tx", None),
        P("tx", None),
    )
    out_specs = (P("tx", None, "gz", None, None), P(None, "gz", None, None))
    return jax.shard_map(shards, mesh=mesh, in_specs=in_specs, out_specs=out_specs, check_vma=False)
```
